32 devices in a mesh: dp: 16 (over z, y, x), mp: 2 (over core).
Axes of the slice: x: 2, y: 2, z: 4, core: 2. Of those that a mesh axis runs over, the one named last changes fastest.
Arguments:
- hidden: bfloat16 [2, 64, 64, 768], P(None, 'dp'), may hold values from -6 to 6
- encoder_tokens: bfloat16 [2, 32, 576, 768], P(None, 'dp'), may hold values from -6 to 6
- segment_ids: int32 [2, 64, 64], P(None, 'dp'), may hold values from 0 to 3, never falling along the last dimension, each value on 1 to 32 neighbouring positions
- image_index: int32 [2, 64], P(None, 'dp'), may hold values from 0 to 1
- cotangent: bfloat16 [2, 64, 64, 768], P(None, 'dp'), may hold values from -6 to 6
- norm_gains: bfloat16 [3, 768], P(None, 'dp'), may hold values from 0.099609375 to 1.8984375
- qkv_weight: bfloat16 [3, 768, 768], P(None, 'dp', 'mp'), may hold values from -0.21875 to 0.21875
- self_out_weight: bfloat16 [768, 768], P('dp', 'mp'), may hold values from -0.875 to 0.875
- cross_query_weight: bfloat16 [768, 768], P('dp', 'mp'), may hold values from -0.21875 to 0.21875
- cross_kv_weight: bfloat16 [2, 768, 768], P(None, 'dp', 'mp'), may hold values from -0.21875 to 0.21875
- cross_out_weight: bfloat16 [768, 768], P('dp', 'mp'), may hold values from -2.5 to 2.5
- up_weight: bfloat16 [768, 3072], P('dp', 'mp'), may hold values from -0.21875 to 0.21875
- down_weight: bfloat16 [768, 3072], P('dp', 'mp'), may hold values from -0.109375 to 0.109375
Outputs:
- output: bfloat16 [2, 64, 64, 768], P(None, 'dp')
- input_grad: float32 [2, 64, 64, 768], P(None, 'dp')
- encoder_grad: float32 [2, 32, 576, 768], P(None, 'dp', None, 'mp')
- grad_norm_gains: float32 [3, 768], P(None, 'dp')
- grad_qkv: float32 [3, 768, 768], P(None, 'dp', 'mp')
- grad_self_out: float32 [768, 768], P('dp', 'mp')
- grad_cross_query: float32 [768, 768], P('dp', 'mp')
- grad_cross_kv: float32 [2, 768, 768], P(None, 'dp', 'mp')
- grad_cross_out: float32 [768, 768], P('dp', 'mp')
- grad_up: float32 [768, 3072], P('dp', 'mp')
- grad_down: float32 [768, 3072], P('dp', 'mp')
The draws below stay inside these ranges and needn't reach their ends.
Inputs may be any that keep to these rules, and one draw needn't show every extreme that they name: `segment_ids`: within a row the ids never fall; they number the 4 captions of the row, each of 1 to 32 tokens. Caption row r of a micro-batch reads image (r // 4) * 2 + image_index of that row.
All inputs are finite; a program needn't handle non-finite values.
Results may differ from the reference program's by a relative error of at most 0.019.
Values may be sent and summed in bfloat16 or wider, within the bound.
A program may use at most 192 MiB of HBM per device.

```python
import math
import jax
import jax.numpy as jnp
import numpy as np
from jax import lax

D = 768
HEADS = 12
HEAD = 64
FF = 3072
CTX = 576
SEQ = 64
CAPTIONS = 4
MICRO = 2
ROW_MB = 4
IMG_MB = 2
ROWS = 64
IMAGES = 32
N_DP = 16


def plant(result, key, low, largest):
    longest = result.shape.index(max(result.shape))
    spots = []
    for shift in (0, 1):
        where = [jax.random.randint(jax.random.fold_in(key, axis), (), 0, length) for axis, length in enumerate(result.shape)]
        where[longest] = (where[longest] + shift) % result.shape[longest]
        spots.append(tuple(where))
    return result.at[spots[0]].set(low).at[spots[1]].set(largest)


def spiked(array, stream_key, source, target, parts, factor):
    def block_of(dim):
        return (jnp.arange(array.shape[dim]) // (array.shape[dim] // parts)).reshape((-1,) + (1,) * (array.ndim - 1 - dim))

    one_side = jax.random.permutation(stream_key, parts)[block_of(target)]
    other_side = (block_of(target) + parts // 2) % parts
    return jnp.where((block_of(source) == one_side) | (block_of(source) == other_side), factor * array, array)


def block_levels(key, shape, pieces, smallest, high):
    level = 1.0
    for position, parts in pieces:
        draws = jax.random.uniform(jax.random.fold_in(jax.random.fold_in(key, 6), position), (parts,), jnp.float32, smallest / len(pieces), high / len(pieces))
        level = level * jnp.repeat(jnp.exp(draws), shape[position] // parts).reshape((-1,) + (1,) * (len(shape) - 1 - position))
    return level


def length_profile(amount, total, bound, slope):
    loads = [(1 << 20) // math.isqrt(rank ** slope) + 1 for rank in range(2, amount + 1)]
    rest, holding = total - bound - (amount - 1), [1] * (amount - 1)
    while rest > 0:
        movable = [i for i in range(amount - 1) if holding[i] < bound]
        whole, budget = sum([loads[i] for i in movable]), rest
        for i in movable:
            extra = min(bound - holding[i], max(1, budget * loads[i] // whole), rest)
            holding[i] = holding[i] + extra
            rest = rest - extra
    return np.array([bound] + holding)


def uneven(own_key, count, total, most, lean):
    if count == 2:
        one = jax.random.randint(own_key, (), max(1, total - most), min(most, total - 1) + 1)
        return jnp.stack([one, total - one])
    tallies = jnp.asarray(length_profile(count, total, most, lean), jnp.int32)
    pairs = (count - 1) // 2
    source_of, sink = tallies[1:1 + 2 * pairs:2], tallies[2:2 + 2 * pairs:2]
    slack = jnp.minimum(source_of - 1, most - sink)
    shifted = jax.random.randint(jax.random.fold_in(own_key, 1), (pairs,), 0, 1 << 20) % (slack + 1)
    tallies = tallies.at[1:1 + 2 * pairs:2].set(source_of - shifted).at[2:2 + 2 * pairs:2].set(sink + shifted)
    return tallies[jax.random.permutation(jax.random.fold_in(own_key, 2), count)]


def gaussian(rng, dims, width, limit, cuts=(), held_as=jnp.bfloat16):
    entries = width * jax.random.normal(rng, dims, jnp.float32)
    if cuts:
        entries = entries * block_levels(rng, dims, cuts, -0.22, 0.18)
    return jnp.clip(entries, -limit, limit).astype(held_as)


def heavy_noise(key, extent, deviation, reach, split, heavy, kind=jnp.bfloat16):
    result = deviation * jax.random.normal(key, extent, jnp.float32)
    if split:
        result = result * block_levels(key, extent, split, -0.22, 0.18)
    return jnp.clip(spiked(result, jax.random.fold_in(key, 3), *heavy), -reach, reach).astype(kind)


def setup_inputs(seed: int = 0) -> dict:
    key_list = jax.random.split(jax.random.key(seed), 14)
    return {
        "hidden": gaussian(key_list[0], (MICRO, ROWS, SEQ, D), 1.0, 6.0, ((1, 16),)),
        "encoder_tokens": gaussian(key_list[1], (MICRO, IMAGES, CTX, D), 1.0, 6.0, ((1, 16),)),
        "segment_ids": jax.vmap(lambda own: jnp.searchsorted(jnp.cumsum(uneven(own, CAPTIONS, SEQ, SEQ // 2, 1)), jnp.arange(SEQ), side="right"))(jax.random.split(key_list[2], MICRO * ROWS)).reshape((MICRO, ROWS, SEQ)).astype(jnp.int32),
        "image_index": plant(jax.random.randint(key_list[3], (MICRO, ROWS), 0, IMG_MB), jax.random.fold_in(key_list[3], 1), 0, IMG_MB - 1).astype(jnp.int32),
        "cotangent": heavy_noise(key_list[4], (MICRO, ROWS, SEQ, D), 1.0, 6.0, ((1, 16),), (1, 3, 16, 2.0)),
        "norm_gains": jnp.clip(1.0 + 0.18 * jax.random.normal(key_list[5], (3, D), jnp.float32), 0.099609375, 1.8984375).astype(jnp.bfloat16),
        "qkv_weight": gaussian(key_list[6], (3, D, D), D ** -0.5, 0.21875, ((1, 16), (2, 2))),
        "self_out_weight": gaussian(key_list[7], (D, D), (max(4 * D // SEQ, 1)) ** -0.5, 0.875, ((0, 16), (1, 2))),
        "cross_query_weight": gaussian(key_list[8], (D, D), D ** -0.5, 0.21875, ((0, 16), (1, 2))),
        "cross_kv_weight": gaussian(key_list[9], (2, D, D), D ** -0.5, 0.21875, ((1, 16), (2, 2))),
        "cross_out_weight": gaussian(key_list[10], (D, D), (max(4 * D // CTX, 1)) ** -0.5, 2.5, ((0, 16), (1, 2))),
        "up_weight": gaussian(key_list[11], (D, FF), D ** -0.5, 0.21875, ((0, 16), (1, 2))),
        "down_weight": gaussian(key_list[12], (D, FF), FF ** -0.5, 0.109375, ((0, 16), (1, 2))),
    }


EPSILON = 1e-05
NEGATIVE = -1e+30
HIGHEST = lax.Precision.HIGHEST

@jax.custom_vjp
def low(v):
    return lax.optimization_barrier(v.astype(jnp.bfloat16)).astype(jnp.float32)

@jax.custom_vjp
def low_back(v):
    return v

def low_keep(v):
    return (low(v), None)

def low_pass(kept, grad):
    return (grad,)

def back_keep(v):
    return (v, None)

def back_low(kept, grad):
    return (low(grad),)
low.defvjp(low_keep, low_pass)
low_back.defvjp(back_keep, back_low)

def layer_norm(values, gain_row):
    centred = values - lax.optimization_barrier(jnp.mean(values, axis=-1, keepdims=True))
    spread = lax.optimization_barrier(jnp.mean(centred * centred, axis=-1, keepdims=True))
    return centred * lax.rsqrt(spread + EPSILON) * gain_row

def attention(queries, key_heads, value_heads, allowed):
    scores = jnp.einsum('rqhe,rkhe->rhqk', queries, key_heads, precision=HIGHEST) * HEAD ** (-0.5)
    scores = low_back(scores)
    scores = jnp.where(allowed[:, None], scores, NEGATIVE)
    weights_low = low(jax.nn.softmax(scores, axis=-1))
    mixed_heads = jnp.einsum('rhqk,rkhe->rqhe', weights_low, value_heads, precision=HIGHEST)
    return low(low_back(mixed_heads))

def block_forward(hidden_rows, encoder_rows, params_in, segment_rows, image_rows):
    norm_gains, qkv_weight, self_out_weight, cross_query_weight, cross_kv_weight, cross_out_weight, up_weight, down_weight = params_in
    row_count = hidden_rows.shape[0]
    tokens = row_count * SEQ
    head_shape = (row_count, SEQ, HEADS, HEAD)
    flat_in = hidden_rows.reshape(tokens, D)
    low_one = low(layer_norm(flat_in, norm_gains[0]))
    projected = low(low_back(jnp.einsum('td,jde->jte', low_one, qkv_weight, precision=HIGHEST)))
    positions = jnp.arange(SEQ)
    causal = positions[None, :] <= positions[:, None]
    allowed = causal[None] & (segment_rows[:, :, None] == segment_rows[:, None, :])
    self_mixed = attention(projected[0].reshape(head_shape), projected[1].reshape(head_shape), projected[2].reshape(head_shape), allowed).reshape(tokens, D)
    resid_one = flat_in + low_back(jnp.einsum('te,de->td', self_mixed, self_out_weight, precision=HIGHEST))
    low_two = low(layer_norm(resid_one, norm_gains[1]))
    cross_queries = low(low_back(jnp.dot(low_two, cross_query_weight, precision=HIGHEST))).reshape(head_shape)
    image_kv = low(low_back(jnp.einsum('ncd,jde->jnce', encoder_rows, cross_kv_weight, precision=HIGHEST)))
    row_kv = image_kv[:, image_rows].reshape(2, row_count, CTX, HEADS, HEAD)
    everywhere = jnp.ones((row_count, SEQ, CTX), dtype=jnp.bool_)
    cross_mixed = attention(cross_queries, row_kv[0], row_kv[1], everywhere).reshape(tokens, D)
    resid_two = resid_one + low_back(jnp.einsum('te,de->td', cross_mixed, cross_out_weight, precision=HIGHEST))
    low_three = low(layer_norm(resid_two, norm_gains[2]))
    pre_act = low_back(jnp.dot(low_three, up_weight, precision=HIGHEST))
    activated = low(jax.nn.gelu(pre_act, approximate=False))
    resid_three = resid_two + low_back(jnp.einsum('tf,df->td', activated, down_weight, precision=HIGHEST))
    return resid_three.reshape(row_count, SEQ, D)

def add_pair(first, second):
    return first + second

def reference(hidden, encoder_tokens, segment_ids, image_index, cotangent, norm_gains, qkv_weight, self_out_weight, cross_query_weight, cross_kv_weight, cross_out_weight, up_weight, down_weight):
    blocks = MICRO * N_DP
    hidden_blocks = hidden.astype(jnp.float32).reshape(blocks, ROW_MB, SEQ, D)
    encoder_blocks = encoder_tokens.astype(jnp.float32).reshape(blocks, IMG_MB, CTX, D)
    segment_blocks = segment_ids.reshape(blocks, ROW_MB, SEQ)
    image_blocks = image_index.reshape(blocks, ROW_MB)
    cotangent_blocks = cotangent.astype(jnp.float32).reshape(blocks, ROW_MB, SEQ, D)
    params = (norm_gains.astype(jnp.float32), qkv_weight.astype(jnp.float32), self_out_weight.astype(jnp.float32), cross_query_weight.astype(jnp.float32), cross_kv_weight.astype(jnp.float32), cross_out_weight.astype(jnp.float32), up_weight.astype(jnp.float32), down_weight.astype(jnp.float32))

    def one_block(totals, block_items):
        hidden_rows, encoder_rows, segment_rows, image_rows, cotangent_rows = block_items

        def forward(hidden_in, encoder_in, params_in):
            return block_forward(hidden_in, encoder_in, params_in, segment_rows, image_rows)
        output_rows, backward = jax.vjp(forward, hidden_rows, encoder_rows, params)
        grad_hidden, grad_encoder, grad_params = backward(cotangent_rows)
        return (jax.tree.map(add_pair, totals, grad_params), (output_rows, grad_hidden, grad_encoder))
    zero_grads = jax.tree.map(jnp.zeros_like, params)
    totals, (output_blocks, hidden_grads, encoder_grads) = lax.scan(one_block, zero_grads, (hidden_blocks, encoder_blocks, segment_blocks, image_blocks, cotangent_blocks))
    return (output_blocks.reshape(MICRO, ROW_MB * N_DP, SEQ, D).astype(jnp.bfloat16), hidden_grads.reshape(MICRO, ROW_MB * N_DP, SEQ, D), encoder_grads.reshape(MICRO, IMG_MB * N_DP, CTX, D), totals[0], totals[1], totals[2], totals[3], totals[4], totals[5], totals[6], totals[7])
```

```python
import functools
from types import SimpleNamespace

import jax
import jax.numpy as jnp
from jax import lax
from jax.experimental import pallas as pl
from jax.experimental.pallas import tpu as pltpu
from jax.sharding import PartitionSpec as P

HEAD = 64
PAIR = 2 * HEAD
EPSILON = 1e-05
NEGATIVE = -1e30
ROOT_HALF = 0.7071067811865476
DENSITY = 0.3989422804014327
MESH = pl.DeviceIdType.MESH
LOW = jnp.bfloat16
F32 = jnp.float32
QKV, SO, CQ, CKV, CO, MATS = 0, 3, 4, 5, 7, 8
UP, DOWN = 0, 1
LN_ROWS = 64
TILE = 256


def dot(left, right, left_dim, right_dim):
    return lax.dot_general(
        left, right, (((left_dim,), (right_dim,)), ((), ())), preferred_element_type=F32
    )


def lanes_of(pair):
    return pl.ds(pair * PAIR, PAIR)


def head_masks():
    lane = lax.broadcasted_iota(jnp.int32, (1, PAIR), 1)
    first = jnp.where(lane < HEAD, 1.0, 0.0)
    return first.astype(LOW), (1.0 - first).astype(LOW)


def stack_heads(values, masks):
    return jnp.concatenate([values * masks[0], values * masks[1]], axis=0)


def join_heads(stacked):
    half = stacked.shape[0] // 2
    lane = lax.broadcasted_iota(jnp.int32, (half, PAIR), 1)
    return jnp.where(lane < HEAD, stacked[:half], stacked[half:])


def centre(values):
    centred = values - jnp.mean(values, axis=-1, keepdims=True)
    spread = jnp.mean(centred * centred, axis=-1, keepdims=True)
    scale = lax.rsqrt(spread + EPSILON)
    return centred * scale, scale


def softmax_keys(scores):
    shifted = jnp.exp(scores - jnp.max(scores, axis=0, keepdims=True))
    return shifted / jnp.sum(shifted, axis=0, keepdims=True)


def layer(g, *refs):
    r = SimpleNamespace(**dict(zip(g.names, refs)))
    me, mp = lax.axis_index("dp"), lax.axis_index("mp")
    zi, col = me // 4, me % 4
    sibling = (me, 1 - mp)
    col_x = col + 1 - 2 * (col % 2)
    col_y = (col + 2) % 4
    col_d = (col_x + 2) % 4
    col_a = mp * col_x + (1 - mp) * col_y
    col_b = mp * col_y + (1 - mp) * col_x
    at_x, at_y = (zi * 4 + col_x, mp), (zi * 4 + col_y, mp)
    at_a, at_b = (zi * 4 + col_a, mp), (zi * 4 + col_b, mp)
    z_of = [(zi + k) % g.nz for k in range(1, g.nz)]
    z_from = [(zi + g.nz - k) % g.nz for k in range(1, g.nz)]
    at_z = [(z * 4 + col, mp) for z in z_of]

    greeted = [sibling] + ([at_x, at_y] + at_z if g.comm else [])
    barrier = pltpu.get_barrier_semaphore()
    for device in greeted:
        pl.semaphore_signal(barrier, inc=1, device_id=device, device_id_type=MESH)

    def remote(src, dst, send, recv, device):
        return pltpu.make_async_remote_copy(
            src_ref=src, dst_ref=dst, send_sem=send, recv_sem=recv, device_id=device, device_id_type=MESH
        )

    def own(matrices, block=None):
        if not g.comm:
            return matrices
        return matrices.at[:, zi, col] if block is None else block

    local = []

    def bring(src, dst):
        copy = pltpu.make_async_copy(src, dst, r.local_sem.at[len(local)])
        copy.start()
        local.append(copy)
        return copy

    def slot(first, count):
        ref = r.w8.at[pl.ds(first, count)]
        return ref.at[:, zi, col] if g.comm else ref

    def wide_slot(which):
        return r.wf.at[which, zi, col] if g.comm else r.wf.at[which]

    weights = [
        bring(r.qkv_in, slot(QKV, 3)),
        bring(r.so_in, slot(SO, 1)),
        bring(r.cq_in, slot(CQ, 1)),
        bring(r.ckv_in, slot(CKV, 2)),
        bring(r.co_in, slot(CO, 1)),
        bring(r.up_in, wide_slot(UP)),
        bring(r.down_in, wide_slot(DOWN)),
    ]
    bring_enc = bring(r.enc_in, r.enc)
    bring_cot = bring(r.cot_in, r.cot)

    half = g.ff // 2
    gather_groups = [
        ("8", QKV, 3), ("8", SO, 2), ("8", CKV, 2), ("8", CO, 1),
        ("f", UP, 0), ("f", UP, half), ("f", DOWN, 0), ("f", DOWN, half),
    ]
    reduce_groups = [
        ("f", DOWN, 0), ("f", DOWN, half), ("f", UP, 0), ("f", UP, half),
        ("8", CO, 1), ("8", CKV, 2), ("8", CQ, 1), ("8", SO, 1), ("8", QKV, 3),
    ]

    def block_of(group, small, wide, z, c):
        kind, first, more = group
        if kind == "8":
            return small.at[pl.ds(first, more), z, c]
        return wide.at[first, z, c, :, pl.ds(more, half)]

    def column_of(group, small, wide, c):
        kind, first, more = group
        if kind == "8":
            return small.at[pl.ds(first, more), :, c]
        return wide.at[first, :, c, :, pl.ds(more, half)]

    started = []

    def start(copy):
        copy.start()
        started.append(copy)

    def gather_z(i):
        group = gather_groups[i]
        for k in range(g.nz - 1):
            block = block_of(group, r.w8, r.wf, zi, col)
            start(remote(block, block, r.agz_s.at[i, k], r.agz_r.at[i, k], at_z[k]))

    def gather_ab(i):
        group = gather_groups[i]
        for k in range(g.nz - 1):
            block = block_of(group, r.w8, r.wf, z_from[k], col)
            remote(block, block, r.agz_s.at[i, k], r.agz_r.at[i, k], at_z[k]).wait_recv()
        column = column_of(group, r.w8, r.wf, col)
        start(remote(column, column, r.aga_s.at[i], r.aga_r.at[i], at_a))
        start(remote(column, column, r.agb_s.at[i, 0], r.agb_r.at[i, 0], at_b))

    def gather_b(i):
        column = column_of(gather_groups[i], r.w8, r.wf, col_a)
        remote(column, column, r.aga_s.at[i], r.aga_r.at[i], at_a).wait_recv()
        start(remote(column, column, r.agb_s.at[i, 1], r.agb_r.at[i, 1], at_b))

    def gather_end(i):
        for k, c in enumerate((col_b, col_d)):
            column = column_of(gather_groups[i], r.w8, r.wf, c)
            remote(column, column, r.agb_s.at[i, k], r.agb_r.at[i, k], at_b).wait_recv()

    def reduce_b(i):
        group = reduce_groups[i]
        for k, c in enumerate((col_b, col_d)):
            start(remote(
                column_of(group, r.p8, r.pf, c), column_of(group, r.lb8.at[k], r.lbf.at[k], 0),
                r.rsb_s.at[i, k], r.rsb_r.at[i, k], at_b,
            ))

    def each_block(group, body):
        kind, first, more = group
        if kind == "8":
            for j in range(first, first + more):
                @pl.loop(0, g.nz)
                def _(z):
                    body(lambda small, wide, c: small.at[j, z, c])
        else:
            @pl.loop(0, g.nz)
            def _(z):
                body(lambda small, wide, c: wide.at[first, z, c, :, pl.ds(more, half)])

    def add_into(group, c, small, wide):
        def body(view):
            target, landed = view(r.p8, r.pf, c), view(small, wide, 0)
            total = target[...].astype(F32) + landed[...].astype(F32)
            target[...] = total.astype(LOW)
        each_block(group, body)

    def reduce_a(i):
        group = reduce_groups[i]
        for k in (1, 0):
            landed = column_of(group, r.lb8.at[k], r.lbf.at[k], 0)
            remote(landed, landed, r.rsb_s.at[i, k], r.rsb_r.at[i, k], at_b).wait_recv()
            add_into(group, (col, col_a)[k], r.lb8.at[k], r.lbf.at[k])
            if k:
                start(remote(
                    column_of(group, r.p8, r.pf, col_a), column_of(group, r.la8, r.laf, 0),
                    r.rsa_s.at[i], r.rsa_r.at[i], at_a,
                ))

    def reduce_z(i):
        group = reduce_groups[i]
        landed = column_of(group, r.la8, r.laf, 0)
        remote(landed, landed, r.rsa_s.at[i], r.rsa_r.at[i], at_a).wait_recv()
        add_into(group, col, r.la8, r.laf)
        for k in range(g.nz - 1):
            start(remote(
                block_of(group, r.p8, r.pf, z_of[k], col), block_of(group, r.lz8, r.lzf, k, 0),
                r.rsz_s.at[i, k], r.rsz_r.at[i, k], at_z[k],
            ))

    def reduce_end(i):
        kind, first, more = reduce_groups[i]
        for k in range(g.nz - 1):
            landed = block_of(reduce_groups[i], r.lz8, r.lzf, k, 0)
            remote(landed, landed, r.rsz_s.at[i, k], r.rsz_r.at[i, k], at_z[k]).wait_recv()
        if kind == "8":
            for j in range(first, first + more):
                total = r.p8[j, zi, col].astype(F32)
                for k in range(g.nz - 1):
                    total = total + r.lz8[j, k, 0].astype(F32)
                r.g8_out[j] = total
        else:
            cols = pl.ds(more, half)
            total = r.pf[first, zi, col, :, cols].astype(F32)
            for k in range(g.nz - 1):
                total = total + r.lzf[first, k, 0, :, cols].astype(F32)
            r.gf_out[first, :, cols] = total

    n_reduce = len(reduce_groups)

    def reduce_start(i):
        if not g.comm:
            return
        if i < n_reduce:
            reduce_b(i)
        if 0 <= i - 3 < n_reduce:
            reduce_end(i - 3)
        if 0 <= i - 2 < n_reduce:
            reduce_z(i - 2)
        if 0 <= i - 1 < n_reduce:
            reduce_a(i - 1)

    def w8(j):
        return r.w8[j].reshape(g.d, g.f)

    def wide(which, cols):
        if g.comm:
            return r.wf[which, :, :, :, cols].reshape(g.d, -1)
        return r.wf[which, :, cols]

    def put8(j, value):
        r.p8[j] = value.astype(LOW).reshape(r.p8.shape[1:])

    def put_wide(which, cols, value):
        if g.comm:
            r.pf[which, :, :, :, cols] = value.astype(LOW).reshape(g.nz, 4, g.blk, -1)
        else:
            r.pf[which, :, cols] = value.astype(LOW)

    part = g.t // 2

    def exchange(e, i):
        rows = pl.ds(i * part, part)
        return remote(
            r.stage.at[e % 2, rows], r.land.at[e % 3, rows], r.ex_s.at[e, i], r.ex_r.at[e, i], sibling
        )

    def exchange_start(e, product):
        for i in range(2):
            rows = pl.ds(i * part, part)
            r.stage[e % 2, rows] = product(rows).astype(LOW)
            exchange(e, i).start()

    def by_rows(e, body):
        for i in range(2):
            exchange(e, i).wait_recv()
            exchange(e, i).wait_send()

            @pl.loop(0, part // LN_ROWS)
            def _(n):
                rows = pl.ds(pl.multiple_of(i * part + n * LN_ROWS, LN_ROWS), LN_ROWS)
                body(rows, r.stage[e % 2, rows].astype(F32) + r.land[e % 3, rows].astype(F32))

    def norm(values, i):
        return (centre(values)[0] * r.gains[i]).astype(LOW)

    def norm_back(i, values, grad):
        normed, scale = centre(values)
        r.gain_sum[i] += jnp.sum((grad * normed).reshape(-1, 8, g.d), axis=0)
        scaled = grad * r.gains[i]
        return scale * (
            scaled
            - jnp.mean(scaled, axis=-1, keepdims=True)
            - normed * jnp.mean(scaled * normed, axis=-1, keepdims=True)
        )

    masks = head_masks()
    score_scale = HEAD ** (-0.5)
    pairs = g.f // PAIR

    pl.semaphore_wait(barrier, len(greeted))
    small = []

    def meet(src, dst, i, device):
        copy = remote(src, dst, r.small_s.at[i], r.small_r.at[i], device)
        copy.start()
        small.append(copy)
        return copy

    if g.comm:
        for k in range(g.nz - 1):
            meet(r.gains_in, r.gain_land.at[k], k, at_z[k])
        weights[0].wait()
        gather_z(0)
        weights[1].wait()
        weights[2].wait()
        gather_z(1)
        for k in range(g.nz - 1):
            small[k].wait_recv()
        total = r.gains_in[...].astype(F32)
        for k in range(g.nz - 1):
            total = total + r.gain_land[k].astype(F32)
        r.gain_pass[0] = total.astype(LOW)
        meet(r.gain_pass.at[0], r.gain_land.at[g.nz - 1], g.nz - 1, at_x).wait_recv()
        total = total + r.gain_land[g.nz - 1].astype(F32)
        r.gain_pass[1] = total.astype(LOW)
        meet(r.gain_pass.at[1], r.gain_land.at[g.nz], g.nz, at_y).wait_recv()
        total = total + r.gain_land[g.nz].astype(F32)
        for copy in weights[3:]:
            copy.wait()
    else:
        total = r.gains_in[...].astype(F32)
        for copy in weights:
            copy.wait()
    for i in range(3):
        r.gains[i] = total[i:i + 1]

    def gather_steps(*steps):
        if g.comm:
            for step, i in steps:
                step(i)

    gather_steps((gather_ab, 0), (gather_z, 2))

    r.gain_sum[...] = jnp.zeros_like(r.gain_sum)

    @pl.loop(0, g.t // LN_ROWS)
    def _(n):
        rows = pl.ds(pl.multiple_of(n * LN_ROWS, LN_ROWS), LN_ROWS)
        r.a1[rows] = norm(r.hidden[rows].astype(F32), 0)

    seg_down = r.seg[...].T
    for p in range(g.t // PAIR):
        key = lax.broadcasted_iota(jnp.int32, (PAIR, PAIR), 0)
        query = lax.broadcasted_iota(jnp.int32, (PAIR, PAIR), 1)
        allowed = (key <= query) & (seg_down[:, p:p + 1] == r.seg[p:p + 1, :])
        r.bias[p] = jnp.where(allowed, 0.0, NEGATIVE)

    gather_steps((gather_b, 0), (gather_ab, 1), (gather_z, 3), (gather_end, 0), (gather_b, 1), (gather_ab, 2), (gather_z, 4))
    for j in range(3):
        r.qkv[j] = dot(r.a1[...], w8(QKV + j), 1, 0).astype(LOW)

    @pl.loop(0, g.t // PAIR)
    def _(p):
        rows = pl.ds(pl.multiple_of(p * PAIR, PAIR), PAIR)
        bias = jnp.concatenate([r.bias[p]] * 2, axis=1)
        for h in range(pairs):
            lanes = lanes_of(h)
            queries = stack_heads(r.qkv[0, rows, lanes], masks)
            scores = dot(r.qkv[1, rows, lanes], queries, 1, 1) * score_scale + bias
            weights_low = softmax_keys(scores).astype(LOW)
            r.self_p[p, h] = weights_low
            r.mixed[rows, lanes] = join_heads(dot(weights_low, r.qkv[2, rows, lanes], 0, 0)).astype(LOW)

    gather_steps((gather_end, 1), (gather_b, 2), (gather_ab, 3), (gather_z, 5))
    exchange_start(0, lambda rows: dot(r.mixed[rows], w8(SO), 1, 1))

    def after_self(rows, total):
        resid = r.hidden[rows].astype(F32) + total
        r.resid_one[rows] = resid
        r.a2[rows] = norm(resid, 1)

    by_rows(0, after_self)
    r.cq[...] = dot(r.a2[...], w8(CQ), 1, 0).astype(LOW)

    gather_steps((gather_end, 2), (gather_b, 3), (gather_ab, 4), (gather_z, 6))
    bring_enc.wait()
    for m in range(2):
        for image in range(g.images):
            rows = pl.ds(image * g.ctx, g.ctx)
            r.kv[m, image] = dot(r.enc[rows], w8(CKV + m), 1, 0).astype(LOW)
        if m == 0:
            gather_steps((gather_b, 4), (gather_ab, 5), (gather_z, 7))

    @pl.loop(0, g.rows)
    def _(row):
        rows = pl.ds(pl.multiple_of(row * g.seq, g.seq), g.seq)
        image = (row // g.row_mb) * g.img_mb + r.image_ids[row]
        for h in range(pairs):
            lanes = lanes_of(h)
            queries = stack_heads(r.cq[rows, lanes], masks)
            scores = dot(r.kv[0, image, :, lanes], queries, 1, 1) * score_scale
            weights_low = softmax_keys(scores).astype(LOW)
            r.cross_p[row * pairs + h] = weights_low
            r.cmixed[rows, lanes] = join_heads(dot(weights_low, r.kv[1, image, :, lanes], 0, 0)).astype(LOW)

    gather_steps((gather_end, 3), (gather_b, 5), (gather_ab, 6))
    exchange_start(1, lambda rows: dot(r.cmixed[rows], w8(CO), 1, 1))

    def after_cross(rows, total):
        resid = r.resid_one[rows] + total
        r.resid_two[rows] = resid
        r.a3[rows] = norm(resid, 2)

    by_rows(1, after_cross)
    bring_cot.wait()

    def up_half(first):
        @pl.loop(0, half // TILE)
        def _(n):
            cols = pl.ds(pl.multiple_of(first + n * TILE, TILE), TILE)
            pre = dot(r.a3[...], wide(UP, cols), 1, 0)
            below = 0.5 * (1.0 + lax.erf(pre * ROOT_HALF))
            r.act[:, cols] = (pre * below).astype(LOW)
            slope = below + pre * (DENSITY * jnp.exp(-0.5 * (pre * pre)))
            r.slope[:, cols] = slope.astype(r.slope.dtype)

    def grad_wide(which, left, right, first):
        cols = pl.ds(first, half)
        put_wide(which, cols, dot(left[...], right[:, cols], 0, 0))

    gather_steps((gather_end, 4), (gather_b, 6), (gather_ab, 7))
    up_half(0)
    gather_steps((gather_end, 5), (gather_b, 7))
    up_half(half)
    grad_wide(DOWN, r.cot, r.act, 0)
    reduce_start(0)
    grad_wide(DOWN, r.cot, r.act, half)

    gather_steps((gather_end, 6), (gather_end, 7))
    reduce_start(1)
    everything = pl.ds(0, g.ff)
    exchange_start(2, lambda rows: dot(r.act[rows], wide(DOWN, everything), 1, 1))

    @pl.loop(0, g.ff // TILE)
    def _(n):
        cols = pl.ds(pl.multiple_of(n * TILE, TILE), TILE)
        grad_act = dot(r.cot[...], wide(DOWN, cols), 1, 0)
        r.slope[:, cols] = (grad_act * r.slope[:, cols].astype(F32)).astype(LOW)

    exchange_start(3, lambda rows: dot(r.slope[rows], wide(UP, everything), 1, 1))
    grad_wide(UP, r.a3, r.slope, 0)
    reduce_start(2)
    grad_wide(UP, r.a3, r.slope, half)
    reduce_start(3)

    def after_down(rows, total):
        r.a3[rows] = (r.resid_two[rows] + total).astype(LOW)

    by_rows(2, after_down)
    write_out = pltpu.make_async_copy(r.a3, r.out, r.write_sem.at[0])
    write_out.start()

    def after_up(rows, total):
        grad = r.cot[rows].astype(F32) + norm_back(2, r.resid_two[rows], total)
        r.grad[rows] = grad
        r.grad_low[rows] = grad.astype(LOW)

    by_rows(3, after_up)
    put8(CO, dot(r.grad_low[...], r.cmixed[...], 0, 0))
    reduce_start(4)
    r.g_mixed[...] = dot(r.grad_low[...], w8(CO), 1, 0).astype(LOW)

    @pl.loop(0, g.micro)
    def _(m):
        for h in range(pairs):
            lanes = lanes_of(h)
            queries, grads, soft = [], [], []
            for n in range(g.row_mb):
                row = m * g.row_mb + n
                rows = pl.ds(pl.multiple_of(row * g.seq, g.seq), g.seq)
                image = m * g.img_mb + r.image_ids[row]
                grads.append(stack_heads(r.g_mixed[rows, lanes], masks))
                queries.append(stack_heads(r.cq[rows, lanes], masks))
                weights_low = r.cross_p[row * pairs + h]
                soft.append(weights_low)
                prob = weights_low.astype(F32)
                grad_p = dot(r.kv[1, image, :, lanes], grads[-1], 1, 1)
                inner = jnp.sum(prob * grad_p, axis=0, keepdims=True)
                grad_s = (prob * (grad_p - inner)).astype(LOW)
                r.cross_ds[:, lanes_of(n)] = grad_s
                grad_q = join_heads(dot(grad_s, r.kv[0, image, :, lanes], 0, 0)) * score_scale
                r.g_cq[rows, lanes] = grad_q.astype(LOW)
            soft = jnp.concatenate(soft, axis=1)
            for i in range(g.img_mb):
                chosen = [
                    jnp.where(r.image_ids[m * g.row_mb + n] == i, jnp.ones((1, PAIR), F32), 0.0).astype(LOW)
                    for n in range(g.row_mb)
                ]
                picked = jnp.concatenate([q * c for q, c in zip(queries, chosen)], axis=0)
                r.kv[0, m * g.img_mb + i, :, lanes] = (dot(r.cross_ds[...], picked, 1, 0) * score_scale).astype(LOW)
                picked = jnp.concatenate([v * c for v, c in zip(grads, chosen)], axis=0)
                r.kv[1, m * g.img_mb + i, :, lanes] = dot(soft, picked, 1, 0).astype(LOW)

    exchange_start(4, lambda rows: dot(r.g_cq[rows], w8(CQ), 1, 1))
    for j in range(2):
        put8(CKV + j, dot(r.enc[...], r.kv[j].reshape(g.images * g.ctx, g.f), 0, 0))
    reduce_start(5)
    put8(CQ, dot(r.a2[...], r.g_cq[...], 0, 0))
    reduce_start(6)

    def after_query(rows, total):
        grad = r.grad[rows] + norm_back(1, r.resid_one[rows], total)
        r.grad[rows] = grad
        r.grad_low[rows] = grad.astype(LOW)

    by_rows(4, after_query)
    put8(SO, dot(r.grad_low[...], r.mixed[...], 0, 0))
    reduce_start(7)
    r.g_mixed[...] = dot(r.grad_low[...], w8(SO), 1, 0).astype(LOW)

    @pl.loop(0, g.t // PAIR)
    def _(p):
        rows = pl.ds(pl.multiple_of(p * PAIR, PAIR), PAIR)
        for h in range(pairs):
            lanes = lanes_of(h)
            queries = stack_heads(r.qkv[0, rows, lanes], masks)
            grads = stack_heads(r.g_mixed[rows, lanes], masks)
            weights_low = r.self_p[p, h]
            prob = weights_low.astype(F32)
            grad_p = dot(r.qkv[2, rows, lanes], grads, 1, 1)
            inner = jnp.sum(prob * grad_p, axis=0, keepdims=True)
            grad_s = (prob * (grad_p - inner)).astype(LOW)
            grad_q = join_heads(dot(grad_s, r.qkv[1, rows, lanes], 0, 0)) * score_scale
            grad_k = dot(grad_s, queries, 1, 0) * score_scale
            grad_v = dot(weights_low, grads, 1, 0)
            r.qkv[0, rows, lanes] = grad_q.astype(LOW)
            r.qkv[1, rows, lanes] = grad_k.astype(LOW)
            r.qkv[2, rows, lanes] = grad_v.astype(LOW)

    for j in range(3):
        put8(QKV + j, dot(r.a1[...], r.qkv[j], 0, 0))
    reduce_start(8)
    exchange_start(
        5,
        lambda rows: dot(r.qkv[0, rows], w8(QKV), 1, 1)
        + dot(r.qkv[1, rows], w8(QKV + 1), 1, 1)
        + dot(r.qkv[2, rows], w8(QKV + 2), 1, 1),
    )

    def features(j, h):
        if g.comm:
            return r.w8[j, pl.ds(h * (g.nz // 2), g.nz // 2)].reshape(g.d // 2, g.f)
        return r.w8[j, pl.ds(pl.multiple_of(h * (g.d // 2), g.d // 2), g.d // 2)]

    def encoder_part(image, h):
        return dot(r.kv[0, image], features(CKV, h), 1, 1) + dot(r.kv[1, image], features(CKV + 1, h), 1, 1)

    strips = g.d // 2 // PAIR

    def encoder_keep(image, value):
        for h in range(strips):
            r.cross_p[image * strips + h] = value[:, h * PAIR:(h + 1) * PAIR].astype(LOW)

    def encoder_copy(image):
        part = pl.ds(image * strips, strips)
        return remote(r.cross_p.at[part], r.enc_land.at[part], r.enc_s.at[image], r.enc_r.at[image], sibling)

    for image in range(g.images):
        encoder_keep(image, encoder_part(image, 1 - mp))
        encoder_copy(image).start()

    def after_qkv(rows, total):
        grad = r.grad[rows] + norm_back(0, r.hidden[rows].astype(F32), total)
        r.grad[rows] = grad

    by_rows(5, after_qkv)
    write = [write_out, pltpu.make_async_copy(r.grad, r.in_grad, r.write_sem.at[1])]
    write[1].start()

    for i in range(3):
        r.gain_total[0, i:i + 1] = jnp.sum(r.gain_sum[i], axis=0, keepdims=True)
    if g.comm:
        first = len(small)
        meet(r.gain_total.at[0], r.total_land.at[0], first, at_x).wait_recv()
        r.gain_total[1] = r.gain_total[0] + r.total_land[0]
        meet(r.gain_total.at[1], r.total_land.at[1], first + 1, at_y).wait_recv()
        r.gain_total[2] = r.gain_total[1] + r.total_land[1]
        for k in range(g.nz - 1):
            meet(r.gain_total.at[2], r.total_land.at[2 + k], first + 2 + k, at_z[k])

    reduce_start(9)
    for image in range(g.images):
        encoder_copy(image).wait_recv()
        encoder_copy(image).wait_send()
        landed = jnp.concatenate([r.enc_land[image * strips + h] for h in range(strips)], axis=1)
        encoder_keep(image, encoder_part(image, mp) + landed.astype(F32))
        rows = pl.ds(image * g.ctx, g.ctx)
        for h in range(strips):
            write.append(pltpu.make_async_copy(
                r.cross_p.at[image * strips + h], r.enc_grad.at[rows, lanes_of(h)],
                r.write_sem.at[2 + image * strips + h],
            ))
            write[-1].start()
    reduce_start(10)
    reduce_start(11)
    if g.comm:
        total = r.gain_total[2]
        for k in range(g.nz - 1):
            small[first + 2 + k].wait_recv()
            total = total + r.total_land[2 + k]
        r.gain_out[...] = total
    else:
        r.gain_out[...] = r.gain_total[0]
    for copy in write:
        copy.wait()
    for copy in small + started:
        copy.wait_send()


def run_layer(g, operands):
    vmem = pl.BlockSpec(memory_space=pltpu.VMEM)
    smem = pl.BlockSpec(memory_space=pltpu.SMEM)
    anywhere = pl.BlockSpec(memory_space=pl.ANY)
    shape = jax.ShapeDtypeStruct
    ins = dict(
        image_ids=smem, seg=vmem, hidden=vmem, gains_in=vmem, cot_in=anywhere, enc_in=anywhere,
        qkv_in=anywhere, so_in=anywhere, cq_in=anywhere, ckv_in=anywhere, co_in=anywhere,
        up_in=anywhere, down_in=anywhere,
    )
    outs = dict(
        out=(shape((g.t, g.d), LOW), anywhere),
        in_grad=(shape((g.t, g.d), F32), anywhere),
        enc_grad=(shape((g.images * g.ctx, g.d // 2), LOW), anywhere),
        gain_out=(shape((8, g.d), F32), vmem),
    )
    grid = (g.nz, 4, g.blk) if g.comm else (g.d,)
    dma = pltpu.SemaphoreType.DMA
    scratch = dict(
        w8=pltpu.VMEM((MATS, *grid, g.f), LOW),
        wf=pltpu.VMEM((2, *grid, g.ff), LOW),
        enc=pltpu.VMEM((g.images * g.ctx, g.d), LOW),
        cot=pltpu.VMEM((g.t, g.d), LOW),
        gains=pltpu.VMEM((3, 1, g.d), F32),
        gain_sum=pltpu.VMEM((3, 8, g.d), F32),
        gain_total=pltpu.VMEM((3, 8, g.d), F32),
        bias=pltpu.VMEM((g.t // PAIR, PAIR, PAIR), F32),
        a1=pltpu.VMEM((g.t, g.d), LOW),
        a2=pltpu.VMEM((g.t, g.d), LOW),
        a3=pltpu.VMEM((g.t, g.d), LOW),
        qkv=pltpu.VMEM((3, g.t, g.f), LOW),
        mixed=pltpu.VMEM((g.t, g.f), LOW),
        cq=pltpu.VMEM((g.t, g.f), LOW),
        cmixed=pltpu.VMEM((g.t, g.f), LOW),
        g_mixed=pltpu.VMEM((g.t, g.f), LOW),
        g_cq=pltpu.VMEM((g.t, g.f), LOW),
        kv=pltpu.VMEM((2, g.images, g.ctx, g.f), LOW),
        self_p=pltpu.VMEM((g.t // PAIR, g.f // PAIR, PAIR, 2 * PAIR), LOW),
        cross_p=pltpu.VMEM((g.rows * (g.f // PAIR), g.ctx, PAIR), LOW),
        cross_ds=pltpu.VMEM((g.ctx, g.row_mb * PAIR), LOW),
        resid_one=pltpu.VMEM((g.t, g.d), F32),
        resid_two=pltpu.VMEM((g.t, g.d), F32),
        grad=pltpu.VMEM((g.t, g.d), F32),
        grad_low=pltpu.VMEM((g.t, g.d), LOW),
        act=pltpu.VMEM((g.t, g.ff), LOW),
        slope=pltpu.VMEM((g.t, g.ff), LOW),
        stage=pltpu.VMEM((2, g.t, g.d), LOW),
        land=pltpu.VMEM((3, g.t, g.d), LOW),
        enc_land=pltpu.VMEM((g.images * (g.d // 2 // PAIR), g.ctx, PAIR), LOW),
        local_sem=dma((9,)),
        ex_s=dma((6, 2)), ex_r=dma((6, 2)),
        enc_s=dma((g.images,)), enc_r=dma((g.images,)),
        write_sem=dma((2 + g.images * (g.d // 2 // PAIR),)),
    )
    if g.comm:
        outs.update(
            g8_out=(shape((MATS, g.blk, g.f), F32), vmem),
            gf_out=(shape((2, g.blk, g.ff), F32), vmem),
        )
        hops = g.nz - 1
        scratch.update(
            p8=pltpu.VMEM((MATS, *grid, g.f), LOW),
            pf=pltpu.VMEM((2, *grid, g.ff), LOW),
            lb8=pltpu.VMEM((2, MATS, g.nz, 1, g.blk, g.f), LOW),
            lbf=pltpu.VMEM((2, 2, g.nz, 1, g.blk, g.ff), LOW),
            la8=pltpu.VMEM((MATS, g.nz, 1, g.blk, g.f), LOW),
            laf=pltpu.VMEM((2, g.nz, 1, g.blk, g.ff), LOW),
            lz8=pltpu.VMEM((MATS, hops, 1, g.blk, g.f), LOW),
            lzf=pltpu.VMEM((2, hops, 1, g.blk, g.ff), LOW),
            gain_land=pltpu.VMEM((hops + 2, 16, g.d), LOW),
            gain_pass=pltpu.VMEM((2, 16, g.d), LOW),
            total_land=pltpu.VMEM((hops + 2, 8, g.d), F32),
            agz_s=dma((8, hops)), agz_r=dma((8, hops)),
            aga_s=dma((8,)), aga_r=dma((8,)),
            agb_s=dma((8, 2)), agb_r=dma((8, 2)),
            rsz_s=dma((9, hops)), rsz_r=dma((9, hops)),
            rsa_s=dma((9,)), rsa_r=dma((9,)),
            rsb_s=dma((9, 2)), rsb_r=dma((9, 2)),
            small_s=dma((2 * hops + 4,)), small_r=dma((2 * hops + 4,)),
        )
    else:
        outs.update(
            p8=(shape((MATS, g.d, g.f), LOW), vmem),
            pf=(shape((2, g.d, g.ff), LOW), vmem),
        )
    g.names = (*ins, *outs, *scratch)
    return dict(zip(outs, pl.pallas_call(
        functools.partial(layer, g),
        out_shape=[o[0] for o in outs.values()],
        in_specs=list(ins.values()),
        out_specs=[o[1] for o in outs.values()],
        scratch_shapes=list(scratch.values()),
        compiler_params=pltpu.CompilerParams(
            collective_id=0, has_side_effects=True, vmem_limit_bytes=62 * 2**20
        ),
        name="layer",
    )(*operands)))


def body(
    dp, mp, hidden, encoder_tokens, segment_ids, image_index, cotangent, norm_gains, qkv_weight,
    self_out_weight, cross_query_weight, cross_kv_weight, cross_out_weight, up_weight, down_weight,
):
    micro, row_mb, seq, d = hidden.shape
    img_mb, ctx = encoder_tokens.shape[1:3]
    blk, f = self_out_weight.shape
    g = SimpleNamespace(
        micro=micro, row_mb=row_mb, seq=seq, d=d, img_mb=img_mb, ctx=ctx, blk=blk, f=f,
        ff=up_weight.shape[1], rows=micro * row_mb, t=micro * row_mb * seq, images=micro * img_mb,
        nz=dp // 4, comm=dp % 4 == 0 and blk % 16 == 0,
    )
    row = jnp.arange(g.rows) % (PAIR // seq)
    seg = (segment_ids.reshape(g.rows, seq) + 64 * row[:, None]).astype(F32).reshape(g.t // PAIR, PAIR)
    seg = jnp.pad(seg, ((0, -seg.shape[0] % 8), (0, 0)))
    me = lax.axis_index("dp")
    if g.comm:
        gains = lax.dynamic_update_slice(jnp.zeros((16, d), LOW), norm_gains, (0, me * blk))
        weights = (qkv_weight, self_out_weight, cross_query_weight, cross_kv_weight, cross_out_weight, up_weight, down_weight)
    else:
        gains = jnp.pad(lax.all_gather(norm_gains, "dp", axis=1, tiled=True), ((0, 13), (0, 0)))
        weights = [
            lax.all_gather(w, "dp", axis=w.ndim - 2, tiled=True)
            for w in (qkv_weight, self_out_weight, cross_query_weight, cross_kv_weight, cross_out_weight, up_weight, down_weight)
        ]
    weights = list(weights)
    for i in (1, 2, 4):
        weights[i] = weights[i][None]
    o = run_layer(g, (
        image_index.reshape(g.rows), seg, hidden.reshape(g.t, d), gains, cotangent.reshape(g.t, d),
        encoder_tokens.reshape(g.images * ctx, d), *weights,
    ))
    if g.comm:
        small, wide = o["g8_out"], o["gf_out"]
        gain_grad = lax.dynamic_slice(o["gain_out"], (0, me * blk), (3, blk))
    else:
        small = lax.psum_scatter(o["p8"].astype(F32), "dp", scatter_dimension=1, tiled=True)
        wide = lax.psum_scatter(o["pf"].astype(F32), "dp", scatter_dimension=1, tiled=True)
        gain_grad = lax.psum_scatter(o["gain_out"][:3], "dp", scatter_dimension=1, tiled=True)
    return (
        o["out"].reshape(hidden.shape),
        o["in_grad"].reshape(hidden.shape),
        o["enc_grad"].astype(F32).reshape(micro, img_mb, ctx, d // 2),
        gain_grad,
        small[QKV:QKV + 3],
        small[SO],
        small[CQ],
        small[CKV:CKV + 2],
        small[CO],
        wide[UP],
        wide[DOWN],
    )


def solution(mesh):
    tokens, kept = P(None, "dp", None, None), P("dp", "mp")
    three = P(None, "dp", "mp")
    return jax.shard_map(
        functools.partial(body, mesh.shape["dp"], mesh.shape["mp"]),
        mesh=mesh,
        in_specs=(
            tokens, tokens, P(None, "dp", None), P(None, "dp"), tokens, P(None, "dp"),
            three, kept, kept, three, kept, kept, kept,
        ),
        out_specs=(
            tokens, tokens, P(None, "dp", None, "mp"), P(None, "dp"),
            three, kept, kept, three, kept, kept, kept,
        ),
        check_vma=False,
    )
```

```python
import functools
from types import SimpleNamespace

import jax
import jax.numpy as jnp
from jax import lax
from jax.experimental import pallas as pl
from jax.experimental.pallas import tpu as pltpu
from jax.sharding import PartitionSpec as P

HEAD = 64
PAIR = 2 * HEAD
EPSILON = 1e-05
NEGATIVE = -1e30
ROOT_HALF = 0.7071067811865476
DENSITY = 0.3989422804014327
MESH = pl.DeviceIdType.MESH
LOW = jnp.bfloat16
F32 = jnp.float32
QKV, SO, CQ, CKV, CO, MATS = 0, 3, 4, 5, 7, 8
UP, DOWN = 0, 1
LN_ROWS = 64
TILE = 256


def dot(left, right, left_dim, right_dim):
    return lax.dot_general(
        left, right, (((left_dim,), (right_dim,)), ((), ())), preferred_element_type=F32
    )


def lanes_of(pair):
    return pl.ds(pair * PAIR, PAIR)


def head_masks():
    lane = lax.broadcasted_iota(jnp.int32, (1, PAIR), 1)
    first = jnp.where(lane < HEAD, 1.0, 0.0)
    return first.astype(LOW), (1.0 - first).astype(LOW)


def stack_heads(values, masks):
    return jnp.concatenate([values * masks[0], values * masks[1]], axis=0)


def join_heads(stacked):
    half = stacked.shape[0] // 2
    lane = lax.broadcasted_iota(jnp.int32, (half, PAIR), 1)
    return jnp.where(lane < HEAD, stacked[:half], stacked[half:])


def centre(values):
    centred = values - jnp.mean(values, axis=-1, keepdims=True)
    spread = jnp.mean(centred * centred, axis=-1, keepdims=True)
    scale = lax.rsqrt(spread + EPSILON)
    return centred * scale, scale


def softmax_keys(scores):
    shifted = jnp.exp(scores - jnp.max(scores, axis=0, keepdims=True))
    return shifted / jnp.sum(shifted, axis=0, keepdims=True)


def layer(g, *refs):
    r = SimpleNamespace(**dict(zip(g.names, refs)))
    me, mp = lax.axis_index("dp"), lax.axis_index("mp")
    zi, col = me // 4, me % 4
    sibling = (me, 1 - mp)
    col_x = col + 1 - 2 * (col % 2)
    col_y = (col + 2) % 4
    col_d = (col_x + 2) % 4
    col_a = mp * col_x + (1 - mp) * col_y
    col_b = mp * col_y + (1 - mp) * col_x
    at_x, at_y = (zi * 4 + col_x, mp), (zi * 4 + col_y, mp)
    at_a, at_b = (zi * 4 + col_a, mp), (zi * 4 + col_b, mp)
    z_of = [(zi + k) % g.nz for k in range(1, g.nz)]
    z_from = [(zi + g.nz - k) % g.nz for k in range(1, g.nz)]
    at_z = [(z * 4 + col, mp) for z in z_of]

    greeted = [sibling] + ([at_x, at_y] + at_z if g.comm else [])
    barrier = pltpu.get_barrier_semaphore()
    for device in greeted:
        pl.semaphore_signal(barrier, inc=1, device_id=device, device_id_type=MESH)

    def remote(src, dst, send, recv, device):
        return pltpu.make_async_remote_copy(
            src_ref=src, dst_ref=dst, send_sem=send, recv_sem=recv, device_id=device, device_id_type=MESH
        )

    local = []

    def bring(src, dst):
        copy = pltpu.make_async_copy(src, dst, r.local_sem.at[len(local)])
        copy.start()
        local.append(copy)
        return copy

    def slot(first, count):
        ref = r.w8.at[pl.ds(first, count)]
        return ref.at[:, zi, col] if g.comm else ref

    def wide_slot(which):
        return r.wf.at[which, zi, col] if g.comm else r.wf.at[which]

    weights = [
        bring(r.qkv_in, slot(QKV, 3)),
        bring(r.so_in, slot(SO, 1)),
        bring(r.cq_in, slot(CQ, 1)),
        bring(r.ckv_in, slot(CKV, 2)),
        bring(r.co_in, slot(CO, 1)),
        bring(r.up_in, wide_slot(UP)),
        bring(r.down_in, wide_slot(DOWN)),
    ]
    bring_hidden = bring(r.hidden_in, r.hidden)
    bring_enc = bring(r.enc_in, r.enc)
    bring_cot = bring(r.cot_in, r.cot)

    half = g.ff // 2

    def mats(first, ref, at):
        part = pl.ds(first, 1)

        def each(c, body):
            @pl.loop(0, g.nz)
            def _(z):
                body(r.p8.at[first, z, c], lambda landed: landed.at[0, z])

        return SimpleNamespace(
            src=lambda: ref.at[pl.ds(at, 1)],
            w=lambda z, c: r.w8.at[part, z, c], w_column=lambda c: r.w8.at[part, :, c],
            w_row=lambda z: r.w8.at[part, z], p_row=lambda z: r.p8.at[part, z],
            p=lambda z, c: r.p8.at[part, z, c], p_column=lambda c: r.p8.at[part, :, c],
            lb=lambda k: r.lb8.at[k, part], la=lambda: r.la8.at[part], lz=lambda k: r.lz8.at[k, part],
            lx=lambda: r.lx8.at[part], in_row=lambda row, c: row.at[:, c],
            tz=lambda k: r.turn8_z.at[k], tb=lambda k: r.turn8_b.at[k], ta=lambda: r.turn8_a,
            tx=lambda: r.turn8_x, each=each, sum=lambda: r.g8.at[part], sum_out=lambda: r.g8_out.at[part],
        )

    def strip(which, first, i, ref):
        cols = pl.ds(first, half)

        def each(c, body):
            @pl.loop(0, g.nz)
            def _(z):
                body(r.pf.at[which, z, c, :, cols], lambda landed: landed.at[z])

        return SimpleNamespace(
            src=lambda: ref.at[:, cols],
            w=lambda z, c: r.wf.at[which, z, c, :, cols], w_column=lambda c: r.wf.at[which, :, c, :, cols],
            w_row=lambda z: r.wf.at[which, z, :, :, cols], p_row=lambda z: r.pf.at[which, z, :, :, cols],
            p=lambda z, c: r.pf.at[which, z, c, :, cols], p_column=lambda c: r.pf.at[which, :, c, :, cols],
            lb=lambda k: r.lbf.at[k, i], la=lambda: r.laf.at[i], lz=lambda k: r.lzf.at[k, i],
            lx=lambda: r.lxf.at[i], in_row=lambda row, c: row.at[c],
            tz=lambda k: r.turnf_z.at[k], tb=lambda k: r.turnf_b.at[k], ta=lambda: r.turnf_a,
            tx=lambda: r.turnf_x, each=each, sum=lambda: r.gf.at[which, :, cols],
            sum_out=lambda: r.gf_out.at[which, :, cols],
        )

    groups = dict(
        q=mats(QKV, r.qkv_in, 0), k=mats(QKV + 1, r.qkv_in, 1), v=mats(QKV + 2, r.qkv_in, 2),
        ck=mats(CKV, r.ckv_in, 0), cv=mats(CKV + 1, r.ckv_in, 1),
        so=mats(SO, r.so_in, 0), cq=mats(CQ, r.cq_in, 0), co=mats(CO, r.co_in, 0),
        up0=strip(UP, 0, 0, r.up_in), up1=strip(UP, half, 1, r.up_in),
        dn0=strip(DOWN, 0, 2, r.down_in), dn1=strip(DOWN, half, 3, r.down_in),
    )
    for i, (name, group) in enumerate(groups.items()):
        group.i, group.turned = i, name in ("co", "dn1")

    inner = (zi == 1) | (zi == 2)
    goes = (zi != 3, None, zi != 0)
    hops = range(3)
    other = 3 * (2 - zi)
    onward = 3 * (zi - 1)
    filled = 2 * jnp.where(zi == 0, 1, 0)

    written = []

    def write(src, dst):
        copy = pltpu.make_async_copy(src, dst, r.write_sem.at[len(written)])
        copy.start()
        written.append(copy)

    started = []

    def only(condition, act):
        if condition is None:
            act()
        else:
            pl.when(condition)(act)

    def start(copy, condition=None):
        only(condition, copy.start)
        started.append((copy, condition))

    def arrived(ref, send, recv, device, condition=None):
        only(condition, remote(ref, ref, send, recv, device).wait_recv)

    def gather_z(name):
        t = groups[name]
        for k in hops:
            src, dst = (t.w_row(zi), t.w_row(zi)) if t.turned else (t.src(), t.w(zi, col))
            start(remote(src, dst, r.agz_s.at[t.i, k], r.agz_r.at[t.i, k], at_z[k]), goes[k])

    def z_part(t, z):
        return t.w_row(z) if t.turned else t.w(z, col)

    def gather_on(name):
        t = groups[name]
        arrived(z_part(t, z_from[1]), r.agz_s.at[t.i, 1], r.agz_r.at[t.i, 1], at_z[1])
        part = z_part(t, jnp.where(inner, other, 0))
        start(
            remote(part, part, r.agz_s.at[t.i, 3], r.agz_r.at[t.i, 2 * jnp.where(zi == 2, 1, 0)],
                   (jnp.where(inner, onward, 0) * 4 + col, mp)),
            inner,
        )

    def to_both(t, i, src, dst):
        start(remote(src, dst, r.aga_s.at[t.i, i], r.aga_r.at[t.i, i], at_a))
        start(remote(src, dst, r.agb_s.at[t.i, i], r.agb_r.at[t.i, i], at_b))

    def gather_own(name):
        t = groups[name]
        to_both(t, 0, t.src(), t.w(zi, col))

    def gather_a(name):
        t = groups[name]
        for k in (1, 0, 2):
            block = t.w(z_from[k], col)
            if k != 1:
                arrived(block, r.agz_s.at[t.i, k], r.agz_r.at[t.i, k], at_z[k])
            to_both(t, 1 + k, block, block)

    def gather_b(name):
        t = groups[name]
        arrived(t.w(zi, col_a), r.aga_s.at[t.i, 0], r.aga_r.at[t.i, 0], at_a)
        part = t.w(zi, col_a)
        if not t.turned:
            for k in hops:
                arrived(t.w(z_from[k], col_a), r.aga_s.at[t.i, 1 + k], r.aga_r.at[t.i, 1 + k], at_a)
            part = t.w_column(col_a)
        start(remote(part, part, r.agb_s.at[t.i, 4], r.agb_r.at[t.i, 4], at_b))

    def gather_end(name):
        t = groups[name]
        arrived(t.w(zi, col_b), r.agb_s.at[t.i, 0], r.agb_r.at[t.i, 0], at_b)
        if not t.turned:
            for k in hops:
                arrived(t.w(z_from[k], col_b), r.agb_s.at[t.i, 1 + k], r.agb_r.at[t.i, 1 + k], at_b)
        part = t.w(zi, col_d) if t.turned else t.w_column(col_d)
        arrived(part, r.agb_s.at[t.i, 4], r.agb_r.at[t.i, 4], at_b)

    def gather_turn(name):
        gather_end(name)
        gather_z(name)

    def gather_turned(name):
        t = groups[name]
        for k in (0, 2):
            arrived(t.w_row(z_from[k]), r.agz_s.at[t.i, k], r.agz_r.at[t.i, k], at_z[k])

    def added(target, *landed):
        total = target[...].astype(F32)
        for ref in landed:
            total = total + ref[...].astype(F32)
        return total

    def z_start(t, part, place):
        for k in hops:
            condition = jnp.logical_not(inner) if k == 1 else goes[k]
            start(remote(part(z_of[k]), place(k), r.rsz_s.at[t.i, k], r.rsz_r.at[t.i, k], at_z[k]), condition)
        end_part = part(jnp.where(inner, 0, 3 - zi))
        beside = (jnp.where(zi == 0, 1, 2) * 4 + col, mp)
        extra = t.tx() if t.turned else t.lx()
        start(remote(end_part, extra, r.rsz_s.at[t.i, 3], r.rsz_r.at[t.i, 3], beside), jnp.logical_not(inner))

    def reduce_b(name):
        t = groups[name]
        if t.turned:
            z_start(t, t.p_row, t.tz)
            return
        for k, c in enumerate((col_b, col_d)):
            start(remote(t.p_column(c), t.lb(k), r.rsb_s.at[t.i, k], r.rsb_r.at[t.i, k], at_b))

    def reduce_on(name):
        t = groups[name]
        far = z_of[1]
        extra = t.tx() if t.turned else t.lx()

        @pl.when(inner)
        def _():
            arrived(extra, r.rsz_s.at[t.i, 3], r.rsz_r.at[t.i, 3], at_z[1])
            if t.turned:
                @pl.loop(0, 4)
                def _(c):
                    target = t.p(far, c)
                    target[...] = added(target, t.in_row(extra, c)).astype(LOW)
            else:
                target = t.p(far, col)
                target[...] = added(target, extra).astype(LOW)

        part, place = (t.p_row(far), t.tz(1)) if t.turned else (t.p(far, col), t.lz(1))
        start(remote(part, place, r.rsz_s.at[t.i, 1], r.rsz_r.at[t.i, 1], at_z[1]), inner)

    def z_arrived(t, place):
        for k, condition in ((1, None), (filled, None), (2, inner)):
            arrived(place(k), r.rsz_s.at[t.i, k], r.rsz_r.at[t.i, k], at_z[1], condition)

    def reduce_turn(name):
        t = groups[name]
        z_arrived(t, t.tz)

        @pl.loop(0, 4)
        def _(c):
            target = t.p(zi, c)
            target[...] = added(target, t.in_row(t.tz(1), c), t.in_row(t.tz(filled), c)).astype(LOW)

        @pl.when(inner)
        def _():
            @pl.loop(0, 4)
            def _(c):
                target = t.p(zi, c)
                target[...] = added(target, t.in_row(t.tz(2), c)).astype(LOW)

        for k, c in enumerate((col_b, col_d)):
            start(remote(t.p(zi, c), t.tb(k), r.rsb_s.at[t.i, k], r.rsb_r.at[t.i, k], at_b))

    def reduce_a(name):
        t = groups[name]
        for k, c in ((1, col_a), (0, col)):
            landed = t.tb(k) if t.turned else t.lb(k)
            arrived(landed, r.rsb_s.at[t.i, k], r.rsb_r.at[t.i, k], at_b)
            if t.turned:
                target = t.p(zi, c)
                target[...] = added(target, landed).astype(LOW)
            else:
                def add(target, view):
                    target[...] = added(target, view(landed)).astype(LOW)
                t.each(c, add)
            if k:
                src, dst = (t.p(zi, c), t.ta()) if t.turned else (t.p_column(c), t.la())
                start(remote(src, dst, r.rsa_s.at[t.i], r.rsa_r.at[t.i], at_a))

    def reduce_z(name):
        t = groups[name]
        landed = t.la()
        arrived(landed, r.rsa_s.at[t.i], r.rsa_r.at[t.i], at_a)

        def add(target, view):
            target[...] = added(target, view(landed)).astype(LOW)
        t.each(col, add)
        z_start(t, lambda z: t.p(z, col), t.lz)

    def reduce_end(name):
        t = groups[name]
        total = t.sum()
        if t.turned:
            arrived(t.ta(), r.rsa_s.at[t.i], r.rsa_r.at[t.i], at_a)
            total[...] = added(t.p(zi, col), t.ta())
        else:
            z_arrived(t, t.lz)
            total[...] = added(t.p(zi, col), t.lz(1), t.lz(filled))

            @pl.when(inner)
            def _():
                total[...] = added(total, t.lz(2))
        write(total, t.sum_out())

    def move(*steps):
        if g.comm:
            for step, name in zip(steps[::2], steps[1::2]):
                step(name)

    def w8(j):
        return r.w8[j].reshape(g.d, g.f)

    def wide(which, cols):
        if g.comm:
            return r.wf[which, :, :, :, cols].reshape(g.d, -1)
        return r.wf[which, :, cols]

    def put8(j, value):
        r.p8[j] = value.astype(LOW).reshape(r.p8.shape[1:])

    def put_wide(which, cols, value):
        if g.comm:
            r.pf[which, :, :, :, cols] = value.astype(LOW).reshape(g.nz, 4, g.blk, -1)
        else:
            r.pf[which, :, cols] = value.astype(LOW)

    part = g.t // 2

    def exchange(e, i):
        rows = pl.ds(i * part, part)
        return remote(
            r.stage.at[e % 2, rows], r.land.at[e % 3, rows], r.ex_s.at[e, i], r.ex_r.at[e, i], sibling
        )

    def exchange_start(e, product):
        for i in range(2):
            rows = pl.ds(i * part, part)
            r.stage[e % 2, rows] = product(rows).astype(LOW)
            exchange(e, i).start()

    def by_rows(e, body):
        for i in range(2):
            exchange(e, i).wait_recv()
            exchange(e, i).wait_send()

            @pl.loop(0, part // LN_ROWS)
            def _(n):
                rows = pl.ds(pl.multiple_of(i * part + n * LN_ROWS, LN_ROWS), LN_ROWS)
                body(rows, r.stage[e % 2, rows].astype(F32) + r.land[e % 3, rows].astype(F32))

    def norm(values, i):
        return (centre(values)[0] * r.gains[i]).astype(LOW)

    def norm_back(i, values, grad):
        normed, scale = centre(values)
        r.gain_sum[i] += jnp.sum((grad * normed).reshape(-1, 8, g.d), axis=0)
        scaled = grad * r.gains[i]
        return scale * (
            scaled
            - jnp.mean(scaled, axis=-1, keepdims=True)
            - normed * jnp.mean(scaled * normed, axis=-1, keepdims=True)
        )

    masks = head_masks()
    score_scale = HEAD ** (-0.5)
    pairs = g.f // PAIR

    pl.semaphore_wait(barrier, len(greeted))
    small = []

    def meet(src, dst, device):
        i = len(small)
        copy = remote(src, dst, r.small_s.at[i], r.small_r.at[i], device)
        copy.start()
        small.append(copy)
        return copy

    if g.comm:
        gather_z("q")
        for name in ("q", "k", "v"):
            gather_own(name)
        spot = lax.broadcasted_iota(jnp.int32, (g.blk, g.d), 0) + me * g.blk
        place = jnp.where(spot == lax.broadcasted_iota(jnp.int32, (g.blk, g.d), 1), 1.0, 0.0).astype(LOW)
        total = dot(r.gains_in[...], place, 1, 0)
        r.gain_pass[0, 0:3] = total.astype(LOW)
        for k in hops:
            meet(r.gain_pass.at[0], r.gain_land.at[k], at_z[k])
        for name in ("k", "v"):
            gather_z(name)
        gather_own("co")
        for copy in weights:
            copy.wait()
        gather_own("dn1")
        for k in hops:
            small[k].wait_recv()
            total = total + r.gain_land[k, 0:3].astype(F32)
        r.gain_pass[1, 0:3] = total.astype(LOW)
        hop = meet(r.gain_pass.at[1], r.gain_land.at[g.nz - 1], at_x)
        move(gather_on, "q", gather_z, "ck", gather_a, "q")
        hop.wait_recv()
        total = total + r.gain_land[g.nz - 1, 0:3].astype(F32)
        r.gain_pass[2, 0:3] = total.astype(LOW)
        hop = meet(r.gain_pass.at[2], r.gain_land.at[g.nz], at_y)
        move(gather_on, "k", gather_z, "cv", gather_own, "ck", gather_a, "k")
        hop.wait_recv()
        total = total + r.gain_land[g.nz, 0:3].astype(F32)
    else:
        total = r.gains_in[...].astype(F32)
        for copy in weights:
            copy.wait()
    for i in range(3):
        r.gains[i] = total[i:i + 1]
    r.gain_sum[...] = jnp.zeros_like(r.gain_sum)

    move(
        gather_b, "co", gather_b, "dn1", gather_b, "q", gather_on, "v", gather_z, "so",
        gather_own, "cv", gather_a, "v", gather_on, "ck", gather_z, "cq",
    )
    bring_hidden.wait()

    @pl.loop(0, g.t // LN_ROWS)
    def _(n):
        rows = pl.ds(pl.multiple_of(n * LN_ROWS, LN_ROWS), LN_ROWS)
        r.a1[rows] = norm(r.hidden[rows].astype(F32), 0)

    r.bias[...] = jnp.full(r.bias.shape, NEGATIVE)
    key = lax.broadcasted_iota(jnp.int32, (g.seq, g.seq), 0)
    query = lax.broadcasted_iota(jnp.int32, (g.seq, g.seq), 1)
    for row in range(g.rows):
        across = r.seg[row // g.row_mb, row % g.row_mb:row % g.row_mb + 1, :].astype(F32)
        down = jnp.sum(jnp.where(key == query, across, 0.0), axis=1, keepdims=True)
        p, at = row * g.seq // PAIR, row * g.seq % PAIR
        r.bias[p, at:at + g.seq, at:at + g.seq] = jnp.where((key <= query) & (down == across), 0.0, NEGATIVE)

    def project(j):
        r.qkv[j] = dot(r.a1[...], w8(QKV + j), 1, 0).astype(LOW)

    move(gather_b, "k", gather_a, "ck", gather_own, "so", gather_on, "cv", gather_z, "up0", gather_end, "q")
    project(0)
    move(gather_b, "v", gather_a, "cv", gather_own, "cq", gather_on, "so", gather_z, "up1", gather_end, "k")
    project(1)
    move(gather_b, "ck", gather_a, "so", gather_on, "cq", gather_turn, "co", gather_end, "v")
    project(2)

    def self_attend(first, last):
        @pl.loop(first, last)
        def _(p):
            rows = pl.ds(pl.multiple_of(p * PAIR, PAIR), PAIR)
            bias = jnp.concatenate([r.bias[p]] * 2, axis=1)
            for h in range(pairs):
                lanes = lanes_of(h)
                queries = stack_heads(r.qkv[0, rows, lanes], masks)
                scores = dot(r.qkv[1, rows, lanes], queries, 1, 1) * score_scale + bias
                weights_low = softmax_keys(scores).astype(LOW)
                r.self_p[p, h] = weights_low
                r.mixed[rows, lanes] = join_heads(dot(weights_low, r.qkv[2, rows, lanes], 0, 0)).astype(LOW)

    def project_images(m):
        for image in range(g.images):
            rows = pl.ds(image * g.ctx, g.ctx)
            r.kv[m, image] = dot(r.enc[rows], w8(CKV + m), 1, 0).astype(LOW)

    self_attend(0, g.t // PAIR)
    bring_enc.wait()
    move(
        gather_b, "cv", gather_a, "cq", gather_own, "up0", gather_on, "up0", gather_z, "dn0",
        gather_end, "ck",
    )
    project_images(0)
    move(gather_b, "so", gather_a, "up0", gather_own, "up1", gather_on, "up1", gather_end, "cv")
    project_images(1)
    move(gather_b, "cq", gather_on, "co", gather_on, "dn0", gather_turn, "dn1", gather_end, "so")
    exchange_start(0, lambda rows: dot(r.mixed[rows], w8(SO), 1, 1))

    def after_self(rows, total):
        resid = r.hidden[rows].astype(F32) + total
        r.resid_one[rows] = resid
        r.a2[rows] = norm(resid, 1)

    by_rows(0, after_self)
    move(gather_a, "up1", gather_end, "cq")
    r.cq[...] = dot(r.a2[...], w8(CQ), 1, 0).astype(LOW)

    def cross_attend(first, last):
        @pl.loop(first, last)
        def _(row):
            rows = pl.ds(pl.multiple_of(row * g.seq, g.seq), g.seq)
            image = (row // g.row_mb) * g.img_mb + r.image_ids[row // g.row_mb, row % g.row_mb]
            for h in range(pairs):
                lanes = lanes_of(h)
                queries = stack_heads(r.cq[rows, lanes], masks)
                scores = dot(r.kv[0, image, :, lanes], queries, 1, 1) * score_scale
                weights_low = softmax_keys(scores).astype(LOW)
                r.cross_p[row * pairs + h] = weights_low
                r.cmixed[rows, lanes] = join_heads(dot(weights_low, r.kv[1, image, :, lanes], 0, 0)).astype(LOW)

    cross_attend(0, g.rows // 2)
    move(gather_b, "up0", gather_own, "dn0", gather_a, "dn0", gather_turned, "co")
    cross_attend(g.rows // 2, g.rows)
    exchange_start(1, lambda rows: dot(r.cmixed[rows], w8(CO), 1, 1))
    move(gather_b, "up1")

    def after_cross(rows, total):
        resid = r.resid_one[rows] + total
        r.resid_two[rows] = resid
        r.a3[rows] = norm(resid, 2)

    by_rows(1, after_cross)
    bring_cot.wait()

    def up_half(first):
        @pl.loop(0, half // TILE)
        def _(n):
            cols = pl.ds(pl.multiple_of(first + n * TILE, TILE), TILE)
            pre = dot(r.a3[...], wide(UP, cols), 1, 0)
            below = 0.5 * (1.0 + lax.erf(pre * ROOT_HALF))
            r.act[:, cols] = (pre * below).astype(LOW)
            slope = below + pre * (DENSITY * jnp.exp(-0.5 * (pre * pre)))
            r.slope[:, cols] = slope.astype(r.slope.dtype)

    def grad_wide(which, left, right, first):
        cols = pl.ds(first, half)
        put_wide(which, cols, dot(left[...], right[:, cols], 0, 0))

    def down_half(first):
        @pl.loop(0, half // TILE)
        def _(n):
            cols = pl.ds(pl.multiple_of(first + n * TILE, TILE), TILE)
            grad_act = dot(r.cot[...], wide(DOWN, cols), 1, 0)
            r.slope[:, cols] = (grad_act * r.slope[:, cols].astype(F32)).astype(LOW)

    move(gather_end, "up0")
    up_half(0)
    move(gather_b, "dn0", gather_on, "dn1", gather_end, "up1")
    up_half(half)
    grad_wide(DOWN, r.cot, r.act, half)
    move(reduce_b, "dn1")
    grad_wide(DOWN, r.cot, r.act, 0)
    move(reduce_b, "dn0")

    everything = pl.ds(0, g.ff)
    move(gather_end, "dn0")
    down_half(0)
    grad_wide(UP, r.a3, r.slope, 0)
    move(reduce_b, "up0", gather_turned, "dn1")
    down_half(half)
    exchange_start(2, lambda rows: dot(r.slope[rows], wide(UP, everything), 1, 1))
    grad_wide(UP, r.a3, r.slope, half)
    move(reduce_b, "up1")

    def after_up(rows, total):
        grad = r.cot[rows].astype(F32) + norm_back(2, r.resid_two[rows], total)
        r.grad[rows] = grad
        r.grad_low[rows] = grad.astype(LOW)

    by_rows(2, after_up)
    put8(CO, dot(r.grad_low[...], r.cmixed[...], 0, 0))
    move(reduce_b, "co")
    r.g_mixed[...] = dot(r.grad_low[...], w8(CO), 1, 0).astype(LOW)
    exchange_start(3, lambda rows: dot(r.act[rows], wide(DOWN, everything), 1, 1))
    move(reduce_on, "dn1", reduce_a, "dn0")

    def after_down(rows, total):
        r.a3[rows] = (r.resid_two[rows] + total).astype(LOW)

    by_rows(3, after_down)
    write(r.a3, r.out)

    def cross_back(first, last):
        @pl.loop(first, last)
        def _(m):
            for h in range(pairs):
                lanes = lanes_of(h)
                queries, grads, soft = [], [], []
                for n in range(g.row_mb):
                    row = m * g.row_mb + n
                    rows = pl.ds(pl.multiple_of(row * g.seq, g.seq), g.seq)
                    image = m * g.img_mb + r.image_ids[m, n]
                    grads.append(stack_heads(r.g_mixed[rows, lanes], masks))
                    queries.append(stack_heads(r.cq[rows, lanes], masks))
                    weights_low = r.cross_p[row * pairs + h]
                    soft.append(weights_low)
                    prob = weights_low.astype(F32)
                    grad_p = dot(r.kv[1, image, :, lanes], grads[-1], 1, 1)
                    inner = jnp.sum(prob * grad_p, axis=0, keepdims=True)
                    grad_s = (prob * (grad_p - inner)).astype(LOW)
                    r.cross_ds[:, lanes_of(n)] = grad_s
                    grad_q = join_heads(dot(grad_s, r.kv[0, image, :, lanes], 0, 0)) * score_scale
                    r.cq[rows, lanes] = grad_q.astype(LOW)
                soft = jnp.concatenate(soft, axis=1)
                for i in range(g.img_mb):
                    chosen = [
                        jnp.where(r.image_ids[m, n] == i, jnp.ones((1, PAIR), F32), 0.0).astype(LOW)
                        for n in range(g.row_mb)
                    ]
                    picked = jnp.concatenate([q * c for q, c in zip(queries, chosen)], axis=0)
                    r.kv[0, m * g.img_mb + i, :, lanes] = (dot(r.cross_ds[...], picked, 1, 0) * score_scale).astype(LOW)
                    picked = jnp.concatenate([v * c for v, c in zip(grads, chosen)], axis=0)
                    r.kv[1, m * g.img_mb + i, :, lanes] = dot(soft, picked, 1, 0).astype(LOW)

    cross_back(0, g.micro // 2)
    move(reduce_z, "dn0", reduce_a, "up0", reduce_on, "co", reduce_turn, "dn1")
    cross_back(g.micro // 2, g.micro)
    exchange_start(4, lambda rows: dot(r.cq[rows], w8(CQ), 1, 1))
    move(reduce_on, "dn0", reduce_z, "up0", reduce_a, "up1")
    for j, name in enumerate(("ck", "cv")):
        put8(CKV + j, dot(r.enc[...], r.kv[j].reshape(g.images * g.ctx, g.f), 0, 0))
        move(reduce_b, name)
    put8(CQ, dot(r.a2[...], r.cq[...], 0, 0))
    move(reduce_b, "cq", reduce_turn, "co", reduce_on, "up0", reduce_z, "up1", reduce_a, "dn1")

    def after_query(rows, total):
        grad = r.grad[rows] + norm_back(1, r.resid_one[rows], total)
        r.grad[rows] = grad
        r.grad_low[rows] = grad.astype(LOW)

    by_rows(4, after_query)
    put8(SO, dot(r.grad_low[...], r.mixed[...], 0, 0))
    move(reduce_b, "so")
    r.g_mixed[...] = dot(r.grad_low[...], w8(SO), 1, 0).astype(LOW)
    move(reduce_end, "dn0", reduce_end, "up0", reduce_end, "dn1", reduce_on, "up1")

    @pl.loop(0, g.t // PAIR)
    def _(p):
        rows = pl.ds(pl.multiple_of(p * PAIR, PAIR), PAIR)
        for h in range(pairs):
            lanes = lanes_of(h)
            queries = stack_heads(r.qkv[0, rows, lanes], masks)
            grads = stack_heads(r.g_mixed[rows, lanes], masks)
            weights_low = r.self_p[p, h]
            prob = weights_low.astype(F32)
            grad_p = dot(r.qkv[2, rows, lanes], grads, 1, 1)
            inner = jnp.sum(prob * grad_p, axis=0, keepdims=True)
            grad_s = (prob * (grad_p - inner)).astype(LOW)
            grad_q = join_heads(dot(grad_s, r.qkv[1, rows, lanes], 0, 0)) * score_scale
            grad_k = dot(grad_s, queries, 1, 0) * score_scale
            grad_v = dot(weights_low, grads, 1, 0)
            r.qkv[0, rows, lanes] = grad_q.astype(LOW)
            r.qkv[1, rows, lanes] = grad_k.astype(LOW)
            r.qkv[2, rows, lanes] = grad_v.astype(LOW)

    exchange_start(
        5,
        lambda rows: dot(r.qkv[0, rows], w8(QKV), 1, 1)
        + dot(r.qkv[1, rows], w8(QKV + 1), 1, 1)
        + dot(r.qkv[2, rows], w8(QKV + 2), 1, 1),
    )
    for j, name in enumerate(("q", "k", "v")):
        put8(QKV + j, dot(r.a1[...], r.qkv[j], 0, 0))
        if name == "v":
            def after_qkv(rows, total):
                grad = r.grad[rows] + norm_back(0, r.hidden[rows].astype(F32), total)
                r.grad[rows] = grad

            by_rows(5, after_qkv)
            for i in range(3):
                r.gain_total[0, i:i + 1] = jnp.sum(r.gain_sum[i], axis=0, keepdims=True)
            if g.comm:
                hop = meet(r.gain_total.at[0], r.total_land.at[0], at_x)
        move(reduce_b, name)
    write(r.grad, r.in_grad)
    move(reduce_a, "ck", reduce_a, "cv", reduce_a, "co", reduce_end, "up1", reduce_z, "ck")

    def features(j, h):
        if g.comm:
            return r.w8[j, pl.ds(h * (g.nz // 2), g.nz // 2)].reshape(g.d // 2, g.f)
        return r.w8[j, pl.ds(pl.multiple_of(h * (g.d // 2), g.d // 2), g.d // 2)]

    def encoder_part(image, h):
        return dot(r.kv[0, image], features(CKV, h), 1, 1) + dot(r.kv[1, image], features(CKV + 1, h), 1, 1)

    strips = g.d // 2 // PAIR

    def encoder_keep(image, value):
        for h in range(strips):
            r.cross_p[image * strips + h] = value[:, h * PAIR:(h + 1) * PAIR].astype(LOW)

    def encoder_copy(image):
        part = pl.ds(image * strips, strips)
        return remote(r.cross_p.at[part], r.enc_land.at[part], r.enc_s.at[image], r.enc_r.at[image], sibling)

    for image in range(g.images):
        encoder_keep(image, encoder_part(image, 1 - mp))
        encoder_copy(image).start()

    move(reduce_z, "cv", reduce_on, "ck", reduce_a, "cq", reduce_a, "so", reduce_end, "co")
    if g.comm:
        hop.wait_recv()
        r.gain_total[1] = r.gain_total[0] + r.total_land[0]
        hop = meet(r.gain_total.at[1], r.total_land.at[1], at_y)
    for image in range(g.images):
        encoder_copy(image).wait_recv()
        encoder_copy(image).wait_send()
        landed = jnp.concatenate([r.enc_land[image * strips + h] for h in range(strips)], axis=1)
        encoder_keep(image, encoder_part(image, mp) + landed.astype(F32))
        rows = pl.ds(image * g.ctx, g.ctx)
        for h in range(strips):
            write(r.cross_p.at[image * strips + h], r.enc_grad.at[rows, lanes_of(h)])
    move(
        reduce_z, "cq", reduce_z, "so", reduce_a, "q", reduce_on, "cv", reduce_end, "ck",
        reduce_on, "cq", reduce_a, "k", reduce_z, "q", reduce_end, "cv", reduce_on, "so",
    )
    if g.comm:
        hop.wait_recv()
        r.gain_total[2] = r.gain_total[1] + r.total_land[1]
        for k in range(g.nz - 1):
            meet(r.gain_total.at[2], r.total_land.at[2 + k], at_z[k])
    move(
        reduce_end, "cq", reduce_a, "v", reduce_z, "k", reduce_on, "q", reduce_end, "so", reduce_z, "v",
        reduce_on, "k", reduce_end, "q", reduce_on, "v", reduce_end, "k", reduce_end, "v",
    )
    if g.comm:
        total = r.gain_total[2]
        for k in hops:
            small[k - g.nz + 1].wait_recv()
            total = total + r.total_land[2 + k]
        spot = lax.broadcasted_iota(jnp.int32, (g.d, g.blk), 1) + me * g.blk
        place = jnp.where(spot == lax.broadcasted_iota(jnp.int32, (g.d, g.blk), 0), 1.0, 0.0)
        mine = lax.dot_general(
            total, place, (((1,), (0,)), ((), ())), precision=lax.Precision.HIGHEST, preferred_element_type=F32
        )
        r.gain_out[...] = mine[0:3]
    else:
        r.gain_out[...] = r.gain_total[0, 0:3]
    for copy in written:
        copy.wait()
    for copy in small:
        copy.wait_send()
    for copy, condition in started:
        only(condition, copy.wait_send)


def run_layer(g, operands):
    vmem = pl.BlockSpec(memory_space=pltpu.VMEM)
    smem = pl.BlockSpec(memory_space=pltpu.SMEM)
    anywhere = pl.BlockSpec(memory_space=pl.ANY)
    shape = jax.ShapeDtypeStruct
    ins = dict(
        image_ids=smem, seg=vmem, hidden_in=anywhere, gains_in=vmem, cot_in=anywhere, enc_in=anywhere,
        qkv_in=anywhere, so_in=anywhere, cq_in=anywhere, ckv_in=anywhere, co_in=anywhere,
        up_in=anywhere, down_in=anywhere,
    )
    outs = dict(
        out=(shape((g.t, g.d), LOW), anywhere),
        in_grad=(shape((g.t, g.d), F32), anywhere),
        enc_grad=(shape((g.images * g.ctx, g.d // 2), LOW), anywhere),
        gain_out=(shape((3, g.blk if g.comm else g.d), F32), vmem),
    )
    grid = (g.nz, 4, g.blk) if g.comm else (g.d,)
    dma = pltpu.SemaphoreType.DMA
    scratch = dict(
        w8=pltpu.VMEM((MATS, *grid, g.f), LOW),
        wf=pltpu.VMEM((2, *grid, g.ff), LOW),
        hidden=pltpu.VMEM((g.t, g.d), LOW),
        enc=pltpu.VMEM((g.images * g.ctx, g.d), LOW),
        cot=pltpu.VMEM((g.t, g.d), LOW),
        gains=pltpu.VMEM((3, 1, g.d), F32),
        gain_sum=pltpu.VMEM((3, 8, g.d), F32),
        gain_total=pltpu.VMEM((3, 8, g.d), F32),
        bias=pltpu.VMEM((g.t // PAIR, PAIR, PAIR), F32),
        a1=pltpu.VMEM((g.t, g.d), LOW),
        a2=pltpu.VMEM((g.t, g.d), LOW),
        a3=pltpu.VMEM((g.t, g.d), LOW),
        qkv=pltpu.VMEM((3, g.t, g.f), LOW),
        mixed=pltpu.VMEM((g.t, g.f), LOW),
        cq=pltpu.VMEM((g.t, g.f), LOW),
        cmixed=pltpu.VMEM((g.t, g.f), LOW),
        g_mixed=pltpu.VMEM((g.t, g.f), LOW),
        kv=pltpu.VMEM((2, g.images, g.ctx, g.f), LOW),
        self_p=pltpu.VMEM((g.t // PAIR, g.f // PAIR, PAIR, 2 * PAIR), LOW),
        cross_p=pltpu.VMEM((g.rows * (g.f // PAIR), g.ctx, PAIR), LOW),
        cross_ds=pltpu.VMEM((g.ctx, g.row_mb * PAIR), LOW),
        resid_one=pltpu.VMEM((g.t, g.d), F32),
        resid_two=pltpu.VMEM((g.t, g.d), F32),
        grad=pltpu.VMEM((g.t, g.d), F32),
        grad_low=pltpu.VMEM((g.t, g.d), LOW),
        act=pltpu.VMEM((g.t, g.ff), LOW),
        slope=pltpu.VMEM((g.t, g.ff), LOW),
        stage=pltpu.VMEM((2, g.t, g.d), LOW),
        land=pltpu.VMEM((3, g.t, g.d), LOW),
        enc_land=pltpu.VMEM((g.images * (g.d // 2 // PAIR), g.ctx, PAIR), LOW),
        local_sem=dma((10,)),
        ex_s=dma((6, 2)), ex_r=dma((6, 2)),
        enc_s=dma((g.images,)), enc_r=dma((g.images,)),
        write_sem=dma((16 + g.images * (g.d // 2 // PAIR),)),
    )
    if g.comm:
        outs.update(
            g8_out=(shape((MATS, g.blk, g.f), F32), anywhere),
            gf_out=(shape((2, g.blk, g.ff), F32), anywhere),
        )
        hops = g.nz - 1
        scratch.update(
            g8=pltpu.VMEM((MATS, g.blk, g.f), F32),
            gf=pltpu.VMEM((2, g.blk, g.ff), F32),
            p8=pltpu.VMEM((MATS, *grid, g.f), LOW),
            pf=pltpu.VMEM((2, *grid, g.ff), LOW),
            lb8=pltpu.VMEM((2, MATS, g.nz, g.blk, g.f), LOW),
            lbf=pltpu.VMEM((2, 3, g.nz, g.blk, g.ff // 2), LOW),
            la8=pltpu.VMEM((MATS, g.nz, g.blk, g.f), LOW),
            laf=pltpu.VMEM((3, g.nz, g.blk, g.ff // 2), LOW),
            lz8=pltpu.VMEM((hops, MATS, g.blk, g.f), LOW),
            lzf=pltpu.VMEM((hops, 3, g.blk, g.ff // 2), LOW),
            lx8=pltpu.VMEM((MATS, g.blk, g.f), LOW),
            lxf=pltpu.VMEM((3, g.blk, g.ff // 2), LOW),
            turnf_z=pltpu.VMEM((hops, 4, g.blk, g.ff // 2), LOW),
            turnf_x=pltpu.VMEM((4, g.blk, g.ff // 2), LOW),
            turnf_b=pltpu.VMEM((2, g.blk, g.ff // 2), LOW),
            turnf_a=pltpu.VMEM((g.blk, g.ff // 2), LOW),
            turn8_z=pltpu.VMEM((hops, 1, 4, g.blk, g.f), LOW),
            turn8_x=pltpu.VMEM((1, 4, g.blk, g.f), LOW),
            turn8_b=pltpu.VMEM((2, 1, g.blk, g.f), LOW),
            turn8_a=pltpu.VMEM((1, g.blk, g.f), LOW),
            gain_land=pltpu.VMEM((hops + 2, 16, g.d), LOW),
            gain_pass=pltpu.VMEM((3, 16, g.d), LOW),
            total_land=pltpu.VMEM((hops + 2, 8, g.d), F32),
            agz_s=dma((12, 4)), agz_r=dma((12, 4)),
            aga_s=dma((12, g.nz)), aga_r=dma((12, g.nz)),
            agb_s=dma((12, g.nz + 1)), agb_r=dma((12, g.nz + 1)),
            rsz_s=dma((12, 4)), rsz_r=dma((12, 4)),
            rsa_s=dma((12,)), rsa_r=dma((12,)),
            rsb_s=dma((12, 2)), rsb_r=dma((12, 2)),
            small_s=dma((2 * hops + 4,)), small_r=dma((2 * hops + 4,)),
        )
    else:
        outs.update(
            p8=(shape((MATS, g.d, g.f), LOW), vmem),
            pf=(shape((2, g.d, g.ff), LOW), vmem),
        )
    g.names = (*ins, *outs, *scratch)
    return dict(zip(outs, pl.pallas_call(
        functools.partial(layer, g),
        out_shape=[o[0] for o in outs.values()],
        in_specs=list(ins.values()),
        out_specs=[o[1] for o in outs.values()],
        scratch_shapes=list(scratch.values()),
        compiler_params=pltpu.CompilerParams(
            collective_id=0, has_side_effects=True, vmem_limit_bytes=63 * 2**20
        ),
        name="layer",
    )(*operands)))


def pass_on(g, out, in_grad, enc, gain, g8, gf, *refs):
    outs, (v_out, v_in, v_gain, v_g8, v_gf, low, full, in_sem, out_sem) = refs[:11], refs[11:]
    coming, leaving = [], []

    def bring(src, dst):
        coming.append(pltpu.make_async_copy(src, dst, in_sem.at[len(coming)]))
        coming[-1].start()

    def leave(src, dst):
        leaving.append(pltpu.make_async_copy(src, dst, out_sem.at[len(leaving)]))
        leaving[-1].start()

    halves = [pl.ds(i * g.t // 2, g.t // 2) for i in range(2)]
    images = [pl.ds(i * g.ctx, g.ctx) for i in range(g.images)]
    for rows in images:
        bring(enc.at[rows], low.at[rows])
    for rows in halves:
        bring(in_grad.at[rows], v_in.at[rows])
    bring(out, v_out)
    bring(g8, v_g8)
    bring(gf, v_gf)
    bring(gain, v_gain)
    for i, rows in enumerate(images):
        coming[i].wait()
        full[rows] = low[rows].astype(F32)
        leave(full.at[rows], outs[2].at[rows])
    for copy, rows in zip(coming[g.images:], halves):
        copy.wait()
        leave(v_in.at[rows], outs[1].at[rows])
    for copy in coming[g.images + 2:]:
        copy.wait()
    leave(v_out, outs[0])
    leave(v_gain, outs[3])
    for src, dst in zip(
        (v_g8.at[pl.ds(QKV, 3)], v_g8.at[SO], v_g8.at[CQ], v_g8.at[pl.ds(CKV, 2)], v_g8.at[CO], v_gf.at[UP], v_gf.at[DOWN]),
        outs[4:],
    ):
        leave(src, dst)
    for copy in leaving:
        copy.wait()


def hand_over(g, o):
    shape = jax.ShapeDtypeStruct
    tokens, enc = (g.t, g.d), (g.images * g.ctx, g.d // 2)
    one, wide = (g.blk, g.f), (g.blk, g.ff)
    shapes = (tokens, tokens, enc, (3, g.blk), (3, *one), one, one, (2, *one), one, wide, wide)
    anywhere = pl.BlockSpec(memory_space=pl.ANY)
    dma = pltpu.SemaphoreType.DMA
    return pl.pallas_call(
        functools.partial(pass_on, g),
        out_shape=[shape(s, LOW if i == 0 else F32) for i, s in enumerate(shapes)],
        in_specs=[anywhere] * 6,
        out_specs=[anywhere] * 11,
        scratch_shapes=[
            pltpu.VMEM(tokens, LOW), pltpu.VMEM(tokens, F32), pltpu.VMEM((3, g.blk), F32),
            pltpu.VMEM((MATS, *one), F32), pltpu.VMEM((2, *wide), F32),
            pltpu.VMEM(enc, LOW), pltpu.VMEM(enc, F32), dma((g.images + 6,)), dma((g.images + 11,)),
        ],
        compiler_params=pltpu.CompilerParams(vmem_limit_bytes=63 * 2**20),
        name="hand_over",
    )(o["out"], o["in_grad"], o["enc_grad"], o["gain_out"], o["g8_out"], o["gf_out"])


def body(
    dp, mp, hidden, encoder_tokens, segment_ids, image_index, cotangent, norm_gains, qkv_weight,
    self_out_weight, cross_query_weight, cross_kv_weight, cross_out_weight, up_weight, down_weight,
):
    micro, row_mb, seq, d = hidden.shape
    img_mb, ctx = encoder_tokens.shape[1:3]
    blk, f = self_out_weight.shape
    g = SimpleNamespace(
        micro=micro, row_mb=row_mb, seq=seq, d=d, img_mb=img_mb, ctx=ctx, blk=blk, f=f,
        ff=up_weight.shape[1], rows=micro * row_mb, t=micro * row_mb * seq, images=micro * img_mb,
        nz=dp // 4, comm=dp == 16 and blk % 16 == 0,
    )
    weights = [
        qkv_weight, self_out_weight, cross_query_weight, cross_kv_weight, cross_out_weight, up_weight, down_weight,
    ]
    gains = norm_gains
    if not g.comm:
        gains = lax.all_gather(norm_gains, "dp", axis=1, tiled=True)
        weights = [lax.all_gather(w, "dp", axis=w.ndim - 2, tiled=True) for w in weights]
    for i in (1, 2, 4):
        weights[i] = weights[i][None]
    o = run_layer(g, (
        image_index, segment_ids, hidden.reshape(g.t, d), gains, cotangent.reshape(g.t, d),
        encoder_tokens.reshape(g.images * ctx, d), *weights,
    ))
    if g.comm:
        whole = hand_over(g, o)
    else:
        small = lax.psum_scatter(o["p8"].astype(F32), "dp", scatter_dimension=1, tiled=True)
        wide = lax.psum_scatter(o["pf"].astype(F32), "dp", scatter_dimension=1, tiled=True)
        whole = (
            o["out"], o["in_grad"], o["enc_grad"].astype(F32),
            lax.psum_scatter(o["gain_out"], "dp", scatter_dimension=1, tiled=True),
            small[QKV:QKV + 3], small[SO], small[CQ], small[CKV:CKV + 2], small[CO], wide[UP], wide[DOWN],
        )
    return (
        whole[0].reshape(hidden.shape), whole[1].reshape(hidden.shape),
        whole[2].reshape(micro, img_mb, ctx, d // 2), *whole[3:],
    )


def solution(mesh):
    tokens, kept = P(None, "dp", None, None), P("dp", "mp")
    three = P(None, "dp", "mp")
    return jax.shard_map(
        functools.partial(body, mesh.shape["dp"], mesh.shape["mp"]),
        mesh=mesh,
        in_specs=(
            tokens, tokens, P(None, "dp", None), P(None, "dp"), tokens, P(None, "dp"),
            three, kept, kept, three, kept, kept, kept,
        ),
        out_specs=(
            tokens, tokens, P(None, "dp", None, "mp"), P(None, "dp"),
            three, kept, kept, three, kept, kept, kept,
        ),
        check_vma=False,
    )
```

```python
import functools
from types import SimpleNamespace

import jax
import jax.numpy as jnp
from jax import lax
from jax.experimental import pallas as pl
from jax.experimental.pallas import tpu as pltpu
from jax.sharding import PartitionSpec as P

HEAD = 64
PAIR = 2 * HEAD
EPSILON = 1e-05
NEGATIVE = -1e30
ROOT_HALF = 0.7071067811865476
DENSITY = 0.3989422804014327
MESH = pl.DeviceIdType.MESH
LOW = jnp.bfloat16
F32 = jnp.float32
QKV, SO, CQ, CKV, CO, MATS = 0, 3, 4, 5, 7, 8
DIRECT = ("q", "k", "v")
UP, DOWN = 0, 1
LN_ROWS = 128
TILE = 256


def dot(left, right, left_dim, right_dim):
    return lax.dot_general(
        left, right, (((left_dim,), (right_dim,)), ((), ())), preferred_element_type=F32
    )


def lanes_of(pair):
    return pl.ds(pair * PAIR, PAIR)


def head_masks():
    lane = lax.broadcasted_iota(jnp.int32, (1, PAIR), 1)
    first = jnp.where(lane < HEAD, 1.0, 0.0)
    return first.astype(LOW), (1.0 - first).astype(LOW)


def stack_heads(values, masks):
    return jnp.concatenate([values * masks[0], values * masks[1]], axis=0)


def join_heads(stacked):
    half = stacked.shape[0] // 2
    lane = lax.broadcasted_iota(jnp.int32, (half, PAIR), 1)
    return jnp.where(lane < HEAD, stacked[:half], stacked[half:])


def centre(values):
    centred = values - jnp.mean(values, axis=-1, keepdims=True)
    spread = jnp.mean(centred * centred, axis=-1, keepdims=True)
    scale = lax.rsqrt(spread + EPSILON)
    return centred * scale, scale


def softmax_keys(scores):
    shifted = jnp.exp(scores - jnp.max(scores, axis=0, keepdims=True))
    return shifted / jnp.sum(shifted, axis=0, keepdims=True)


def layer(g, *refs):
    r = SimpleNamespace(**dict(zip(g.names, refs)))
    me, mp = lax.axis_index("dp"), lax.axis_index("mp")
    zi, col = me // 4, me % 4
    sibling = (me, 1 - mp)
    col_x = col + 1 - 2 * (col % 2)
    col_y = (col + 2) % 4
    col_d = (col_x + 2) % 4
    col_a = mp * col_x + (1 - mp) * col_y
    col_b = mp * col_y + (1 - mp) * col_x
    at_x, at_y = (zi * 4 + col_x, mp), (zi * 4 + col_y, mp)
    at_a, at_b = (zi * 4 + col_a, mp), (zi * 4 + col_b, mp)
    z_of = [(zi + k) % g.nz for k in range(1, g.nz)]
    z_from = [(zi + g.nz - k) % g.nz for k in range(1, g.nz)]
    at_z = [(z * 4 + col, mp) for z in z_of]

    greeted = [sibling] + ([at_x, at_y] + at_z if g.comm else [])
    barrier = pltpu.get_barrier_semaphore()
    for device in greeted:
        pl.semaphore_signal(barrier, inc=1, device_id=device, device_id_type=MESH)

    def remote(src, dst, send, recv, device):
        return pltpu.make_async_remote_copy(
            src_ref=src, dst_ref=dst, send_sem=send, recv_sem=recv, device_id=device, device_id_type=MESH
        )

    local = []

    def bring(src, dst):
        copy = pltpu.make_async_copy(src, dst, r.local_sem.at[len(local)])
        copy.start()
        local.append(copy)
        return copy

    def slot(first, count):
        ref = r.w8.at[pl.ds(first, count)]
        return ref.at[:, zi, col] if g.comm else ref

    def wide_slot(which):
        return r.wf.at[which, zi, col] if g.comm else r.wf.at[which]

    weights = [
        bring(r.qkv_in, slot(QKV, 3)),
        bring(r.so_in, slot(SO, 1)),
        bring(r.cq_in, slot(CQ, 1)),
        bring(r.ckv_in, slot(CKV, 2)),
        bring(r.co_in, slot(CO, 1)),
        bring(r.up_in, wide_slot(UP)),
        bring(r.down_in, wide_slot(DOWN)),
    ]
    bring_hidden = bring(r.hidden_in, r.hidden)
    bring_enc = bring(r.enc_in, r.enc)
    bring_cot = bring(r.cot_in, r.cot)

    half = g.ff // 2

    def mats(first, ref, at):
        part = pl.ds(first, 1)

        def each(c, body):
            @pl.loop(0, g.nz)
            def _(z):
                body(r.p8.at[first, z, c], lambda landed: landed.at[0, z])

        return SimpleNamespace(
            src=lambda: ref.at[pl.ds(at, 1)],
            w=lambda z, c: r.w8.at[part, z, c], w_column=lambda c: r.w8.at[part, :, c],
            w_row=lambda z: r.w8.at[part, z], p_row=lambda z: r.p8.at[part, z],
            p=lambda z, c: r.p8.at[part, z, c], p_column=lambda c: r.p8.at[part, :, c],
            lb=lambda k: r.lb8.at[k, part], la=lambda: r.la8.at[part], lz=lambda k: r.lz8.at[k, part],
            lx=lambda: r.lx8.at[part], in_row=lambda row, c: row.at[:, c],
            tz=lambda k: r.turn8_z.at[k], tb=lambda k: r.turn8_b.at[k], ta=lambda: r.turn8_a,
            tx=lambda: r.turn8_x, each=each, sum=lambda: r.g8.at[part], sum_out=lambda: r.g8_out.at[part],
        )

    def strip(which, first, i, ref):
        cols = pl.ds(first, half)

        def each(c, body):
            @pl.loop(0, g.nz)
            def _(z):
                body(r.pf.at[which, z, c, :, cols], lambda landed: landed.at[z])

        return SimpleNamespace(
            src=lambda: ref.at[:, cols],
            w=lambda z, c: r.wf.at[which, z, c, :, cols], w_column=lambda c: r.wf.at[which, :, c, :, cols],
            w_row=lambda z: r.wf.at[which, z, :, :, cols], p_row=lambda z: r.pf.at[which, z, :, :, cols],
            p=lambda z, c: r.pf.at[which, z, c, :, cols], p_column=lambda c: r.pf.at[which, :, c, :, cols],
            lb=lambda k: r.lbf.at[k, i], la=lambda: r.laf.at[i], lz=lambda k: r.lzf.at[k, i],
            lx=lambda: r.lxf.at[i], in_row=lambda row, c: row.at[c],
            tz=lambda k: r.turnf_z.at[k], tb=lambda k: r.turnf_b.at[k], ta=lambda: r.turnf_a,
            tx=lambda: r.turnf_x, each=each, sum=lambda: r.gf.at[which, :, cols],
            sum_out=lambda: r.gf_out.at[which, :, cols],
        )

    groups = dict(
        q=mats(QKV, r.qkv_in, 0), k=mats(QKV + 1, r.qkv_in, 1), v=mats(QKV + 2, r.qkv_in, 2),
        ck=mats(CKV, r.ckv_in, 0), cv=mats(CKV + 1, r.ckv_in, 1),
        so=mats(SO, r.so_in, 0), cq=mats(CQ, r.cq_in, 0), co=mats(CO, r.co_in, 0),
        up0=strip(UP, 0, 0, r.up_in), up1=strip(UP, half, 1, r.up_in),
        dn0=strip(DOWN, 0, 2, r.down_in), dn1=strip(DOWN, half, 3, r.down_in),
    )
    for i, (name, group) in enumerate(groups.items()):
        group.i, group.turned, group.direct = i, name in ("co", "dn1"), name in DIRECT

    inner = (zi == 1) | (zi == 2)
    goes = (zi != 3, None, zi != 0)
    hops = range(3)
    other = 3 * (2 - zi)
    onward = 3 * (zi - 1)
    filled = 2 * jnp.where(zi == 0, 1, 0)

    written = []

    def write(src, dst):
        copy = pltpu.make_async_copy(src, dst, r.write_sem.at[len(written)])
        copy.start()
        written.append(copy)

    started = []

    def only(condition, act):
        if condition is None:
            act()
        else:
            pl.when(condition)(act)

    def start(copy, condition=None):
        only(condition, copy.start)
        started.append((copy, condition))

    def arrived(ref, send, recv, device, condition=None):
        only(condition, remote(ref, ref, send, recv, device).wait_recv)

    def gather_z(name):
        t = groups[name]
        for k in hops:
            src, dst = (t.w_row(zi), t.w_row(zi)) if t.turned else (t.src(), t.w(zi, col))
            start(remote(src, dst, r.agz_s.at[t.i, k], r.agz_r.at[t.i, k], at_z[k]), None if t.direct else goes[k])

    def z_part(t, z):
        return t.w_row(z) if t.turned else t.w(z, col)

    def gather_on(name):
        t = groups[name]
        arrived(z_part(t, z_from[1]), r.agz_s.at[t.i, 1], r.agz_r.at[t.i, 1], at_z[1])
        if t.direct:
            return
        part = z_part(t, jnp.where(inner, other, 0))
        start(
            remote(part, part, r.agz_s.at[t.i, 3], r.agz_r.at[t.i, 2 * jnp.where(zi == 2, 1, 0)],
                   (jnp.where(inner, onward, 0) * 4 + col, mp)),
            inner,
        )

    def to_both(t, i, src, dst):
        start(remote(src, dst, r.aga_s.at[t.i, i], r.aga_r.at[t.i, i], at_a))
        start(remote(src, dst, r.agb_s.at[t.i, i], r.agb_r.at[t.i, i], at_b))

    def gather_own(name):
        t = groups[name]
        to_both(t, 0, t.src(), t.w(zi, col))

    def gather_a(name):
        t = groups[name]
        for k in (1, 0, 2):
            block = t.w(z_from[k], col)
            if k != 1:
                arrived(block, r.agz_s.at[t.i, k], r.agz_r.at[t.i, k], at_z[k])
            to_both(t, 1 + k, block, block)

    def gather_b(name):
        t = groups[name]
        arrived(t.w(zi, col_a), r.aga_s.at[t.i, 0], r.aga_r.at[t.i, 0], at_a)
        part = t.w(zi, col_a)
        if not t.turned:
            for k in hops:
                arrived(t.w(z_from[k], col_a), r.aga_s.at[t.i, 1 + k], r.aga_r.at[t.i, 1 + k], at_a)
            part = t.w_column(col_a)
        start(remote(part, part, r.agb_s.at[t.i, 4], r.agb_r.at[t.i, 4], at_b))

    def gather_end(name):
        t = groups[name]
        arrived(t.w(zi, col_b), r.agb_s.at[t.i, 0], r.agb_r.at[t.i, 0], at_b)
        if not t.turned:
            for k in hops:
                arrived(t.w(z_from[k], col_b), r.agb_s.at[t.i, 1 + k], r.agb_r.at[t.i, 1 + k], at_b)
        part = t.w(zi, col_d) if t.turned else t.w_column(col_d)
        arrived(part, r.agb_s.at[t.i, 4], r.agb_r.at[t.i, 4], at_b)

    def gather_turn(name):
        gather_end(name)
        gather_z(name)

    def gather_turned(name):
        t = groups[name]
        for k in (0, 2):
            arrived(t.w_row(z_from[k]), r.agz_s.at[t.i, k], r.agz_r.at[t.i, k], at_z[k])

    def added(target, *landed):
        total = target[...].astype(F32)
        for ref in landed:
            total = total + ref[...].astype(F32)
        return total

    def z_start(t, part, place):
        for k in hops:
            condition = None if t.direct else jnp.logical_not(inner) if k == 1 else goes[k]
            start(remote(part(z_of[k]), place(k), r.rsz_s.at[t.i, k], r.rsz_r.at[t.i, k], at_z[k]), condition)
        if t.direct:
            return
        end_part = part(jnp.where(inner, 0, 3 - zi))
        beside = (jnp.where(zi == 0, 1, 2) * 4 + col, mp)
        extra = t.tx() if t.turned else t.lx()
        start(remote(end_part, extra, r.rsz_s.at[t.i, 3], r.rsz_r.at[t.i, 3], beside), jnp.logical_not(inner))

    def reduce_b(name):
        t = groups[name]
        if t.turned:
            z_start(t, t.p_row, t.tz)
            return
        for k, c in enumerate((col_b, col_d)):
            start(remote(t.p_column(c), t.lb(k), r.rsb_s.at[t.i, k], r.rsb_r.at[t.i, k], at_b))

    def reduce_on(name):
        t = groups[name]
        if t.direct:
            return
        far = z_of[1]
        extra = t.tx() if t.turned else t.lx()

        @pl.when(inner)
        def _():
            arrived(extra, r.rsz_s.at[t.i, 3], r.rsz_r.at[t.i, 3], at_z[1])
            if t.turned:
                @pl.loop(0, 4)
                def _(c):
                    target = t.p(far, c)
                    target[...] = added(target, t.in_row(extra, c)).astype(LOW)
            else:
                target = t.p(far, col)
                target[...] = added(target, extra).astype(LOW)

        part, place = (t.p_row(far), t.tz(1)) if t.turned else (t.p(far, col), t.lz(1))
        start(remote(part, place, r.rsz_s.at[t.i, 1], r.rsz_r.at[t.i, 1], at_z[1]), inner)

    def z_arrived(t, place):
        places = ((0, None), (1, None), (2, None)) if t.direct else ((1, None), (filled, None), (2, inner))
        for k, condition in places:
            arrived(place(k), r.rsz_s.at[t.i, k], r.rsz_r.at[t.i, k], at_z[1], condition)

    def reduce_turn(name):
        t = groups[name]
        z_arrived(t, t.tz)

        @pl.loop(0, 4)
        def _(c):
            target = t.p(zi, c)
            target[...] = added(target, t.in_row(t.tz(1), c), t.in_row(t.tz(filled), c)).astype(LOW)

        @pl.when(inner)
        def _():
            @pl.loop(0, 4)
            def _(c):
                target = t.p(zi, c)
                target[...] = added(target, t.in_row(t.tz(2), c)).astype(LOW)

        for k, c in enumerate((col_b, col_d)):
            start(remote(t.p(zi, c), t.tb(k), r.rsb_s.at[t.i, k], r.rsb_r.at[t.i, k], at_b))

    def reduce_a(name):
        t = groups[name]
        for k, c in ((1, col_a), (0, col)):
            landed = t.tb(k) if t.turned else t.lb(k)
            arrived(landed, r.rsb_s.at[t.i, k], r.rsb_r.at[t.i, k], at_b)
            if t.turned:
                target = t.p(zi, c)
                target[...] = added(target, landed).astype(LOW)
            else:
                def add(target, view):
                    target[...] = added(target, view(landed)).astype(LOW)
                t.each(c, add)
            if k:
                src, dst = (t.p(zi, c), t.ta()) if t.turned else (t.p_column(c), t.la())
                start(remote(src, dst, r.rsa_s.at[t.i], r.rsa_r.at[t.i], at_a))

    def reduce_z(name):
        t = groups[name]
        landed = t.la()
        arrived(landed, r.rsa_s.at[t.i], r.rsa_r.at[t.i], at_a)

        def add(target, view):
            target[...] = added(target, view(landed)).astype(LOW)
        t.each(col, add)
        z_start(t, lambda z: t.p(z, col), t.lz)

    def reduce_end(name):
        t = groups[name]
        total = t.sum()
        if t.turned:
            arrived(t.ta(), r.rsa_s.at[t.i], r.rsa_r.at[t.i], at_a)
            total[...] = added(t.p(zi, col), t.ta())
        else:
            z_arrived(t, t.lz)
            if t.direct:
                total[...] = added(t.p(zi, col), t.lz(0), t.lz(1), t.lz(2))
            else:
                total[...] = added(t.p(zi, col), t.lz(1), t.lz(filled))

                @pl.when(inner)
                def _():
                    total[...] = added(total, t.lz(2))
        write(total, t.sum_out())

    def move(*steps):
        if g.comm:
            for step, name in zip(steps[::2], steps[1::2]):
                step(name)

    def w8(j):
        return r.w8[j].reshape(g.d, g.f)

    def wide(which, cols):
        if g.comm:
            return r.wf[which, :, :, :, cols].reshape(g.d, -1)
        return r.wf[which, :, cols]

    def put8(j, value):
        r.p8[j] = value.astype(LOW).reshape(r.p8.shape[1:])

    def put_wide(which, cols, value):
        if g.comm:
            r.pf[which, :, :, :, cols] = value.astype(LOW).reshape(g.nz, 4, g.blk, -1)
        else:
            r.pf[which, :, cols] = value.astype(LOW)

    part = g.t // 2

    def exchange(e, i):
        rows = pl.ds(i * part, part)
        return remote(
            r.stage.at[e % 2, rows], r.land.at[e % 3, rows], r.ex_s.at[e, i], r.ex_r.at[e, i], sibling
        )

    def exchange_start(e, product):
        for i in range(2):
            rows = pl.ds(i * part, part)
            r.stage[e % 2, rows] = product(rows).astype(LOW)
            exchange(e, i).start()

    def by_rows(e, body):
        for i in range(2):
            exchange(e, i).wait_recv()
            exchange(e, i).wait_send()

            @pl.loop(0, part // LN_ROWS)
            def _(n):
                rows = pl.ds(pl.multiple_of(i * part + n * LN_ROWS, LN_ROWS), LN_ROWS)
                body(rows, r.stage[e % 2, rows].astype(F32) + r.land[e % 3, rows].astype(F32))

    def norm(values, i):
        return (centre(values)[0] * r.gains[i]).astype(LOW)

    def norm_back(i, values, grad):
        normed, scale = centre(values)
        r.gain_sum[i] += jnp.sum((grad * normed).reshape(-1, 8, g.d), axis=0)
        scaled = grad * r.gains[i]
        return scale * (
            scaled
            - jnp.mean(scaled, axis=-1, keepdims=True)
            - normed * jnp.mean(scaled * normed, axis=-1, keepdims=True)
        )

    masks = head_masks()
    score_scale = HEAD ** (-0.5)
    pairs = g.f // PAIR

    pl.semaphore_wait(barrier, len(greeted))
    small = []

    def meet(src, dst, device):
        i = len(small)
        copy = remote(src, dst, r.small_s.at[i], r.small_r.at[i], device)
        copy.start()
        small.append(copy)
        return copy

    if g.comm:
        spot = lax.broadcasted_iota(jnp.int32, (g.blk, g.d), 0) + me * g.blk
        place = jnp.where(spot == lax.broadcasted_iota(jnp.int32, (g.blk, g.d), 1), 1.0, 0.0).astype(LOW)
        r.gain_pass[0, 0:3] = dot(r.gains_in[...], place, 1, 0).astype(LOW)
        for k in hops:
            meet(r.gain_pass.at[0], r.gain_land.at[k], at_z[k])
    move(
        gather_z, "q", gather_own, "q", gather_own, "co", gather_own, "dn1", gather_z, "k", gather_own, "k",
        gather_z, "v", gather_own, "v", gather_own, "ck", gather_own, "cv", gather_own, "so",
        gather_own, "cq",
    )
    for copy in weights:
        copy.wait()
    total = r.gain_pass[0, 0:3].astype(F32) if g.comm else r.gains_in[...].astype(F32)
    if g.comm:
        for k in hops:
            small[k].wait_recv()
            total = total + r.gain_land[k, 0:3].astype(F32)
        r.gain_pass[1, 0:3] = total.astype(LOW)
        hop = meet(r.gain_pass.at[1], r.gain_land.at[3], at_x)
    r.bias[...] = jnp.full(r.bias.shape, NEGATIVE)
    key = lax.broadcasted_iota(jnp.int32, (g.seq, g.seq), 0)
    query = lax.broadcasted_iota(jnp.int32, (g.seq, g.seq), 1)
    for row in range(g.rows):
        across = r.seg[row // g.row_mb, row % g.row_mb:row % g.row_mb + 1, :].astype(F32)
        down = jnp.sum(jnp.where(key == query, across, 0.0), axis=1, keepdims=True)
        p, at = row * g.seq // PAIR, row * g.seq % PAIR
        r.bias[p, at:at + g.seq, at:at + g.seq] = jnp.where((key <= query) & (down == across), 0.0, NEGATIVE)
    r.gain_sum[...] = jnp.zeros_like(r.gain_sum)
    move(gather_b, "co", gather_on, "q", gather_a, "q", gather_b, "dn1", gather_z, "ck")
    if g.comm:
        hop.wait_recv()
        total = total + r.gain_land[3, 0:3].astype(F32)
        r.gain_pass[2, 0:3] = total.astype(LOW)
        hop = meet(r.gain_pass.at[2], r.gain_land.at[4], at_y)
    move(gather_on, "k", gather_a, "k", gather_z, "cv")
    if g.comm:
        hop.wait_recv()
        total = total + r.gain_land[4, 0:3].astype(F32)
    for i in range(3):
        r.gains[i] = total[i:i + 1]
    bring_hidden.wait()

    @pl.loop(0, g.t // LN_ROWS)
    def _(n):
        rows = pl.ds(pl.multiple_of(n * LN_ROWS, LN_ROWS), LN_ROWS)
        r.a1[rows] = norm(r.hidden[rows].astype(F32), 0)

    def project(j):
        r.qkv[j] = dot(r.a1[...], w8(QKV + j), 1, 0).astype(LOW)

    move(
        gather_on, "v", gather_a, "v", gather_z, "so", gather_b, "q", gather_on, "ck", gather_z, "cq",
        gather_on, "cv", gather_b, "k", gather_z, "up0", gather_on, "so", gather_turn, "co", gather_z, "up1",
        gather_a, "ck", gather_b, "v", gather_on, "cq", gather_z, "dn0", gather_a, "cv", gather_end, "q",
    )
    project(0)
    move(gather_b, "ck", gather_on, "up0", gather_a, "so", gather_own, "up0", gather_end, "k")
    project(1)
    move(gather_b, "cv", gather_end, "v")
    project(2)

    def self_attend(first, last):
        @pl.loop(first, last)
        def _(p):
            rows = pl.ds(pl.multiple_of(p * PAIR, PAIR), PAIR)
            bias = jnp.concatenate([r.bias[p]] * 2, axis=1)
            for h in range(pairs):
                lanes = lanes_of(h)
                queries = stack_heads(r.qkv[0, rows, lanes], masks)
                scores = dot(r.qkv[1, rows, lanes], queries, 1, 1) * score_scale + bias
                weights_low = softmax_keys(scores).astype(LOW)
                r.self_p[p, h] = weights_low
                r.mixed[rows, lanes] = join_heads(dot(weights_low, r.qkv[2, rows, lanes], 0, 0)).astype(LOW)

    def project_images(m):
        for image in range(g.images):
            rows = pl.ds(image * g.ctx, g.ctx)
            r.kv[m, image] = dot(r.enc[rows], w8(CKV + m), 1, 0).astype(LOW)

    self_attend(0, g.t // PAIR // 2)
    move(gather_b, "so", gather_on, "co")
    self_attend(g.t // PAIR // 2, g.t // PAIR)
    bring_enc.wait()
    move(gather_end, "ck")
    project_images(0)
    move(gather_a, "cq", gather_own, "up1", gather_on, "up1", gather_end, "cv")
    project_images(1)
    move(gather_on, "dn0", gather_turn, "dn1", gather_end, "so")
    exchange_start(0, lambda rows: dot(r.mixed[rows], w8(SO), 1, 1))

    def after_self(rows, total):
        resid = r.hidden[rows].astype(F32) + total
        r.resid_one[rows] = resid
        r.a2[rows] = norm(resid, 1)

    move(gather_a, "up0", gather_own, "dn0", gather_b, "cq")
    by_rows(0, after_self)
    move(gather_a, "up1", gather_a, "dn0", gather_b, "up0", gather_end, "cq")
    r.cq[...] = dot(r.a2[...], w8(CQ), 1, 0).astype(LOW)

    def cross_attend(first, last):
        @pl.loop(first, last)
        def _(row):
            rows = pl.ds(pl.multiple_of(row * g.seq, g.seq), g.seq)
            image = (row // g.row_mb) * g.img_mb + r.image_ids[row // g.row_mb, row % g.row_mb]
            for h in range(pairs):
                lanes = lanes_of(h)
                queries = stack_heads(r.cq[rows, lanes], masks)
                scores = dot(r.kv[0, image, :, lanes], queries, 1, 1) * score_scale
                weights_low = softmax_keys(scores).astype(LOW)
                r.cross_p[row * pairs + h] = weights_low
                r.cmixed[rows, lanes] = join_heads(dot(weights_low, r.kv[1, image, :, lanes], 0, 0)).astype(LOW)

    cross_attend(g.rows * 0 // 4, g.rows * 1 // 4)
    move(gather_b, "up1")
    cross_attend(g.rows * 1 // 4, g.rows * 2 // 4)
    cross_attend(g.rows * 2 // 4, g.rows * 3 // 4)
    cross_attend(g.rows * 3 // 4, g.rows * 4 // 4)
    move(gather_on, "dn1", gather_b, "dn0", gather_turned, "co")
    exchange_start(1, lambda rows: dot(r.cmixed[rows], w8(CO), 1, 1))

    def after_cross(rows, total):
        resid = r.resid_one[rows] + total
        r.resid_two[rows] = resid
        r.a3[rows] = norm(resid, 2)

    by_rows(1, after_cross)
    bring_cot.wait()

    def up_half(first):
        @pl.loop(0, half // TILE)
        def _(n):
            cols = pl.ds(pl.multiple_of(first + n * TILE, TILE), TILE)
            pre = dot(r.a3[...], wide(UP, cols), 1, 0)
            below = 0.5 * (1.0 + lax.erf(pre * ROOT_HALF))
            r.act[:, cols] = (pre * below).astype(LOW)
            slope = below + pre * (DENSITY * jnp.exp(-0.5 * (pre * pre)))
            r.slope[:, cols] = slope.astype(r.slope.dtype)

    def grad_wide(which, left, right, first):
        cols = pl.ds(first, half)
        put_wide(which, cols, dot(left[...], right[:, cols], 0, 0))

    def down_half(first):
        @pl.loop(0, half // TILE)
        def _(n):
            cols = pl.ds(pl.multiple_of(first + n * TILE, TILE), TILE)
            grad_act = dot(r.cot[...], wide(DOWN, cols), 1, 0)
            r.slope[:, cols] = (grad_act * r.slope[:, cols].astype(F32)).astype(LOW)

    move(gather_end, "up0")
    up_half(0)
    move(gather_end, "up1")
    up_half(half)
    grad_wide(DOWN, r.cot, r.act, half)
    move(reduce_b, "dn1")
    grad_wide(DOWN, r.cot, r.act, 0)
    move(reduce_b, "dn0")

    everything = pl.ds(0, g.ff)
    move(gather_end, "dn0")
    down_half(0)
    grad_wide(UP, r.a3, r.slope, 0)
    move(reduce_b, "up0")
    move(gather_turned, "dn1")
    down_half(half)
    exchange_start(2, lambda rows: dot(r.slope[rows], wide(UP, everything), 1, 1))
    grad_wide(UP, r.a3, r.slope, half)
    move(reduce_b, "up1")

    def after_up(rows, total):
        grad = r.cot[rows].astype(F32) + norm_back(2, r.resid_two[rows], total)
        r.grad[rows] = grad
        r.grad_low[rows] = grad.astype(LOW)

    by_rows(2, after_up)
    move(reduce_a, "dn0")
    put8(CO, dot(r.grad_low[...], r.cmixed[...], 0, 0))
    move(reduce_b, "co")
    r.g_mixed[...] = dot(r.grad_low[...], w8(CO), 1, 0).astype(LOW)

    def cross_back(m, h):
        lanes = lanes_of(h)
        queries, grads, soft = [], [], []
        for n in range(g.row_mb):
            row = m * g.row_mb + n
            rows = pl.ds(row * g.seq, g.seq)
            image = m * g.img_mb + r.image_ids[m, n]
            grads.append(stack_heads(r.g_mixed[rows, lanes], masks))
            queries.append(stack_heads(r.cq[rows, lanes], masks))
            weights_low = r.cross_p[row * pairs + h]
            soft.append(weights_low)
            prob = weights_low.astype(F32)
            grad_p = dot(r.kv[1, image, :, lanes], grads[-1], 1, 1)
            inner = jnp.sum(prob * grad_p, axis=0, keepdims=True)
            grad_s = (prob * (grad_p - inner)).astype(LOW)
            r.cross_ds[:, lanes_of(n)] = grad_s
            grad_q = join_heads(dot(grad_s, r.kv[0, image, :, lanes], 0, 0)) * score_scale
            r.cq[rows, lanes] = grad_q.astype(LOW)
        soft = jnp.concatenate(soft, axis=1)
        chosen = [
            [
                jnp.where(r.image_ids[m, n] == i, jnp.ones((1, PAIR), F32), 0.0).astype(LOW)
                for i in range(g.img_mb)
            ]
            for n in range(g.row_mb)
        ]

        def picked(parts):
            return jnp.concatenate(
                [jnp.concatenate([v * c for c in cs], axis=1) for v, cs in zip(parts, chosen)], axis=0
            )

        for j, left, parts, scale in ((0, r.cross_ds[...], queries, score_scale), (1, soft, grads, 1.0)):
            both = dot(left, picked(parts), 1, 0)
            for i in range(g.img_mb):
                part = both[:, i * PAIR:(i + 1) * PAIR] * scale
                r.kv[j, m * g.img_mb + i, :, lanes] = part.astype(LOW)

    cross_back(0, 0)
    cross_back(0, 1)
    move(reduce_on, "dn1")
    cross_back(0, 2)
    cross_back(1, 0)
    cross_back(1, 1)
    move(reduce_z, "dn0", reduce_a, "up0")
    cross_back(1, 2)
    move(reduce_on, "co")
    exchange_start(3, lambda rows: dot(r.cq[rows], w8(CQ), 1, 1))
    def grad_images(j):
        put8(CKV + j, dot(r.enc[...], r.kv[j].reshape(g.images * g.ctx, g.f), 0, 0))

    grad_images(0)
    move(reduce_b, "ck")
    grad_images(1)
    move(reduce_b, "cv")
    move(reduce_turn, "dn1", reduce_z, "up0", reduce_a, "up1")
    put8(CQ, dot(r.a2[...], r.cq[...], 0, 0))
    move(reduce_b, "cq")

    def after_query(rows, total):
        grad = r.grad[rows] + norm_back(1, r.resid_one[rows], total)
        r.grad[rows] = grad
        r.grad_low[rows] = grad.astype(LOW)

    by_rows(3, after_query)
    move(reduce_on, "dn0", reduce_a, "ck")
    put8(SO, dot(r.grad_low[...], r.mixed[...], 0, 0))
    move(reduce_b, "so")
    r.g_mixed[...] = dot(r.grad_low[...], w8(SO), 1, 0).astype(LOW)

    def self_back(first, last):
        @pl.loop(first, last)
        def _(p):
            rows = pl.ds(pl.multiple_of(p * PAIR, PAIR), PAIR)
            for h in range(pairs):
                lanes = lanes_of(h)
                queries = stack_heads(r.qkv[0, rows, lanes], masks)
                grads = stack_heads(r.g_mixed[rows, lanes], masks)
                weights_low = r.self_p[p, h]
                prob = weights_low.astype(F32)
                grad_p = dot(r.qkv[2, rows, lanes], grads, 1, 1)
                inner = jnp.sum(prob * grad_p, axis=0, keepdims=True)
                grad_s = (prob * (grad_p - inner)).astype(LOW)
                grad_q = join_heads(dot(grad_s, r.qkv[1, rows, lanes], 0, 0)) * score_scale
                grad_k = dot(grad_s, queries, 1, 0) * score_scale
                grad_v = dot(weights_low, grads, 1, 0)
                r.qkv[0, rows, lanes] = grad_q.astype(LOW)
                r.qkv[1, rows, lanes] = grad_k.astype(LOW)
                r.qkv[2, rows, lanes] = grad_v.astype(LOW)

    move(reduce_turn, "co")
    self_back(0, g.t // PAIR // 2)
    self_back(g.t // PAIR // 2, g.t // PAIR)
    move(reduce_on, "up0", reduce_a, "cv", reduce_z, "up1")
    exchange_start(
        4,
        lambda rows: dot(r.qkv[0, rows], w8(QKV), 1, 1)
        + dot(r.qkv[1, rows], w8(QKV + 1), 1, 1)
        + dot(r.qkv[2, rows], w8(QKV + 2), 1, 1),
    )
    for_name = ("q", "k", "v")

    def grad_project(j):
        put8(QKV + j, dot(r.a1[...], r.qkv[j], 0, 0))
        move(reduce_b, for_name[j])

    def after_qkv(rows, total):
        r.grad[rows] = r.grad[rows] + norm_back(0, r.hidden[rows].astype(F32), total)

    grad_project(0)
    grad_project(1)
    move(reduce_a, "dn1", reduce_z, "ck")
    grad_project(2)
    by_rows(4, after_qkv)
    write(r.grad, r.in_grad)
    for i in range(3):
        r.gain_total[0, i:i + 1] = jnp.sum(r.gain_sum[i], axis=0, keepdims=True)
    if g.comm:
        first = len(small)
        for k in hops:
            meet(r.gain_total.at[0], r.total_land.at[k], at_z[k])

    def features(j, h):
        if g.comm:
            return r.w8[j, pl.ds(h * (g.nz // 2), g.nz // 2)].reshape(g.d // 2, g.f)
        return r.w8[j, pl.ds(pl.multiple_of(h * (g.d // 2), g.d // 2), g.d // 2)]

    def encoder_part(image, h):
        return dot(r.kv[0, image], features(CKV, h), 1, 1) + dot(r.kv[1, image], features(CKV + 1, h), 1, 1)

    strips = g.d // 2 // PAIR

    def encoder_keep(image, value):
        for h in range(strips):
            r.cross_p[image * strips + h] = value[:, h * PAIR:(h + 1) * PAIR].astype(LOW)

    def encoder_copy(image):
        part = pl.ds(image * strips, strips)
        return remote(r.cross_p.at[part], r.enc_land.at[part], r.enc_s.at[image], r.enc_r.at[image], sibling)

    def encoder_leave(image):
        encoder_keep(image, encoder_part(image, 1 - mp))
        encoder_copy(image).start()

    def encoder_join(image):
        encoder_copy(image).wait_recv()
        encoder_copy(image).wait_send()
        landed = jnp.concatenate([r.enc_land[image * strips + h] for h in range(strips)], axis=1)
        encoder_keep(image, encoder_part(image, mp) + landed.astype(F32))
        rows = pl.ds(image * g.ctx, g.ctx)
        for h in range(strips):
            write(r.cross_p.at[image * strips + h], r.enc_grad.at[rows, lanes_of(h)])

    def after_down(rows, total):
        r.a3[rows] = (r.resid_two[rows] + total).astype(LOW)

    move(reduce_z, "cv")
    encoder_leave(0)
    move(reduce_on, "up1")
    encoder_leave(1)
    encoder_leave(2)
    move(reduce_on, "ck", reduce_a, "cq")
    encoder_leave(3)
    exchange_start(5, lambda rows: dot(r.act[rows], wide(DOWN, everything), 1, 1))
    move(reduce_on, "cv")
    if g.comm:
        total = r.gain_total[0]
        for k in hops:
            small[first + k].wait_recv()
            total = total + r.total_land[k]
        r.gain_total[1] = total
        hop = meet(r.gain_total.at[1], r.total_land.at[3], at_x)
    encoder_join(0)
    move(reduce_a, "so")
    encoder_join(1)
    encoder_join(2)
    move(reduce_a, "co")
    encoder_join(3)
    move(reduce_z, "cq")
    by_rows(5, after_down)
    write(r.a3, r.out)
    move(
        reduce_end, "dn1", reduce_end, "dn0", reduce_end, "up0", reduce_end, "up1", reduce_end, "ck",
        reduce_end, "cv", reduce_z, "so", reduce_end, "co", reduce_on, "cq", reduce_a, "q",
    )
    if g.comm:
        hop.wait_recv()
        r.gain_total[2] = r.gain_total[1] + r.total_land[3]
        hop = meet(r.gain_total.at[2], r.total_land.at[4], at_y)
    move(reduce_on, "so", reduce_end, "cq", reduce_a, "k", reduce_z, "q", reduce_end, "so")
    if g.comm:
        hop.wait_recv()
        total = r.gain_total[2] + r.total_land[4]
    if g.comm:
        spot = lax.broadcasted_iota(jnp.int32, (g.d, g.blk), 1) + me * g.blk
        place = jnp.where(spot == lax.broadcasted_iota(jnp.int32, (g.d, g.blk), 0), 1.0, 0.0)
        mine = lax.dot_general(
            total, place, (((1,), (0,)), ((), ())), precision=lax.Precision.HIGHEST, preferred_element_type=F32
        )
        r.gain_out[...] = mine[0:3]
    else:
        r.gain_out[...] = r.gain_total[0, 0:3]
    move(reduce_z, "k", reduce_a, "v", reduce_end, "q", reduce_z, "v", reduce_end, "k", reduce_end, "v")
    for copy in written:
        copy.wait()
    for copy in small:
        copy.wait_send()
    for copy, condition in started:
        only(condition, copy.wait_send)


def run_layer(g, operands):
    vmem = pl.BlockSpec(memory_space=pltpu.VMEM)
    smem = pl.BlockSpec(memory_space=pltpu.SMEM)
    anywhere = pl.BlockSpec(memory_space=pl.ANY)
    shape = jax.ShapeDtypeStruct
    ins = dict(
        image_ids=smem, seg=vmem, hidden_in=anywhere, gains_in=vmem, cot_in=anywhere, enc_in=anywhere,
        qkv_in=anywhere, so_in=anywhere, cq_in=anywhere, ckv_in=anywhere, co_in=anywhere,
        up_in=anywhere, down_in=anywhere,
    )
    outs = dict(
        out=(shape((g.t, g.d), LOW), anywhere),
        in_grad=(shape((g.t, g.d), F32), anywhere),
        enc_grad=(shape((g.images * g.ctx, g.d // 2), LOW), anywhere),
        gain_out=(shape((3, g.blk if g.comm else g.d), F32), vmem),
    )
    grid = (g.nz, 4, g.blk) if g.comm else (g.d,)
    dma = pltpu.SemaphoreType.DMA
    scratch = dict(
        w8=pltpu.VMEM((MATS, *grid, g.f), LOW),
        wf=pltpu.VMEM((2, *grid, g.ff), LOW),
        hidden=pltpu.VMEM((g.t, g.d), LOW),
        enc=pltpu.VMEM((g.images * g.ctx, g.d), LOW),
        cot=pltpu.VMEM((g.t, g.d), LOW),
        gains=pltpu.VMEM((3, 1, g.d), F32),
        gain_sum=pltpu.VMEM((3, 8, g.d), F32),
        gain_total=pltpu.VMEM((3, 8, g.d), F32),
        bias=pltpu.VMEM((g.t // PAIR, PAIR, PAIR), F32),
        a1=pltpu.VMEM((g.t, g.d), LOW),
        a2=pltpu.VMEM((g.t, g.d), LOW),
        a3=pltpu.VMEM((g.t, g.d), LOW),
        qkv=pltpu.VMEM((3, g.t, g.f), LOW),
        mixed=pltpu.VMEM((g.t, g.f), LOW),
        cq=pltpu.VMEM((g.t, g.f), LOW),
        cmixed=pltpu.VMEM((g.t, g.f), LOW),
        g_mixed=pltpu.VMEM((g.t, g.f), LOW),
        kv=pltpu.VMEM((2, g.images, g.ctx, g.f), LOW),
        self_p=pltpu.VMEM((g.t // PAIR, g.f // PAIR, PAIR, 2 * PAIR), LOW),
        cross_p=pltpu.VMEM((g.rows * (g.f // PAIR), g.ctx, PAIR), LOW),
        cross_ds=pltpu.VMEM((g.ctx, g.row_mb * PAIR), LOW),
        resid_one=pltpu.VMEM((g.t, g.d), F32),
        resid_two=pltpu.VMEM((g.t, g.d), F32),
        grad=pltpu.VMEM((g.t, g.d), F32),
        grad_low=pltpu.VMEM((g.t, g.d), LOW),
        act=pltpu.VMEM((g.t, g.ff), LOW),
        slope=pltpu.VMEM((g.t, g.ff), LOW),
        stage=pltpu.VMEM((2, g.t, g.d), LOW),
        land=pltpu.VMEM((3, g.t, g.d), LOW),
        enc_land=pltpu.VMEM((g.images * (g.d // 2 // PAIR), g.ctx, PAIR), LOW),
        local_sem=dma((10,)),
        ex_s=dma((6, 2)), ex_r=dma((6, 2)),
        enc_s=dma((g.images,)), enc_r=dma((g.images,)),
        write_sem=dma((16 + g.images * (g.d // 2 // PAIR),)),
    )
    if g.comm:
        outs.update(
            g8_out=(shape((MATS, g.blk, g.f), F32), anywhere),
            gf_out=(shape((2, g.blk, g.ff), F32), anywhere),
        )
        hops = g.nz - 1
        scratch.update(
            g8=pltpu.VMEM((MATS, g.blk, g.f), F32),
            gf=pltpu.VMEM((2, g.blk, g.ff), F32),
            p8=pltpu.VMEM((MATS, *grid, g.f), LOW),
            pf=pltpu.VMEM((2, *grid, g.ff), LOW),
            lb8=pltpu.VMEM((2, MATS - 1, g.nz, g.blk, g.f), LOW),
            lbf=pltpu.VMEM((2, 3, g.nz, g.blk, g.ff // 2), LOW),
            la8=pltpu.VMEM((MATS - 1, g.nz, g.blk, g.f), LOW),
            laf=pltpu.VMEM((3, g.nz, g.blk, g.ff // 2), LOW),
            lz8=pltpu.VMEM((hops, MATS - 1, g.blk, g.f), LOW),
            lzf=pltpu.VMEM((hops, 3, g.blk, g.ff // 2), LOW),
            lx8=pltpu.VMEM((MATS - 1, g.blk, g.f), LOW),
            lxf=pltpu.VMEM((3, g.blk, g.ff // 2), LOW),
            turnf_z=pltpu.VMEM((hops, 4, g.blk, g.ff // 2), LOW),
            turnf_x=pltpu.VMEM((4, g.blk, g.ff // 2), LOW),
            turnf_b=pltpu.VMEM((2, g.blk, g.ff // 2), LOW),
            turnf_a=pltpu.VMEM((g.blk, g.ff // 2), LOW),
            turn8_z=pltpu.VMEM((hops, 1, 4, g.blk, g.f), LOW),
            turn8_x=pltpu.VMEM((1, 4, g.blk, g.f), LOW),
            turn8_b=pltpu.VMEM((2, 1, g.blk, g.f), LOW),
            turn8_a=pltpu.VMEM((1, g.blk, g.f), LOW),
            gain_land=pltpu.VMEM((hops + 2, 16, g.d), LOW),
            gain_pass=pltpu.VMEM((3, 16, g.d), LOW),
            total_land=pltpu.VMEM((hops + 2, 8, g.d), F32),
            agz_s=dma((12, 4)), agz_r=dma((12, 4)),
            aga_s=dma((12, g.nz)), aga_r=dma((12, g.nz)),
            agb_s=dma((12, g.nz + 1)), agb_r=dma((12, g.nz + 1)),
            rsz_s=dma((12, 4)), rsz_r=dma((12, 4)),
            rsa_s=dma((12,)), rsa_r=dma((12,)),
            rsb_s=dma((12, 2)), rsb_r=dma((12, 2)),
            small_s=dma((2 * hops + 4,)), small_r=dma((2 * hops + 4,)),
        )
    else:
        outs.update(
            p8=(shape((MATS, g.d, g.f), LOW), vmem),
            pf=(shape((2, g.d, g.ff), LOW), vmem),
        )
    g.names = (*ins, *outs, *scratch)
    return dict(zip(outs, pl.pallas_call(
        functools.partial(layer, g),
        out_shape=[o[0] for o in outs.values()],
        in_specs=list(ins.values()),
        out_specs=[o[1] for o in outs.values()],
        scratch_shapes=list(scratch.values()),
        compiler_params=pltpu.CompilerParams(
            collective_id=0, has_side_effects=True, vmem_limit_bytes=63 * 2**20
        ),
        name="layer",
    )(*operands)))


def pass_on(g, out, in_grad, enc, gain, g8, gf, *refs):
    outs, (v_out, v_in, v_gain, v_g8, v_gf, low, full, in_sem, out_sem) = refs[:11], refs[11:]
    coming, leaving = [], []

    def bring(src, dst):
        coming.append(pltpu.make_async_copy(src, dst, in_sem.at[len(coming)]))
        coming[-1].start()

    def leave(src, dst):
        leaving.append(pltpu.make_async_copy(src, dst, out_sem.at[len(leaving)]))
        leaving[-1].start()

    halves = [pl.ds(i * g.t // 2, g.t // 2) for i in range(2)]
    images = [pl.ds(i * g.ctx, g.ctx) for i in range(g.images)]
    for rows in images:
        bring(enc.at[rows], low.at[rows])
    for rows in halves:
        bring(in_grad.at[rows], v_in.at[rows])
    bring(out, v_out)
    bring(g8, v_g8)
    bring(gf, v_gf)
    bring(gain, v_gain)
    for i, rows in enumerate(images):
        coming[i].wait()
        full[rows] = low[rows].astype(F32)
        leave(full.at[rows], outs[2].at[rows])
    for copy, rows in zip(coming[g.images:], halves):
        copy.wait()
        leave(v_in.at[rows], outs[1].at[rows])
    for copy in coming[g.images + 2:]:
        copy.wait()
    leave(v_out, outs[0])
    leave(v_gain, outs[3])
    for src, dst in zip(
        (v_g8.at[pl.ds(QKV, 3)], v_g8.at[SO], v_g8.at[CQ], v_g8.at[pl.ds(CKV, 2)], v_g8.at[CO], v_gf.at[UP], v_gf.at[DOWN]),
        outs[4:],
    ):
        leave(src, dst)
    for copy in leaving:
        copy.wait()


def hand_over(g, o):
    shape = jax.ShapeDtypeStruct
    tokens, enc = (g.t, g.d), (g.images * g.ctx, g.d // 2)
    one, wide = (g.blk, g.f), (g.blk, g.ff)
    shapes = (tokens, tokens, enc, (3, g.blk), (3, *one), one, one, (2, *one), one, wide, wide)
    anywhere = pl.BlockSpec(memory_space=pl.ANY)
    dma = pltpu.SemaphoreType.DMA
    return pl.pallas_call(
        functools.partial(pass_on, g),
        out_shape=[shape(s, LOW if i == 0 else F32) for i, s in enumerate(shapes)],
        in_specs=[anywhere] * 6,
        out_specs=[anywhere] * 11,
        scratch_shapes=[
            pltpu.VMEM(tokens, LOW), pltpu.VMEM(tokens, F32), pltpu.VMEM((3, g.blk), F32),
            pltpu.VMEM((MATS, *one), F32), pltpu.VMEM((2, *wide), F32),
            pltpu.VMEM(enc, LOW), pltpu.VMEM(enc, F32), dma((g.images + 6,)), dma((g.images + 11,)),
        ],
        compiler_params=pltpu.CompilerParams(vmem_limit_bytes=63 * 2**20),
        name="hand_over",
    )(o["out"], o["in_grad"], o["enc_grad"], o["gain_out"], o["g8_out"], o["gf_out"])


def body(
    dp, mp, hidden, encoder_tokens, segment_ids, image_index, cotangent, norm_gains, qkv_weight,
    self_out_weight, cross_query_weight, cross_kv_weight, cross_out_weight, up_weight, down_weight,
):
    micro, row_mb, seq, d = hidden.shape
    img_mb, ctx = encoder_tokens.shape[1:3]
    blk, f = self_out_weight.shape
    g = SimpleNamespace(
        micro=micro, row_mb=row_mb, seq=seq, d=d, img_mb=img_mb, ctx=ctx, blk=blk, f=f,
        ff=up_weight.shape[1], rows=micro * row_mb, t=micro * row_mb * seq, images=micro * img_mb,
        nz=dp // 4, comm=dp == 16 and blk % 16 == 0,
    )
    weights = [
        qkv_weight, self_out_weight, cross_query_weight, cross_kv_weight, cross_out_weight, up_weight, down_weight,
    ]
    gains = norm_gains
    if not g.comm:
        gains = lax.all_gather(norm_gains, "dp", axis=1, tiled=True)
        weights = [lax.all_gather(w, "dp", axis=w.ndim - 2, tiled=True) for w in weights]
    for i in (1, 2, 4):
        weights[i] = weights[i][None]
    o = run_layer(g, (
        image_index, segment_ids, hidden.reshape(g.t, d), gains, cotangent.reshape(g.t, d),
        encoder_tokens.reshape(g.images * ctx, d), *weights,
    ))
    if g.comm:
        whole = hand_over(g, o)
    else:
        small = lax.psum_scatter(o["p8"].astype(F32), "dp", scatter_dimension=1, tiled=True)
        wide = lax.psum_scatter(o["pf"].astype(F32), "dp", scatter_dimension=1, tiled=True)
        whole = (
            o["out"], o["in_grad"], o["enc_grad"].astype(F32),
            lax.psum_scatter(o["gain_out"], "dp", scatter_dimension=1, tiled=True),
            small[QKV:QKV + 3], small[SO], small[CQ], small[CKV:CKV + 2], small[CO], wide[UP], wide[DOWN],
        )
    return (
        whole[0].reshape(hidden.shape), whole[1].reshape(hidden.shape),
        whole[2].reshape(micro, img_mb, ctx, d // 2), *whole[3:],
    )


def solution(mesh):
    tokens, kept = P(None, "dp", None, None), P("dp", "mp")
    three = P(None, "dp", "mp")
    return jax.shard_map(
        functools.partial(body, mesh.shape["dp"], mesh.shape["mp"]),
        mesh=mesh,
        in_specs=(
            tokens, tokens, P(None, "dp", None), P(None, "dp"), tokens, P(None, "dp"),
            three, kept, kept, three, kept, kept, kept,
        ),
        out_specs=(
            tokens, tokens, P(None, "dp", None, "mp"), P(None, "dp"),
            three, kept, kept, three, kept, kept, kept,
        ),
        check_vma=False,
    )
```

```python
import functools
from types import SimpleNamespace

import jax
import jax.numpy as jnp
from jax import lax
from jax.experimental import pallas as pl
from jax.experimental.pallas import tpu as pltpu
from jax.sharding import PartitionSpec as P

HEAD = 64
PAIR = 2 * HEAD
EPSILON = 1e-05
NEGATIVE = -1e30
ROOT_HALF = 0.7071067811865476
DENSITY = 0.3989422804014327
MESH = pl.DeviceIdType.MESH
LOW = jnp.bfloat16
F32 = jnp.float32
QKV, SO, CQ, CKV, CO, MATS = 0, 3, 4, 5, 7, 8
DIRECT = ("q", "k", "v")
UP, DOWN = 0, 1
LN_ROWS = 128
TILE = 256


def dot(left, right, left_dim, right_dim):
    return lax.dot_general(
        left, right, (((left_dim,), (right_dim,)), ((), ())), preferred_element_type=F32
    )


def lanes_of(pair):
    return pl.ds(pair * PAIR, PAIR)


def head_masks():
    lane = lax.broadcasted_iota(jnp.int32, (1, PAIR), 1)
    first = jnp.where(lane < HEAD, 1.0, 0.0)
    return first.astype(LOW), (1.0 - first).astype(LOW)


def stack_heads(values, masks):
    return jnp.concatenate([values * masks[0], values * masks[1]], axis=0)


def join_heads(stacked):
    half = stacked.shape[0] // 2
    lane = lax.broadcasted_iota(jnp.int32, (half, PAIR), 1)
    return jnp.where(lane < HEAD, stacked[:half], stacked[half:])


def centre(values):
    centred = values - jnp.mean(values, axis=-1, keepdims=True)
    spread = jnp.mean(centred * centred, axis=-1, keepdims=True)
    scale = lax.rsqrt(spread + EPSILON)
    return centred * scale, scale


def softmax_keys(scores):
    shifted = jnp.exp(scores - jnp.max(scores, axis=0, keepdims=True))
    return shifted / jnp.sum(shifted, axis=0, keepdims=True)


def layer(g, *refs):
    r = SimpleNamespace(**dict(zip(g.names, refs)))
    me, mp = lax.axis_index("dp"), lax.axis_index("mp")
    zi, col = me // 4, me % 4
    sibling = (me, 1 - mp)
    col_x = col + 1 - 2 * (col % 2)
    col_y = (col + 2) % 4
    col_d = (col_x + 2) % 4
    col_a = mp * col_x + (1 - mp) * col_y
    col_b = mp * col_y + (1 - mp) * col_x
    at_x, at_y = (zi * 4 + col_x, mp), (zi * 4 + col_y, mp)
    at_a, at_b = (zi * 4 + col_a, mp), (zi * 4 + col_b, mp)
    z_of = [(zi + k) % g.nz for k in range(1, g.nz)]
    z_from = [(zi + g.nz - k) % g.nz for k in range(1, g.nz)]
    at_z = [(z * 4 + col, mp) for z in z_of]

    greeted = [sibling] + ([at_x, at_y] + at_z if g.comm else [])
    barrier = pltpu.get_barrier_semaphore()
    for device in greeted:
        pl.semaphore_signal(barrier, inc=1, device_id=device, device_id_type=MESH)

    def remote(src, dst, send, recv, device):
        return pltpu.make_async_remote_copy(
            src_ref=src, dst_ref=dst, send_sem=send, recv_sem=recv, device_id=device, device_id_type=MESH
        )

    local = []

    def bring(src, dst):
        copy = pltpu.make_async_copy(src, dst, r.local_sem.at[len(local)])
        copy.start()
        local.append(copy)
        return copy

    def slot(first, count):
        ref = r.w8.at[pl.ds(first, count)]
        return ref.at[:, zi, col] if g.comm else ref

    def wide_slot(which):
        return r.wf.at[which, zi, col] if g.comm else r.wf.at[which]

    weights = [
        bring(r.qkv_in, slot(QKV, 3)),
        bring(r.so_in, slot(SO, 1)),
        bring(r.cq_in, slot(CQ, 1)),
        bring(r.ckv_in, slot(CKV, 2)),
        bring(r.co_in, slot(CO, 1)),
        bring(r.up_in, wide_slot(UP)),
        bring(r.down_in, wide_slot(DOWN)),
    ]
    bring_hidden = bring(r.hidden_in, r.hidden)
    bring_enc = bring(r.enc_in, r.enc)
    bring_cot = bring(r.cot_in, r.cot)

    half = g.ff // 2

    def mats(first, ref, at):
        part = pl.ds(first, 1)

        def each(c, body):
            @pl.loop(0, g.nz)
            def _(z):
                body(r.p8.at[first, z, c], lambda landed: landed.at[0, z])

        return SimpleNamespace(
            src=lambda: ref.at[pl.ds(at, 1)],
            w=lambda z, c: r.w8.at[part, z, c], w_column=lambda c: r.w8.at[part, :, c],
            w_row=lambda z: r.w8.at[part, z], p_row=lambda z: r.p8.at[part, z],
            p=lambda z, c: r.p8.at[part, z, c], p_column=lambda c: r.p8.at[part, :, c],
            lb=lambda k: r.lb8.at[k, part], la=lambda: r.la8.at[part], lz=lambda k: r.lz8.at[k, part],
            lx=lambda: r.lx8.at[part], in_row=lambda row, c: row.at[:, c],
            tz=lambda k: r.turn8_z.at[k], tb=lambda k: r.turn8_b.at[k], ta=lambda: r.turn8_a,
            tx=lambda: r.turn8_x, each=each, sum=lambda: r.g8.at[part], sum_out=lambda: r.g8_out.at[part],
        )

    def strip(which, first, i, ref):
        cols = pl.ds(first, half)

        def each(c, body):
            @pl.loop(0, g.nz)
            def _(z):
                body(r.pf.at[which, z, c, :, cols], lambda landed: landed.at[z])

        return SimpleNamespace(
            src=lambda: ref.at[:, cols],
            w=lambda z, c: r.wf.at[which, z, c, :, cols], w_column=lambda c: r.wf.at[which, :, c, :, cols],
            w_row=lambda z: r.wf.at[which, z, :, :, cols], p_row=lambda z: r.pf.at[which, z, :, :, cols],
            p=lambda z, c: r.pf.at[which, z, c, :, cols], p_column=lambda c: r.pf.at[which, :, c, :, cols],
            lb=lambda k: r.lbf.at[k, i], la=lambda: r.laf.at[i], lz=lambda k: r.lzf.at[k, i],
            lx=lambda: r.lxf.at[i], in_row=lambda row, c: row.at[c],
            tz=lambda k: r.turnf_z.at[k], tb=lambda k: r.turnf_b.at[k], ta=lambda: r.turnf_a,
            tx=lambda: r.turnf_x, each=each, sum=lambda: r.gf.at[which, :, cols],
            sum_out=lambda: r.gf_out.at[which, :, cols],
        )

    groups = dict(
        q=mats(QKV, r.qkv_in, 0), k=mats(QKV + 1, r.qkv_in, 1), v=mats(QKV + 2, r.qkv_in, 2),
        ck=mats(CKV, r.ckv_in, 0), cv=mats(CKV + 1, r.ckv_in, 1),
        so=mats(SO, r.so_in, 0), cq=mats(CQ, r.cq_in, 0), co=mats(CO, r.co_in, 0),
        up0=strip(UP, 0, 0, r.up_in), up1=strip(UP, half, 1, r.up_in),
        dn0=strip(DOWN, 0, 2, r.down_in), dn1=strip(DOWN, half, 3, r.down_in),
    )
    for i, (name, group) in enumerate(groups.items()):
        group.i, group.turned, group.direct = i, name in ("co", "dn1"), name in DIRECT

    inner = (zi == 1) | (zi == 2)
    goes = (zi != 3, None, zi != 0)
    hops = range(3)
    other = 3 * (2 - zi)
    onward = 3 * (zi - 1)
    filled = 2 * jnp.where(zi == 0, 1, 0)

    written = []

    def write(src, dst):
        copy = pltpu.make_async_copy(src, dst, r.write_sem.at[len(written)])
        copy.start()
        written.append(copy)

    started = []

    def only(condition, act):
        if condition is None:
            act()
        else:
            pl.when(condition)(act)

    def start(copy, condition=None):
        only(condition, copy.start)
        started.append((copy, condition))

    def arrived(ref, send, recv, device, condition=None):
        only(condition, remote(ref, ref, send, recv, device).wait_recv)

    def gather_z(name):
        t = groups[name]
        for k in hops:
            src, dst = (t.w_row(zi), t.w_row(zi)) if t.turned else (t.src(), t.w(zi, col))
            start(remote(src, dst, r.agz_s.at[t.i, k], r.agz_r.at[t.i, k], at_z[k]), None if t.direct else goes[k])

    def z_part(t, z):
        return t.w_row(z) if t.turned else t.w(z, col)

    def gather_on(name):
        t = groups[name]
        arrived(z_part(t, z_from[1]), r.agz_s.at[t.i, 1], r.agz_r.at[t.i, 1], at_z[1])
        if t.direct:
            return
        part = z_part(t, jnp.where(inner, other, 0))
        start(
            remote(part, part, r.agz_s.at[t.i, 3], r.agz_r.at[t.i, 2 * jnp.where(zi == 2, 1, 0)],
                   (jnp.where(inner, onward, 0) * 4 + col, mp)),
            inner,
        )

    def to_both(t, i, src, dst):
        start(remote(src, dst, r.aga_s.at[t.i, i], r.aga_r.at[t.i, i], at_a))
        start(remote(src, dst, r.agb_s.at[t.i, i], r.agb_r.at[t.i, i], at_b))

    def gather_own(name):
        t = groups[name]
        to_both(t, 0, t.src(), t.w(zi, col))

    def gather_a(name):
        t = groups[name]
        for k in (1, 0, 2):
            block = t.w(z_from[k], col)
            if k != 1:
                arrived(block, r.agz_s.at[t.i, k], r.agz_r.at[t.i, k], at_z[k])
            to_both(t, 1 + k, block, block)

    def gather_b(name):
        t = groups[name]
        arrived(t.w(zi, col_a), r.aga_s.at[t.i, 0], r.aga_r.at[t.i, 0], at_a)
        part = t.w(zi, col_a)
        if not t.turned:
            for k in hops:
                arrived(t.w(z_from[k], col_a), r.aga_s.at[t.i, 1 + k], r.aga_r.at[t.i, 1 + k], at_a)
            part = t.w_column(col_a)
        start(remote(part, part, r.agb_s.at[t.i, 4], r.agb_r.at[t.i, 4], at_b))

    def gather_end(name):
        t = groups[name]
        arrived(t.w(zi, col_b), r.agb_s.at[t.i, 0], r.agb_r.at[t.i, 0], at_b)
        if not t.turned:
            for k in hops:
                arrived(t.w(z_from[k], col_b), r.agb_s.at[t.i, 1 + k], r.agb_r.at[t.i, 1 + k], at_b)
        part = t.w(zi, col_d) if t.turned else t.w_column(col_d)
        arrived(part, r.agb_s.at[t.i, 4], r.agb_r.at[t.i, 4], at_b)

    def gather_turn(name):
        gather_end(name)
        gather_z(name)

    def gather_turned(name):
        t = groups[name]
        for k in (0, 2):
            arrived(t.w_row(z_from[k]), r.agz_s.at[t.i, k], r.agz_r.at[t.i, k], at_z[k])

    def added(target, *landed):
        total = target[...].astype(F32)
        for ref in landed:
            total = total + ref[...].astype(F32)
        return total

    def z_start(t, part, place):
        for k in hops:
            condition = None if t.direct else jnp.logical_not(inner) if k == 1 else goes[k]
            start(remote(part(z_of[k]), place(k), r.rsz_s.at[t.i, k], r.rsz_r.at[t.i, k], at_z[k]), condition)
        if t.direct:
            return
        end_part = part(jnp.where(inner, 0, 3 - zi))
        beside = (jnp.where(zi == 0, 1, 2) * 4 + col, mp)
        extra = t.tx() if t.turned else t.lx()
        start(remote(end_part, extra, r.rsz_s.at[t.i, 3], r.rsz_r.at[t.i, 3], beside), jnp.logical_not(inner))

    def reduce_b(name):
        t = groups[name]
        if t.turned:
            z_start(t, t.p_row, t.tz)
            return
        for k, c in enumerate((col_b, col_d)):
            start(remote(t.p_column(c), t.lb(k), r.rsb_s.at[t.i, k], r.rsb_r.at[t.i, k], at_b))

    def reduce_on(name):
        t = groups[name]
        if t.direct:
            return
        far = z_of[1]
        extra = t.tx() if t.turned else t.lx()

        @pl.when(inner)
        def _():
            arrived(extra, r.rsz_s.at[t.i, 3], r.rsz_r.at[t.i, 3], at_z[1])
            if t.turned:
                @pl.loop(0, 4)
                def _(c):
                    target = t.p(far, c)
                    target[...] = added(target, t.in_row(extra, c)).astype(LOW)
            else:
                target = t.p(far, col)
                target[...] = added(target, extra).astype(LOW)

        part, place = (t.p_row(far), t.tz(1)) if t.turned else (t.p(far, col), t.lz(1))
        start(remote(part, place, r.rsz_s.at[t.i, 1], r.rsz_r.at[t.i, 1], at_z[1]), inner)

    def z_arrived(t, place):
        places = ((0, None), (1, None), (2, None)) if t.direct else ((1, None), (filled, None), (2, inner))
        for k, condition in places:
            arrived(place(k), r.rsz_s.at[t.i, k], r.rsz_r.at[t.i, k], at_z[1], condition)

    def reduce_turn(name):
        t = groups[name]
        z_arrived(t, t.tz)

        @pl.loop(0, 4)
        def _(c):
            target = t.p(zi, c)
            target[...] = added(target, t.in_row(t.tz(1), c), t.in_row(t.tz(filled), c)).astype(LOW)

        @pl.when(inner)
        def _():
            @pl.loop(0, 4)
            def _(c):
                target = t.p(zi, c)
                target[...] = added(target, t.in_row(t.tz(2), c)).astype(LOW)

        for k, c in enumerate((col_b, col_d)):
            start(remote(t.p(zi, c), t.tb(k), r.rsb_s.at[t.i, k], r.rsb_r.at[t.i, k], at_b))

    def reduce_a(name):
        t = groups[name]
        for k, c in ((1, col_a), (0, col)):
            landed = t.tb(k) if t.turned else t.lb(k)
            arrived(landed, r.rsb_s.at[t.i, k], r.rsb_r.at[t.i, k], at_b)
            if t.turned:
                target = t.p(zi, c)
                target[...] = added(target, landed).astype(LOW)
            else:
                def add(target, view):
                    target[...] = added(target, view(landed)).astype(LOW)
                t.each(c, add)
            if k:
                src, dst = (t.p(zi, c), t.ta()) if t.turned else (t.p_column(c), t.la())
                start(remote(src, dst, r.rsa_s.at[t.i], r.rsa_r.at[t.i], at_a))

    def reduce_z(name):
        t = groups[name]
        landed = t.la()
        arrived(landed, r.rsa_s.at[t.i], r.rsa_r.at[t.i], at_a)

        def add(target, view):
            target[...] = added(target, view(landed)).astype(LOW)
        t.each(col, add)
        z_start(t, lambda z: t.p(z, col), t.lz)

    def reduce_end(name):
        t = groups[name]
        total = t.sum()
        if t.turned:
            arrived(t.ta(), r.rsa_s.at[t.i], r.rsa_r.at[t.i], at_a)
            total[...] = added(t.p(zi, col), t.ta())
        else:
            z_arrived(t, t.lz)
            if t.direct:
                total[...] = added(t.p(zi, col), t.lz(0), t.lz(1), t.lz(2))
            else:
                total[...] = added(t.p(zi, col), t.lz(1), t.lz(filled))

                @pl.when(inner)
                def _():
                    total[...] = added(total, t.lz(2))
        write(total, t.sum_out())

    def move(*steps):
        if g.comm:
            for step, name in zip(steps[::2], steps[1::2]):
                step(name)

    def w8(j):
        return r.w8[j].reshape(g.d, g.f)

    def wide(which, cols):
        if g.comm:
            return r.wf[which, :, :, :, cols].reshape(g.d, -1)
        return r.wf[which, :, cols]

    def put8(j, value):
        r.p8[j] = value.astype(LOW).reshape(r.p8.shape[1:])

    def put_wide(which, cols, value):
        if g.comm:
            r.pf[which, :, :, :, cols] = value.astype(LOW).reshape(g.nz, 4, g.blk, -1)
        else:
            r.pf[which, :, cols] = value.astype(LOW)

    part = g.t // 2

    def exchange(e, i):
        rows = pl.ds(i * part, part)
        return remote(
            r.stage.at[e % 2, rows], r.land.at[e % 3, rows], r.ex_s.at[e, i], r.ex_r.at[e, i], sibling
        )

    def exchange_start(e, product):
        for i in range(2):
            rows = pl.ds(i * part, part)
            r.stage[e % 2, rows] = product(rows).astype(LOW)
            exchange(e, i).start()

    def by_rows(e, body):
        for i in range(2):
            exchange(e, i).wait_recv()
            exchange(e, i).wait_send()

            @pl.loop(0, part // LN_ROWS)
            def _(n):
                rows = pl.ds(pl.multiple_of(i * part + n * LN_ROWS, LN_ROWS), LN_ROWS)
                body(rows, r.stage[e % 2, rows].astype(F32) + r.land[e % 3, rows].astype(F32))

    def norm(values, i):
        return (centre(values)[0] * r.gains[i]).astype(LOW)

    def norm_back(i, values, grad):
        normed, scale = centre(values)
        r.gain_sum[i] += jnp.sum((grad * normed).reshape(-1, 8, g.d), axis=0)
        scaled = grad * r.gains[i]
        return scale * (
            scaled
            - jnp.mean(scaled, axis=-1, keepdims=True)
            - normed * jnp.mean(scaled * normed, axis=-1, keepdims=True)
        )

    masks = head_masks()
    score_scale = HEAD ** (-0.5)
    pairs = g.f // PAIR

    pl.semaphore_wait(barrier, len(greeted))
    small = []

    def meet(src, dst, device):
        i = len(small)
        copy = remote(src, dst, r.small_s.at[i], r.small_r.at[i], device)
        copy.start()
        small.append(copy)
        return copy

    if g.comm:
        spot = lax.broadcasted_iota(jnp.int32, (g.blk, g.d), 0) + me * g.blk
        place = jnp.where(spot == lax.broadcasted_iota(jnp.int32, (g.blk, g.d), 1), 1.0, 0.0).astype(LOW)
        r.gain_pass[0, 0:3] = dot(r.gains_in[...], place, 1, 0).astype(LOW)
        for k in hops:
            meet(r.gain_pass.at[0], r.gain_land.at[k], at_z[k])
    move(
        gather_z, "q", gather_own, "q", gather_own, "co", gather_own, "dn1", gather_z, "k", gather_own, "k",
        gather_own, "v", gather_own, "ck", gather_own, "cv", gather_own, "so", gather_own, "cq",
    )
    for copy in weights:
        copy.wait()
    total = r.gain_pass[0, 0:3].astype(F32) if g.comm else r.gains_in[...].astype(F32)
    if g.comm:
        for k in hops:
            small[k].wait_recv()
            total = total + r.gain_land[k, 0:3].astype(F32)
        r.gain_pass[1, 0:3] = total.astype(LOW)
        hop = meet(r.gain_pass.at[1], r.gain_land.at[3], at_x)
    r.bias[...] = jnp.full(r.bias.shape, NEGATIVE)
    key = lax.broadcasted_iota(jnp.int32, (g.seq, g.seq), 0)
    query = lax.broadcasted_iota(jnp.int32, (g.seq, g.seq), 1)
    for row in range(g.rows):
        across = r.seg[row // g.row_mb, row % g.row_mb:row % g.row_mb + 1, :].astype(F32)
        down = jnp.sum(jnp.where(key == query, across, 0.0), axis=1, keepdims=True)
        p, at = row * g.seq // PAIR, row * g.seq % PAIR
        r.bias[p, at:at + g.seq, at:at + g.seq] = jnp.where((key <= query) & (down == across), 0.0, NEGATIVE)
    r.gain_sum[...] = jnp.zeros_like(r.gain_sum)
    move(gather_b, "co", gather_on, "q", gather_a, "q", gather_b, "dn1", gather_z, "v")
    if g.comm:
        hop.wait_recv()
        total = total + r.gain_land[3, 0:3].astype(F32)
        r.gain_pass[2, 0:3] = total.astype(LOW)
        hop = meet(r.gain_pass.at[2], r.gain_land.at[4], at_y)
    move(gather_on, "k", gather_a, "k", gather_z, "ck")
    if g.comm:
        hop.wait_recv()
        total = total + r.gain_land[4, 0:3].astype(F32)
    for i in range(3):
        r.gains[i] = total[i:i + 1]
    bring_hidden.wait()

    @pl.loop(0, g.t // LN_ROWS)
    def _(n):
        rows = pl.ds(pl.multiple_of(n * LN_ROWS, LN_ROWS), LN_ROWS)
        r.a1[rows] = norm(r.hidden[rows].astype(F32), 0)

    def project(j):
        r.qkv[j] = dot(r.a1[...], w8(QKV + j), 1, 0).astype(LOW)

    move(
        gather_on, "v", gather_a, "v", gather_z, "cv", gather_b, "q", gather_on, "ck", gather_z, "so",
        gather_b, "k", gather_on, "cv", gather_z, "cq", gather_a, "ck", gather_b, "v", gather_on, "so",
        gather_z, "up0", gather_a, "cv", gather_end, "q",
    )
    project(0)
    move(
        gather_on, "cq", gather_turn, "co", gather_z, "up1", gather_b, "ck", gather_a, "so",
        gather_own, "up0", gather_end, "k",
    )
    project(1)
    move(
        gather_b, "cv", gather_on, "up0", gather_z, "dn0", gather_a, "cq", gather_own, "up1", gather_b, "so",
        gather_end, "v",
    )
    project(2)

    def self_attend(first, last):
        @pl.loop(first, last)
        def _(p):
            rows = pl.ds(pl.multiple_of(p * PAIR, PAIR), PAIR)
            bias = jnp.concatenate([r.bias[p]] * 2, axis=1)
            for h in range(pairs):
                lanes = lanes_of(h)
                queries = stack_heads(r.qkv[0, rows, lanes], masks)
                scores = dot(r.qkv[1, rows, lanes], queries, 1, 1) * score_scale + bias
                weights_low = softmax_keys(scores).astype(LOW)
                r.self_p[p, h] = weights_low
                r.mixed[rows, lanes] = join_heads(dot(weights_low, r.qkv[2, rows, lanes], 0, 0)).astype(LOW)

    def project_images(m):
        @pl.loop(0, g.images)
        def _(image):
            rows = pl.ds(pl.multiple_of(image * g.ctx, g.ctx), g.ctx)
            r.kv[m, image] = dot(r.enc[rows], w8(CKV + m), 1, 0).astype(LOW)

    self_attend(0, g.t // PAIR)
    bring_enc.wait()
    move(gather_b, "cq", gather_on, "co", gather_end, "ck")
    project_images(0)
    move(gather_a, "up0", gather_on, "up1", gather_own, "dn0", gather_end, "cv")
    project_images(1)
    move(gather_on, "dn0", gather_turn, "dn1", gather_end, "so")
    exchange_start(0, lambda rows: dot(r.mixed[rows], w8(SO), 1, 1))

    def after_self(rows, total):
        resid = r.hidden[rows].astype(F32) + total
        r.resid_one[rows] = resid
        r.a2[rows] = norm(resid, 1)

    move(gather_a, "up1")
    by_rows(0, after_self)
    move(gather_b, "up0", gather_a, "dn0", gather_end, "cq")
    r.cq[...] = dot(r.a2[...], w8(CQ), 1, 0).astype(LOW)

    def cross_attend(first, last):
        @pl.loop(first, last)
        def _(row):
            rows = pl.ds(pl.multiple_of(row * g.seq, g.seq), g.seq)
            image = (row // g.row_mb) * g.img_mb + r.image_ids[row // g.row_mb, row % g.row_mb]
            for h in range(pairs):
                lanes = lanes_of(h)
                queries = stack_heads(r.cq[rows, lanes], masks)
                scores = dot(r.kv[0, image, :, lanes], queries, 1, 1) * score_scale
                weights_low = softmax_keys(scores).astype(LOW)
                r.cross_p[row * pairs + h] = weights_low
                r.cmixed[rows, lanes] = join_heads(dot(weights_low, r.kv[1, image, :, lanes], 0, 0)).astype(LOW)

    cross_attend(g.rows * 0 // 2, g.rows * 1 // 2)
    cross_attend(g.rows * 1 // 2, g.rows * 2 // 2)
    move(gather_b, "up1", gather_turned, "co")
    exchange_start(1, lambda rows: dot(r.cmixed[rows], w8(CO), 1, 1))

    def after_cross(rows, total):
        resid = r.resid_one[rows] + total
        r.resid_two[rows] = resid
        r.a3[rows] = norm(resid, 2)

    move(gather_b, "dn0", gather_on, "dn1")
    by_rows(1, after_cross)
    bring_cot.wait()

    def up_half(first):
        @pl.loop(0, half // TILE)
        def _(n):
            cols = pl.ds(pl.multiple_of(first + n * TILE, TILE), TILE)
            pre = dot(r.a3[...], wide(UP, cols), 1, 0)
            below = 0.5 * (1.0 + lax.erf(pre * ROOT_HALF))
            r.act[:, cols] = (pre * below).astype(LOW)
            slope = below + pre * (DENSITY * jnp.exp(-0.5 * (pre * pre)))
            r.slope[:, cols] = slope.astype(r.slope.dtype)

    def grad_wide(which, left, right, first):
        cols = pl.ds(first, half)
        put_wide(which, cols, dot(left[...], right[:, cols], 0, 0))

    def down_half(first):
        @pl.loop(0, half // TILE)
        def _(n):
            cols = pl.ds(pl.multiple_of(first + n * TILE, TILE), TILE)
            grad_act = dot(r.cot[...], wide(DOWN, cols), 1, 0)
            r.slope[:, cols] = (grad_act * r.slope[:, cols].astype(F32)).astype(LOW)

    move(gather_end, "up0")
    up_half(0)
    grad_wide(DOWN, r.cot, r.act, 0)
    move(reduce_b, "dn0")
    move(gather_end, "up1")
    up_half(half)
    grad_wide(DOWN, r.cot, r.act, half)
    move(reduce_b, "dn1")
    everything = pl.ds(0, g.ff)
    move(gather_end, "dn0")
    down_half(0)
    grad_wide(UP, r.a3, r.slope, 0)
    move(reduce_b, "up0")
    move(gather_turned, "dn1")
    down_half(half)
    exchange_start(2, lambda rows: dot(r.slope[rows], wide(UP, everything), 1, 1))
    grad_wide(UP, r.a3, r.slope, half)
    move(reduce_b, "up1")

    def after_up(rows, total):
        grad = r.cot[rows].astype(F32) + norm_back(2, r.resid_two[rows], total)
        r.grad[rows] = grad
        r.grad_low[rows] = grad.astype(LOW)

    move(reduce_a, "dn0")
    by_rows(2, after_up)
    put8(CO, dot(r.grad_low[...], r.cmixed[...], 0, 0))
    move(reduce_b, "co")
    r.g_mixed[...] = dot(r.grad_low[...], w8(CO), 1, 0).astype(LOW)

    def cross_back(m):
        @pl.loop(0, pairs)
        def _(h):
            lanes = pl.ds(pl.multiple_of(h * PAIR, PAIR), PAIR)
            queries, grads, soft = [], [], []
            for n in range(g.row_mb):
                row = m * g.row_mb + n
                rows = pl.ds(row * g.seq, g.seq)
                image = m * g.img_mb + r.image_ids[m, n]
                grads.append(stack_heads(r.g_mixed[rows, lanes], masks))
                queries.append(stack_heads(r.cq[rows, lanes], masks))
                weights_low = r.cross_p[row * pairs + h]
                soft.append(weights_low)
                prob = weights_low.astype(F32)
                grad_p = dot(r.kv[1, image, :, lanes], grads[-1], 1, 1)
                inner = jnp.sum(prob * grad_p, axis=0, keepdims=True)
                grad_s = (prob * (grad_p - inner)).astype(LOW)
                r.cross_ds[:, lanes_of(n)] = grad_s
                grad_q = join_heads(dot(grad_s, r.kv[0, image, :, lanes], 0, 0)) * score_scale
                r.cq[rows, lanes] = grad_q.astype(LOW)
            soft = jnp.concatenate(soft, axis=1)
            chosen = [
                [
                    jnp.where(r.image_ids[m, n] == i, jnp.ones((1, PAIR), F32), 0.0).astype(LOW)
                    for i in range(g.img_mb)
                ]
                for n in range(g.row_mb)
            ]

            def picked(parts):
                return jnp.concatenate(
                    [jnp.concatenate([v * c for c in cs], axis=1) for v, cs in zip(parts, chosen)], axis=0
                )

            for j, left, parts, scale in ((0, r.cross_ds[...], queries, score_scale), (1, soft, grads, 1.0)):
                both = dot(left, picked(parts), 1, 0)
                for i in range(g.img_mb):
                    part = both[:, i * PAIR:(i + 1) * PAIR] * scale
                    r.kv[j, m * g.img_mb + i, :, lanes] = part.astype(LOW)

    cross_back(0)
    move(reduce_on, "dn1", reduce_z, "dn0", reduce_a, "up0")
    cross_back(1)
    move(reduce_a, "up1", reduce_on, "co", reduce_z, "up0")
    exchange_start(3, lambda rows: dot(r.cq[rows], w8(CQ), 1, 1))
    def grad_images(j):
        put8(CKV + j, dot(r.enc[...], r.kv[j].reshape(g.images * g.ctx, g.f), 0, 0))

    put8(CQ, dot(r.a2[...], r.cq[...], 0, 0))
    move(reduce_b, "cq")
    move(reduce_turn, "dn1")
    grad_images(0)
    move(reduce_b, "ck")
    move(reduce_on, "dn0", reduce_z, "up1")
    grad_images(1)
    move(reduce_b, "cv")
    def after_query(rows, total):
        grad = r.grad[rows] + norm_back(1, r.resid_one[rows], total)
        r.grad[rows] = grad
        r.grad_low[rows] = grad.astype(LOW)

    move(reduce_turn, "co", reduce_a, "dn1", reduce_a, "cq")
    by_rows(3, after_query)
    move(reduce_on, "up0")
    put8(SO, dot(r.grad_low[...], r.mixed[...], 0, 0))
    move(reduce_b, "so")
    r.g_mixed[...] = dot(r.grad_low[...], w8(SO), 1, 0).astype(LOW)

    def self_back(first, last):
        @pl.loop(first, last)
        def _(p):
            rows = pl.ds(pl.multiple_of(p * PAIR, PAIR), PAIR)
            for h in range(pairs):
                lanes = lanes_of(h)
                queries = stack_heads(r.qkv[0, rows, lanes], masks)
                grads = stack_heads(r.g_mixed[rows, lanes], masks)
                weights_low = r.self_p[p, h]
                prob = weights_low.astype(F32)
                grad_p = dot(r.qkv[2, rows, lanes], grads, 1, 1)
                inner = jnp.sum(prob * grad_p, axis=0, keepdims=True)
                grad_s = (prob * (grad_p - inner)).astype(LOW)
                grad_q = join_heads(dot(grad_s, r.qkv[1, rows, lanes], 0, 0)) * score_scale
                grad_k = dot(grad_s, queries, 1, 0) * score_scale
                grad_v = dot(weights_low, grads, 1, 0)
                r.qkv[0, rows, lanes] = grad_q.astype(LOW)
                r.qkv[1, rows, lanes] = grad_k.astype(LOW)
                r.qkv[2, rows, lanes] = grad_v.astype(LOW)

    move(reduce_a, "ck")
    self_back(0, g.t // PAIR)
    move(reduce_on, "up1", reduce_z, "cq")
    exchange_start(
        4,
        lambda rows: dot(r.qkv[0, rows], w8(QKV), 1, 1)
        + dot(r.qkv[1, rows], w8(QKV + 1), 1, 1)
        + dot(r.qkv[2, rows], w8(QKV + 2), 1, 1),
    )
    for_name = ("q", "k", "v")

    def grad_project(j):
        put8(QKV + j, dot(r.a1[...], r.qkv[j], 0, 0))
        move(reduce_b, for_name[j])

    def after_qkv(rows, total):
        r.grad[rows] = r.grad[rows] + norm_back(0, r.hidden[rows].astype(F32), total)

    move(reduce_z, "ck", reduce_a, "cv", reduce_a, "co")
    grad_project(0)
    grad_project(1)
    grad_project(2)
    by_rows(4, after_qkv)
    write(r.grad, r.in_grad)
    move(reduce_on, "cq", reduce_on, "ck", reduce_a, "so", reduce_z, "cv")
    for i in range(3):
        r.gain_total[0, i:i + 1] = jnp.sum(r.gain_sum[i], axis=0, keepdims=True)
    if g.comm:
        first = len(small)
        for k in hops:
            meet(r.gain_total.at[0], r.total_land.at[k], at_z[k])

    def features(j, h):
        if g.comm:
            return r.w8[j, pl.ds(h * (g.nz // 2), g.nz // 2)].reshape(g.d // 2, g.f)
        return r.w8[j, pl.ds(pl.multiple_of(h * (g.d // 2), g.d // 2), g.d // 2)]

    def encoder_part(image, h):
        return dot(r.kv[0, image], features(CKV, h), 1, 1) + dot(r.kv[1, image], features(CKV + 1, h), 1, 1)

    strips = g.d // 2 // PAIR

    def encoder_keep(image, value):
        for h in range(strips):
            r.cross_p[image * strips + h] = value[:, h * PAIR:(h + 1) * PAIR].astype(LOW)

    def encoder_copy(image):
        part = pl.ds(image * strips, strips)
        return remote(r.cross_p.at[part], r.enc_land.at[part], r.enc_s.at[image], r.enc_r.at[image], sibling)

    def encoder_leave():
        @pl.loop(0, g.images)
        def _(image):
            encoder_keep(image, encoder_part(image, 1 - mp))

        for image in range(g.images):
            encoder_copy(image).start()

    def encoder_join():
        for image in range(g.images):
            encoder_copy(image).wait_recv()
            encoder_copy(image).wait_send()

        @pl.loop(0, g.images)
        def _(image):
            landed = jnp.concatenate([r.enc_land[image * strips + h] for h in range(strips)], axis=1)
            encoder_keep(image, encoder_part(image, mp) + landed.astype(F32))

        for image in range(g.images):
            for h in range(strips):
                rows = pl.ds(image * g.ctx, g.ctx)
                write(r.cross_p.at[image * strips + h], r.enc_grad.at[rows, lanes_of(h)])

    def after_down(rows, total):
        r.a3[rows] = (r.resid_two[rows] + total).astype(LOW)

    encoder_leave()
    move(reduce_a, "q")
    exchange_start(5, lambda rows: dot(r.act[rows], wide(DOWN, everything), 1, 1))
    move(reduce_on, "cv", reduce_z, "so")
    if g.comm:
        total = r.gain_total[0]
        for k in hops:
            small[first + k].wait_recv()
            total = total + r.total_land[k]
        r.gain_total[1] = total
        hop = meet(r.gain_total.at[1], r.total_land.at[3], at_x)
    move(
        reduce_end, "dn1", reduce_end, "dn0", reduce_end, "up0", reduce_end, "up1", reduce_end, "co",
        reduce_end, "cq", reduce_end, "ck",
    )
    encoder_join()
    move(reduce_on, "so", reduce_z, "q", reduce_a, "k", reduce_a, "v")
    by_rows(5, after_down)
    write(r.a3, r.out)
    move(reduce_end, "cv")
    if g.comm:
        hop.wait_recv()
        r.gain_total[2] = r.gain_total[1] + r.total_land[3]
        hop = meet(r.gain_total.at[2], r.total_land.at[4], at_y)
    move(reduce_end, "so", reduce_z, "k", reduce_z, "v", reduce_end, "q")
    if g.comm:
        hop.wait_recv()
        total = r.gain_total[2] + r.total_land[4]
    if g.comm:
        spot = lax.broadcasted_iota(jnp.int32, (g.d, g.blk), 1) + me * g.blk
        place = jnp.where(spot == lax.broadcasted_iota(jnp.int32, (g.d, g.blk), 0), 1.0, 0.0)
        mine = lax.dot_general(
            total, place, (((1,), (0,)), ((), ())), precision=lax.Precision.HIGHEST, preferred_element_type=F32
        )
        r.gain_out[...] = mine[0:3]
    else:
        r.gain_out[...] = r.gain_total[0, 0:3]
    move(reduce_end, "k", reduce_end, "v")
    for copy in written:
        copy.wait()
    for copy in small:
        copy.wait_send()
    for copy, condition in started:
        only(condition, copy.wait_send)


def run_layer(g, operands):
    vmem = pl.BlockSpec(memory_space=pltpu.VMEM)
    smem = pl.BlockSpec(memory_space=pltpu.SMEM)
    anywhere = pl.BlockSpec(memory_space=pl.ANY)
    shape = jax.ShapeDtypeStruct
    ins = dict(
        image_ids=smem, seg=vmem, hidden_in=anywhere, gains_in=vmem, cot_in=anywhere, enc_in=anywhere,
        qkv_in=anywhere, so_in=anywhere, cq_in=anywhere, ckv_in=anywhere, co_in=anywhere,
        up_in=anywhere, down_in=anywhere,
    )
    outs = dict(
        out=(shape((g.t, g.d), LOW), anywhere),
        in_grad=(shape((g.t, g.d), F32), anywhere),
        enc_grad=(shape((g.images * g.ctx, g.d // 2), LOW), anywhere),
        gain_out=(shape((3, g.blk if g.comm else g.d), F32), vmem),
    )
    grid = (g.nz, 4, g.blk) if g.comm else (g.d,)
    dma = pltpu.SemaphoreType.DMA
    scratch = dict(
        w8=pltpu.VMEM((MATS, *grid, g.f), LOW),
        wf=pltpu.VMEM((2, *grid, g.ff), LOW),
        hidden=pltpu.VMEM((g.t, g.d), LOW),
        enc=pltpu.VMEM((g.images * g.ctx, g.d), LOW),
        cot=pltpu.VMEM((g.t, g.d), LOW),
        gains=pltpu.VMEM((3, 1, g.d), F32),
        gain_sum=pltpu.VMEM((3, 8, g.d), F32),
        gain_total=pltpu.VMEM((3, 8, g.d), F32),
        bias=pltpu.VMEM((g.t // PAIR, PAIR, PAIR), F32),
        a1=pltpu.VMEM((g.t, g.d), LOW),
        a2=pltpu.VMEM((g.t, g.d), LOW),
        a3=pltpu.VMEM((g.t, g.d), LOW),
        qkv=pltpu.VMEM((3, g.t, g.f), LOW),
        mixed=pltpu.VMEM((g.t, g.f), LOW),
        cq=pltpu.VMEM((g.t, g.f), LOW),
        cmixed=pltpu.VMEM((g.t, g.f), LOW),
        g_mixed=pltpu.VMEM((g.t, g.f), LOW),
        kv=pltpu.VMEM((2, g.images, g.ctx, g.f), LOW),
        self_p=pltpu.VMEM((g.t // PAIR, g.f // PAIR, PAIR, 2 * PAIR), LOW),
        cross_p=pltpu.VMEM((g.rows * (g.f // PAIR), g.ctx, PAIR), LOW),
        cross_ds=pltpu.VMEM((g.ctx, g.row_mb * PAIR), LOW),
        resid_one=pltpu.VMEM((g.t, g.d), F32),
        resid_two=pltpu.VMEM((g.t, g.d), F32),
        grad=pltpu.VMEM((g.t, g.d), F32),
        grad_low=pltpu.VMEM((g.t, g.d), LOW),
        act=pltpu.VMEM((g.t, g.ff), LOW),
        slope=pltpu.VMEM((g.t, g.ff), LOW),
        stage=pltpu.VMEM((2, g.t, g.d), LOW),
        land=pltpu.VMEM((3, g.t, g.d), LOW),
        enc_land=pltpu.VMEM((g.images * (g.d // 2 // PAIR), g.ctx, PAIR), LOW),
        local_sem=dma((10,)),
        ex_s=dma((6, 2)), ex_r=dma((6, 2)),
        enc_s=dma((g.images,)), enc_r=dma((g.images,)),
        write_sem=dma((16 + g.images * (g.d // 2 // PAIR),)),
    )
    if g.comm:
        outs.update(
            g8_out=(shape((MATS, g.blk, g.f), F32), anywhere),
            gf_out=(shape((2, g.blk, g.ff), F32), anywhere),
        )
        hops = g.nz - 1
        scratch.update(
            g8=pltpu.VMEM((MATS, g.blk, g.f), F32),
            gf=pltpu.VMEM((2, g.blk, g.ff), F32),
            p8=pltpu.VMEM((MATS, *grid, g.f), LOW),
            pf=pltpu.VMEM((2, *grid, g.ff), LOW),
            lb8=pltpu.VMEM((2, MATS - 1, g.nz, g.blk, g.f), LOW),
            lbf=pltpu.VMEM((2, 3, g.nz, g.blk, g.ff // 2), LOW),
            la8=pltpu.VMEM((MATS - 1, g.nz, g.blk, g.f), LOW),
            laf=pltpu.VMEM((3, g.nz, g.blk, g.ff // 2), LOW),
            lz8=pltpu.VMEM((hops, MATS - 1, g.blk, g.f), LOW),
            lzf=pltpu.VMEM((hops, 3, g.blk, g.ff // 2), LOW),
            lx8=pltpu.VMEM((MATS - 1, g.blk, g.f), LOW),
            lxf=pltpu.VMEM((3, g.blk, g.ff // 2), LOW),
            turnf_z=pltpu.VMEM((hops, 4, g.blk, g.ff // 2), LOW),
            turnf_x=pltpu.VMEM((4, g.blk, g.ff // 2), LOW),
            turnf_b=pltpu.VMEM((2, g.blk, g.ff // 2), LOW),
            turnf_a=pltpu.VMEM((g.blk, g.ff // 2), LOW),
            turn8_z=pltpu.VMEM((hops, 1, 4, g.blk, g.f), LOW),
            turn8_x=pltpu.VMEM((1, 4, g.blk, g.f), LOW),
            turn8_b=pltpu.VMEM((2, 1, g.blk, g.f), LOW),
            turn8_a=pltpu.VMEM((1, g.blk, g.f), LOW),
            gain_land=pltpu.VMEM((hops + 2, 16, g.d), LOW),
            gain_pass=pltpu.VMEM((3, 16, g.d), LOW),
            total_land=pltpu.VMEM((hops + 2, 8, g.d), F32),
            agz_s=dma((12, 4)), agz_r=dma((12, 4)),
            aga_s=dma((12, g.nz)), aga_r=dma((12, g.nz)),
            agb_s=dma((12, g.nz + 1)), agb_r=dma((12, g.nz + 1)),
            rsz_s=dma((12, 4)), rsz_r=dma((12, 4)),
            rsa_s=dma((12,)), rsa_r=dma((12,)),
            rsb_s=dma((12, 2)), rsb_r=dma((12, 2)),
            small_s=dma((2 * hops + 4,)), small_r=dma((2 * hops + 4,)),
        )
    else:
        outs.update(
            p8=(shape((MATS, g.d, g.f), LOW), vmem),
            pf=(shape((2, g.d, g.ff), LOW), vmem),
        )
    g.names = (*ins, *outs, *scratch)
    return dict(zip(outs, pl.pallas_call(
        functools.partial(layer, g),
        out_shape=[o[0] for o in outs.values()],
        in_specs=list(ins.values()),
        out_specs=[o[1] for o in outs.values()],
        scratch_shapes=list(scratch.values()),
        compiler_params=pltpu.CompilerParams(
            collective_id=0, has_side_effects=True, vmem_limit_bytes=63 * 2**20
        ),
        name="layer",
    )(*operands)))


def pass_on(g, out, in_grad, enc, gain, g8, gf, *refs):
    outs, (v_out, v_in, v_gain, v_g8, v_gf, low, full, in_sem, out_sem) = refs[:11], refs[11:]
    coming, leaving = [], []

    def bring(src, dst):
        coming.append(pltpu.make_async_copy(src, dst, in_sem.at[len(coming)]))
        coming[-1].start()

    def leave(src, dst):
        leaving.append(pltpu.make_async_copy(src, dst, out_sem.at[len(leaving)]))
        leaving[-1].start()

    halves = [pl.ds(i * g.t // 2, g.t // 2) for i in range(2)]
    images = [pl.ds(i * g.ctx, g.ctx) for i in range(g.images)]
    for rows in images:
        bring(enc.at[rows], low.at[rows])
    for rows in halves:
        bring(in_grad.at[rows], v_in.at[rows])
    bring(out, v_out)
    bring(g8, v_g8)
    bring(gf, v_gf)
    bring(gain, v_gain)
    for i, rows in enumerate(images):
        coming[i].wait()
        full[rows] = low[rows].astype(F32)
        leave(full.at[rows], outs[2].at[rows])
    for copy, rows in zip(coming[g.images:], halves):
        copy.wait()
        leave(v_in.at[rows], outs[1].at[rows])
    for copy in coming[g.images + 2:]:
        copy.wait()
    leave(v_out, outs[0])
    leave(v_gain, outs[3])
    for src, dst in zip(
        (v_g8.at[pl.ds(QKV, 3)], v_g8.at[SO], v_g8.at[CQ], v_g8.at[pl.ds(CKV, 2)], v_g8.at[CO], v_gf.at[UP], v_gf.at[DOWN]),
        outs[4:],
    ):
        leave(src, dst)
    for copy in leaving:
        copy.wait()


def hand_over(g, o):
    shape = jax.ShapeDtypeStruct
    tokens, enc = (g.t, g.d), (g.images * g.ctx, g.d // 2)
    one, wide = (g.blk, g.f), (g.blk, g.ff)
    shapes = (tokens, tokens, enc, (3, g.blk), (3, *one), one, one, (2, *one), one, wide, wide)
    anywhere = pl.BlockSpec(memory_space=pl.ANY)
    dma = pltpu.SemaphoreType.DMA
    return pl.pallas_call(
        functools.partial(pass_on, g),
        out_shape=[shape(s, LOW if i == 0 else F32) for i, s in enumerate(shapes)],
        in_specs=[anywhere] * 6,
        out_specs=[anywhere] * 11,
        scratch_shapes=[
            pltpu.VMEM(tokens, LOW), pltpu.VMEM(tokens, F32), pltpu.VMEM((3, g.blk), F32),
            pltpu.VMEM((MATS, *one), F32), pltpu.VMEM((2, *wide), F32),
            pltpu.VMEM(enc, LOW), pltpu.VMEM(enc, F32), dma((g.images + 6,)), dma((g.images + 11,)),
        ],
        compiler_params=pltpu.CompilerParams(vmem_limit_bytes=63 * 2**20),
        name="hand_over",
    )(o["out"], o["in_grad"], o["enc_grad"], o["gain_out"], o["g8_out"], o["gf_out"])


def body(
    dp, mp, hidden, encoder_tokens, segment_ids, image_index, cotangent, norm_gains, qkv_weight,
    self_out_weight, cross_query_weight, cross_kv_weight, cross_out_weight, up_weight, down_weight,
):
    micro, row_mb, seq, d = hidden.shape
    img_mb, ctx = encoder_tokens.shape[1:3]
    blk, f = self_out_weight.shape
    g = SimpleNamespace(
        micro=micro, row_mb=row_mb, seq=seq, d=d, img_mb=img_mb, ctx=ctx, blk=blk, f=f,
        ff=up_weight.shape[1], rows=micro * row_mb, t=micro * row_mb * seq, images=micro * img_mb,
        nz=dp // 4, comm=dp == 16 and blk % 16 == 0,
    )
    weights = [
        qkv_weight, self_out_weight, cross_query_weight, cross_kv_weight, cross_out_weight, up_weight, down_weight,
    ]
    gains = norm_gains
    if not g.comm:
        gains = lax.all_gather(norm_gains, "dp", axis=1, tiled=True)
        weights = [lax.all_gather(w, "dp", axis=w.ndim - 2, tiled=True) for w in weights]
    for i in (1, 2, 4):
        weights[i] = weights[i][None]
    o = run_layer(g, (
        image_index, segment_ids, hidden.reshape(g.t, d), gains, cotangent.reshape(g.t, d),
        encoder_tokens.reshape(g.images * ctx, d), *weights,
    ))
    if g.comm:
        whole = hand_over(g, o)
    else:
        small = lax.psum_scatter(o["p8"].astype(F32), "dp", scatter_dimension=1, tiled=True)
        wide = lax.psum_scatter(o["pf"].astype(F32), "dp", scatter_dimension=1, tiled=True)
        whole = (
            o["out"], o["in_grad"], o["enc_grad"].astype(F32),
            lax.psum_scatter(o["gain_out"], "dp", scatter_dimension=1, tiled=True),
            small[QKV:QKV + 3], small[SO], small[CQ], small[CKV:CKV + 2], small[CO], wide[UP], wide[DOWN],
        )
    return (
        whole[0].reshape(hidden.shape), whole[1].reshape(hidden.shape),
        whole[2].reshape(micro, img_mb, ctx, d // 2), *whole[3:],
    )


def solution(mesh):
    tokens, kept = P(None, "dp", None, None), P("dp", "mp")
    three = P(None, "dp", "mp")
    return jax.shard_map(
        functools.partial(body, mesh.shape["dp"], mesh.shape["mp"]),
        mesh=mesh,
        in_specs=(
            tokens, tokens, P(None, "dp", None), P(None, "dp"), tokens, P(None, "dp"),
            three, kept, kept, three, kept, kept, kept,
        ),
        out_specs=(
            tokens, tokens, P(None, "dp", None, "mp"), P(None, "dp"),
            three, kept, kept, three, kept, kept, kept,
        ),
        check_vma=False,
    )
```

```python
import functools
from types import SimpleNamespace

import jax
import jax.numpy as jnp
from jax import lax
from jax.experimental import pallas as pl
from jax.experimental.pallas import tpu as pltpu
from jax.sharding import PartitionSpec as P

HEAD = 64
PAIR = 2 * HEAD
EPSILON = 1e-05
NEGATIVE = -1e30
ROOT_HALF = 0.7071067811865476
DENSITY = 0.3989422804014327
MESH = pl.DeviceIdType.MESH
LOW = jnp.bfloat16
F32 = jnp.float32
QKV, SO, CQ, CKV, CO, MATS = 0, 3, 4, 5, 7, 8
DIRECT = ("q", "k", "v")
UP, DOWN = 0, 1
LN_ROWS = 128
TILE = 256


def dot(left, right, left_dim, right_dim):
    return lax.dot_general(
        left, right, (((left_dim,), (right_dim,)), ((), ())), preferred_element_type=F32
    )


def lanes_of(pair):
    return pl.ds(pair * PAIR, PAIR)


def head_masks():
    lane = lax.broadcasted_iota(jnp.int32, (1, PAIR), 1)
    first = jnp.where(lane < HEAD, 1.0, 0.0)
    return first.astype(LOW), (1.0 - first).astype(LOW)


def stack_heads(values, masks):
    return jnp.concatenate([values * masks[0], values * masks[1]], axis=0)


def join_heads(stacked):
    half = stacked.shape[0] // 2
    lane = lax.broadcasted_iota(jnp.int32, (half, PAIR), 1)
    return jnp.where(lane < HEAD, stacked[:half], stacked[half:])


def centre(values):
    centred = values - jnp.mean(values, axis=-1, keepdims=True)
    spread = jnp.mean(centred * centred, axis=-1, keepdims=True)
    scale = lax.rsqrt(spread + EPSILON)
    return centred * scale, scale


def softmax_keys(scores):
    shifted = jnp.exp(scores - jnp.max(scores, axis=0, keepdims=True))
    return shifted / jnp.sum(shifted, axis=0, keepdims=True)


def layer(g, *refs):
    r = SimpleNamespace(**dict(zip(g.names, refs)))
    me, mp = lax.axis_index("dp"), lax.axis_index("mp")
    zi, col = me // 4, me % 4
    sibling = (me, 1 - mp)
    col_x = col + 1 - 2 * (col % 2)
    col_y = (col + 2) % 4
    col_d = (col_x + 2) % 4
    col_a = mp * col_x + (1 - mp) * col_y
    col_b = mp * col_y + (1 - mp) * col_x
    at_x, at_y = (zi * 4 + col_x, mp), (zi * 4 + col_y, mp)
    at_a, at_b = (zi * 4 + col_a, mp), (zi * 4 + col_b, mp)
    z_of = [(zi + k) % g.nz for k in range(1, g.nz)]
    z_from = [(zi + g.nz - k) % g.nz for k in range(1, g.nz)]
    at_z = [(z * 4 + col, mp) for z in z_of]

    greeted = [sibling] + ([at_x, at_y] + at_z if g.comm else [])
    barrier = pltpu.get_barrier_semaphore()
    for device in greeted:
        pl.semaphore_signal(barrier, inc=1, device_id=device, device_id_type=MESH)

    def remote(src, dst, send, recv, device):
        return pltpu.make_async_remote_copy(
            src_ref=src, dst_ref=dst, send_sem=send, recv_sem=recv, device_id=device, device_id_type=MESH
        )

    local = []

    def bring(src, dst):
        copy = pltpu.make_async_copy(src, dst, r.local_sem.at[len(local)])
        copy.start()
        local.append(copy)
        return copy

    def slot(first, count):
        ref = r.w8.at[pl.ds(first, count)]
        return ref.at[:, zi, col] if g.comm else ref

    def wide_slot(which):
        return r.wf.at[which, zi, col] if g.comm else r.wf.at[which]

    weights = [
        bring(r.qkv_in, slot(QKV, 3)),
        bring(r.so_in, slot(SO, 1)),
        bring(r.cq_in, slot(CQ, 1)),
        bring(r.ckv_in, slot(CKV, 2)),
        bring(r.co_in, slot(CO, 1)),
        bring(r.up_in, wide_slot(UP)),
        bring(r.down_in, wide_slot(DOWN)),
    ]
    bring_hidden = bring(r.hidden_in, r.hidden)
    bring_enc = bring(r.enc_in, r.enc)
    bring_cot = bring(r.cot_in, r.cot)

    half = g.ff // 2

    def mats(first, ref, at):
        part = pl.ds(first, 1)

        def each(c, body):
            @pl.loop(0, g.nz)
            def _(z):
                body(r.p8.at[first, z, c], lambda landed: landed.at[0, z])

        return SimpleNamespace(
            src=lambda: ref.at[pl.ds(at, 1)],
            w=lambda z, c: r.w8.at[part, z, c], w_column=lambda c: r.w8.at[part, :, c],
            w_row=lambda z: r.w8.at[part, z], p_row=lambda z: r.p8.at[part, z],
            p=lambda z, c: r.p8.at[part, z, c], p_column=lambda c: r.p8.at[part, :, c],
            lb=lambda k: r.lb8.at[k, part], la=lambda: r.la8.at[part], lz=lambda k: r.lz8.at[k, part],
            lx=lambda: r.lx8.at[part], in_row=lambda row, c: row.at[:, c],
            tz=lambda k: r.turn8_z.at[k], tb=lambda k: r.turn8_b.at[k], ta=lambda: r.turn8_a,
            tx=lambda: r.turn8_x, each=each, sum=lambda: r.g8.at[part], sum_out=lambda: r.g8_out.at[part],
        )

    def strip(which, first, i, ref):
        cols = pl.ds(first, half)

        def each(c, body):
            @pl.loop(0, g.nz)
            def _(z):
                body(r.pf.at[which, z, c, :, cols], lambda landed: landed.at[z])

        return SimpleNamespace(
            src=lambda: ref.at[:, cols],
            w=lambda z, c: r.wf.at[which, z, c, :, cols], w_column=lambda c: r.wf.at[which, :, c, :, cols],
            w_row=lambda z: r.wf.at[which, z, :, :, cols], p_row=lambda z: r.pf.at[which, z, :, :, cols],
            p=lambda z, c: r.pf.at[which, z, c, :, cols], p_column=lambda c: r.pf.at[which, :, c, :, cols],
            lb=lambda k: r.lbf.at[k, i], la=lambda: r.laf.at[i], lz=lambda k: r.lzf.at[k, i],
            lx=lambda: r.lxf.at[i], in_row=lambda row, c: row.at[c],
            tz=lambda k: r.turnf_z.at[k], tb=lambda k: r.turnf_b.at[k], ta=lambda: r.turnf_a,
            tx=lambda: r.turnf_x, each=each, sum=lambda: r.gf.at[which, :, cols],
            sum_out=lambda: r.gf_out.at[which, :, cols],
        )

    groups = dict(
        q=mats(QKV, r.qkv_in, 0), k=mats(QKV + 1, r.qkv_in, 1), v=mats(QKV + 2, r.qkv_in, 2),
        ck=mats(CKV, r.ckv_in, 0), cv=mats(CKV + 1, r.ckv_in, 1),
        so=mats(SO, r.so_in, 0), cq=mats(CQ, r.cq_in, 0), co=mats(CO, r.co_in, 0),
        up0=strip(UP, 0, 0, r.up_in), up1=strip(UP, half, 1, r.up_in),
        dn0=strip(DOWN, 0, 2, r.down_in), dn1=strip(DOWN, half, 3, r.down_in),
    )
    for i, (name, group) in enumerate(groups.items()):
        group.i, group.turned, group.direct = i, name in ("co", "dn1"), name in DIRECT

    inner = (zi == 1) | (zi == 2)
    goes = (zi != 3, None, zi != 0)
    hops = range(3)
    other = 3 * (2 - zi)
    onward = 3 * (zi - 1)
    filled = 2 * jnp.where(zi == 0, 1, 0)

    written = []

    def write(src, dst):
        copy = pltpu.make_async_copy(src, dst, r.write_sem.at[len(written)])
        copy.start()
        written.append(copy)

    started = []

    def only(condition, act):
        if condition is None:
            act()
        else:
            pl.when(condition)(act)

    def start(copy, condition=None):
        only(condition, copy.start)
        started.append((copy, condition))

    def arrived(ref, send, recv, device, condition=None):
        only(condition, remote(ref, ref, send, recv, device).wait_recv)

    def gather_z(name):
        t = groups[name]
        for k in hops:
            src, dst = (t.w_row(zi), t.w_row(zi)) if t.turned else (t.src(), t.w(zi, col))
            start(remote(src, dst, r.agz_s.at[t.i, k], r.agz_r.at[t.i, k], at_z[k]), None if t.direct else goes[k])

    def z_part(t, z):
        return t.w_row(z) if t.turned else t.w(z, col)

    def gather_on(name):
        t = groups[name]
        arrived(z_part(t, z_from[1]), r.agz_s.at[t.i, 1], r.agz_r.at[t.i, 1], at_z[1])
        if t.direct:
            return
        part = z_part(t, jnp.where(inner, other, 0))
        start(
            remote(part, part, r.agz_s.at[t.i, 3], r.agz_r.at[t.i, 2 * jnp.where(zi == 2, 1, 0)],
                   (jnp.where(inner, onward, 0) * 4 + col, mp)),
            inner,
        )

    def to_both(t, i, src, dst):
        start(remote(src, dst, r.aga_s.at[t.i, i], r.aga_r.at[t.i, i], at_a))
        start(remote(src, dst, r.agb_s.at[t.i, i], r.agb_r.at[t.i, i], at_b))

    def gather_own(name):
        t = groups[name]
        to_both(t, 0, t.src(), t.w(zi, col))

    def gather_a(name):
        t = groups[name]
        for k in (1, 0, 2):
            block = t.w(z_from[k], col)
            if k != 1:
                arrived(block, r.agz_s.at[t.i, k], r.agz_r.at[t.i, k], at_z[k])
            to_both(t, 1 + k, block, block)

    def gather_b(name):
        t = groups[name]
        arrived(t.w(zi, col_a), r.aga_s.at[t.i, 0], r.aga_r.at[t.i, 0], at_a)
        part = t.w(zi, col_a)
        if not t.turned:
            for k in hops:
                arrived(t.w(z_from[k], col_a), r.aga_s.at[t.i, 1 + k], r.aga_r.at[t.i, 1 + k], at_a)
            part = t.w_column(col_a)
        start(remote(part, part, r.agb_s.at[t.i, 4], r.agb_r.at[t.i, 4], at_b))

    def gather_end(name):
        t = groups[name]
        arrived(t.w(zi, col_b), r.agb_s.at[t.i, 0], r.agb_r.at[t.i, 0], at_b)
        if not t.turned:
            for k in hops:
                arrived(t.w(z_from[k], col_b), r.agb_s.at[t.i, 1 + k], r.agb_r.at[t.i, 1 + k], at_b)
        part = t.w(zi, col_d) if t.turned else t.w_column(col_d)
        arrived(part, r.agb_s.at[t.i, 4], r.agb_r.at[t.i, 4], at_b)

    def gather_turn(name):
        gather_end(name)
        gather_z(name)

    def gather_turned(name):
        t = groups[name]
        for k in (0, 2):
            arrived(t.w_row(z_from[k]), r.agz_s.at[t.i, k], r.agz_r.at[t.i, k], at_z[k])

    def added(target, *landed):
        total = target[...].astype(F32)
        for ref in landed:
            total = total + ref[...].astype(F32)
        return total

    def z_start(t, part, place):
        for k in hops:
            condition = None if t.direct else jnp.logical_not(inner) if k == 1 else goes[k]
            start(remote(part(z_of[k]), place(k), r.rsz_s.at[t.i, k], r.rsz_r.at[t.i, k], at_z[k]), condition)
        if t.direct:
            return
        end_part = part(jnp.where(inner, 0, 3 - zi))
        beside = (jnp.where(zi == 0, 1, 2) * 4 + col, mp)
        extra = t.tx() if t.turned else t.lx()
        start(remote(end_part, extra, r.rsz_s.at[t.i, 3], r.rsz_r.at[t.i, 3], beside), jnp.logical_not(inner))

    def reduce_b(name):
        t = groups[name]
        if t.turned:
            z_start(t, t.p_row, t.tz)
            return
        for k, c in ((1, col_d), (0, col_b)):
            start(remote(t.p_column(c), t.lb(k), r.rsb_s.at[t.i, k], r.rsb_r.at[t.i, k], at_b))

    def reduce_on(name):
        t = groups[name]
        if t.direct:
            return
        far = z_of[1]
        extra = t.tx() if t.turned else t.lx()

        @pl.when(inner)
        def _():
            arrived(extra, r.rsz_s.at[t.i, 3], r.rsz_r.at[t.i, 3], at_z[1])
            if t.turned:
                @pl.loop(0, 4)
                def _(c):
                    target = t.p(far, c)
                    target[...] = added(target, t.in_row(extra, c)).astype(LOW)
            else:
                target = t.p(far, col)
                target[...] = added(target, extra).astype(LOW)

        part, place = (t.p_row(far), t.tz(1)) if t.turned else (t.p(far, col), t.lz(1))
        start(remote(part, place, r.rsz_s.at[t.i, 1], r.rsz_r.at[t.i, 1], at_z[1]), inner)

    def z_arrived(t, place):
        places = ((0, None), (1, None), (2, None)) if t.direct else ((1, None), (filled, None), (2, inner))
        for k, condition in places:
            arrived(place(k), r.rsz_s.at[t.i, k], r.rsz_r.at[t.i, k], at_z[1], condition)

    def reduce_turn(name):
        t = groups[name]
        z_arrived(t, t.tz)

        @pl.loop(0, 4)
        def _(c):
            target = t.p(zi, c)
            target[...] = added(target, t.in_row(t.tz(1), c), t.in_row(t.tz(filled), c)).astype(LOW)

        @pl.when(inner)
        def _():
            @pl.loop(0, 4)
            def _(c):
                target = t.p(zi, c)
                target[...] = added(target, t.in_row(t.tz(2), c)).astype(LOW)

        for k, c in ((1, col_d), (0, col_b)):
            start(remote(t.p(zi, c), t.tb(k), r.rsb_s.at[t.i, k], r.rsb_r.at[t.i, k], at_b))

    def reduce_a(name):
        t = groups[name]
        for k, c in ((1, col_a), (0, col)):
            landed = t.tb(k) if t.turned else t.lb(k)
            arrived(landed, r.rsb_s.at[t.i, k], r.rsb_r.at[t.i, k], at_b)
            if t.turned:
                target = t.p(zi, c)
                target[...] = added(target, landed).astype(LOW)
            else:
                def add(target, view):
                    target[...] = added(target, view(landed)).astype(LOW)
                t.each(c, add)
            if k:
                src, dst = (t.p(zi, c), t.ta()) if t.turned else (t.p_column(c), t.la())
                start(remote(src, dst, r.rsa_s.at[t.i], r.rsa_r.at[t.i], at_a))

    def reduce_z(name):
        t = groups[name]
        landed = t.la()
        arrived(landed, r.rsa_s.at[t.i], r.rsa_r.at[t.i], at_a)

        def add(target, view):
            target[...] = added(target, view(landed)).astype(LOW)
        t.each(col, add)
        z_start(t, lambda z: t.p(z, col), t.lz)

    def reduce_end(name):
        t = groups[name]
        total = t.sum()
        if t.turned:
            arrived(t.ta(), r.rsa_s.at[t.i], r.rsa_r.at[t.i], at_a)
            total[...] = added(t.p(zi, col), t.ta())
        else:
            z_arrived(t, t.lz)
            if t.direct:
                total[...] = added(t.p(zi, col), t.lz(0), t.lz(1), t.lz(2))
            else:
                total[...] = added(t.p(zi, col), t.lz(1), t.lz(filled))

                @pl.when(inner)
                def _():
                    total[...] = added(total, t.lz(2))
        write(total, t.sum_out())

    def move(*steps):
        if g.comm:
            for step, name in zip(steps[::2], steps[1::2]):
                step(name)

    def w8(j):
        return r.w8[j].reshape(g.d, g.f)

    def wide(which, cols):
        if g.comm:
            return r.wf[which, :, :, :, cols].reshape(g.d, -1)
        return r.wf[which, :, cols]

    def put8(j, value):
        r.p8[j] = value.astype(LOW).reshape(r.p8.shape[1:])

    def put_wide(which, cols, value):
        if g.comm:
            r.pf[which, :, :, :, cols] = value.astype(LOW).reshape(g.nz, 4, g.blk, -1)
        else:
            r.pf[which, :, cols] = value.astype(LOW)

    part = g.t // 2

    def exchange(e, i):
        rows = pl.ds(i * part, part)
        return remote(
            r.stage.at[e % 2, rows], r.land.at[e % 3, rows], r.ex_s.at[e, i], r.ex_r.at[e, i], sibling
        )

    def exchange_start(e, product):
        for i in range(2):
            rows = pl.ds(i * part, part)
            r.stage[e % 2, rows] = product(rows).astype(LOW)
            exchange(e, i).start()

    def by_rows(e, body):
        for i in range(2):
            exchange(e, i).wait_recv()
            exchange(e, i).wait_send()

            @pl.loop(0, part // LN_ROWS)
            def _(n):
                rows = pl.ds(pl.multiple_of(i * part + n * LN_ROWS, LN_ROWS), LN_ROWS)
                body(rows, r.stage[e % 2, rows].astype(F32) + r.land[e % 3, rows].astype(F32))

    def norm(values, i):
        return (centre(values)[0] * r.gains[i]).astype(LOW)

    def norm_back(i, values, grad):
        normed, scale = centre(values)
        r.gain_sum[i] += jnp.sum((grad * normed).reshape(-1, 8, g.d), axis=0)
        scaled = grad * r.gains[i]
        return scale * (
            scaled
            - jnp.mean(scaled, axis=-1, keepdims=True)
            - normed * jnp.mean(scaled * normed, axis=-1, keepdims=True)
        )

    masks = head_masks()
    score_scale = HEAD ** (-0.5)
    pairs = g.f // PAIR

    pl.semaphore_wait(barrier, len(greeted))
    small = []

    def meet(src, dst, device):
        i = len(small)
        copy = remote(src, dst, r.small_s.at[i], r.small_r.at[i], device)
        copy.start()
        small.append(copy)
        return copy

    if g.comm:
        spot = lax.broadcasted_iota(jnp.int32, (g.blk, g.d), 0) + me * g.blk
        place = jnp.where(spot == lax.broadcasted_iota(jnp.int32, (g.blk, g.d), 1), 1.0, 0.0).astype(LOW)
        r.gain_pass[0, 0:3] = dot(r.gains_in[...], place, 1, 0).astype(LOW)
        for k in hops:
            meet(r.gain_pass.at[0], r.gain_land.at[k], at_z[k])
    move(
        gather_z, "q", gather_own, "q", gather_own, "co", gather_own, "dn1", gather_z, "k", gather_own, "k",
        gather_own, "v", gather_own, "ck", gather_own, "cv", gather_own, "so", gather_own, "cq",
    )
    for copy in weights:
        copy.wait()
    total = r.gain_pass[0, 0:3].astype(F32) if g.comm else r.gains_in[...].astype(F32)
    if g.comm:
        for k in hops:
            small[k].wait_recv()
            total = total + r.gain_land[k, 0:3].astype(F32)
        r.gain_pass[1, 0:3] = total.astype(LOW)
        hop = meet(r.gain_pass.at[1], r.gain_land.at[3], at_x)
    r.bias[...] = jnp.full(r.bias.shape, NEGATIVE)
    key = lax.broadcasted_iota(jnp.int32, (g.seq, g.seq), 0)
    query = lax.broadcasted_iota(jnp.int32, (g.seq, g.seq), 1)
    for row in range(g.rows):
        across = r.seg[row // g.row_mb, row % g.row_mb:row % g.row_mb + 1, :].astype(F32)
        down = jnp.sum(jnp.where(key == query, across, 0.0), axis=1, keepdims=True)
        p, at = row * g.seq // PAIR, row * g.seq % PAIR
        r.bias[p, at:at + g.seq, at:at + g.seq] = jnp.where((key <= query) & (down == across), 0.0, NEGATIVE)
    r.gain_sum[...] = jnp.zeros_like(r.gain_sum)
    move(gather_b, "co", gather_on, "q", gather_a, "q", gather_b, "dn1", gather_z, "v")
    if g.comm:
        hop.wait_recv()
        total = total + r.gain_land[3, 0:3].astype(F32)
        r.gain_pass[2, 0:3] = total.astype(LOW)
        hop = meet(r.gain_pass.at[2], r.gain_land.at[4], at_y)
    move(gather_on, "k", gather_a, "k", gather_z, "ck")
    if g.comm:
        hop.wait_recv()
        total = total + r.gain_land[4, 0:3].astype(F32)
    for i in range(3):
        r.gains[i] = total[i:i + 1]
    bring_hidden.wait()

    @pl.loop(0, g.t // LN_ROWS)
    def _(n):
        rows = pl.ds(pl.multiple_of(n * LN_ROWS, LN_ROWS), LN_ROWS)
        r.a1[rows] = norm(r.hidden[rows].astype(F32), 0)

    def project(j):
        r.qkv[j] = dot(r.a1[...], w8(QKV + j), 1, 0).astype(LOW)

    move(
        gather_on, "v", gather_a, "v", gather_z, "cv", gather_b, "q", gather_on, "ck", gather_z, "so",
        gather_b, "k", gather_on, "cv", gather_z, "cq", gather_a, "ck", gather_b, "v", gather_on, "so",
        gather_z, "up0", gather_a, "cv", gather_end, "q",
    )
    project(0)
    move(
        gather_on, "cq", gather_turn, "co", gather_z, "up1", gather_b, "ck", gather_a, "so",
        gather_own, "up0", gather_end, "k",
    )
    project(1)
    move(
        gather_b, "cv", gather_on, "up0", gather_z, "dn0", gather_a, "cq", gather_own, "up1", gather_b, "so",
        gather_end, "v",
    )
    project(2)

    def self_attend(first, last):
        @pl.loop(first, last)
        def _(p):
            rows = pl.ds(pl.multiple_of(p * PAIR, PAIR), PAIR)
            bias = jnp.concatenate([r.bias[p]] * 2, axis=1)
            for h in range(pairs):
                lanes = lanes_of(h)
                queries = stack_heads(r.qkv[0, rows, lanes], masks)
                scores = dot(r.qkv[1, rows, lanes], queries, 1, 1) * score_scale + bias
                weights_low = softmax_keys(scores).astype(LOW)
                r.self_p[p, h] = weights_low
                r.mixed[rows, lanes] = join_heads(dot(weights_low, r.qkv[2, rows, lanes], 0, 0)).astype(LOW)

    def project_images(m):
        @pl.loop(0, g.images)
        def _(image):
            rows = pl.ds(pl.multiple_of(image * g.ctx, g.ctx), g.ctx)
            r.kv[m, image] = dot(r.enc[rows], w8(CKV + m), 1, 0).astype(LOW)

    self_attend(0, g.t // PAIR)
    bring_enc.wait()
    move(gather_b, "cq", gather_on, "co", gather_end, "ck")
    project_images(0)
    move(gather_a, "up0", gather_on, "up1", gather_own, "dn0", gather_end, "cv")
    project_images(1)
    move(gather_on, "dn0", gather_turn, "dn1", gather_end, "so")
    exchange_start(0, lambda rows: dot(r.mixed[rows], w8(SO), 1, 1))

    def after_self(rows, total):
        resid = r.hidden[rows].astype(F32) + total
        r.resid_one[rows] = resid
        r.a2[rows] = norm(resid, 1)

    move(gather_a, "up1")
    by_rows(0, after_self)
    move(gather_b, "up0", gather_a, "dn0", gather_end, "cq")
    r.cq[...] = dot(r.a2[...], w8(CQ), 1, 0).astype(LOW)

    def cross_attend(first, last):
        @pl.loop(first, last)
        def _(row):
            rows = pl.ds(pl.multiple_of(row * g.seq, g.seq), g.seq)
            image = (row // g.row_mb) * g.img_mb + r.image_ids[row // g.row_mb, row % g.row_mb]
            for h in range(pairs):
                lanes = lanes_of(h)
                queries = stack_heads(r.cq[rows, lanes], masks)
                scores = dot(r.kv[0, image, :, lanes], queries, 1, 1) * score_scale
                weights_low = softmax_keys(scores).astype(LOW)
                r.cross_p[row * pairs + h] = weights_low
                r.cmixed[rows, lanes] = join_heads(dot(weights_low, r.kv[1, image, :, lanes], 0, 0)).astype(LOW)

    cross_attend(g.rows * 0 // 2, g.rows * 1 // 2)
    cross_attend(g.rows * 1 // 2, g.rows * 2 // 2)
    move(gather_b, "up1", gather_turned, "co")
    exchange_start(1, lambda rows: dot(r.cmixed[rows], w8(CO), 1, 1))

    def after_cross(rows, total):
        resid = r.resid_one[rows] + total
        r.resid_two[rows] = resid
        r.a3[rows] = norm(resid, 2)

    move(gather_b, "dn0", gather_on, "dn1")
    by_rows(1, after_cross)
    bring_cot.wait()

    def up_half(first):
        @pl.loop(0, half // TILE)
        def _(n):
            cols = pl.ds(pl.multiple_of(first + n * TILE, TILE), TILE)
            pre = dot(r.a3[...], wide(UP, cols), 1, 0)
            below = 0.5 * (1.0 + lax.erf(pre * ROOT_HALF))
            r.act[:, cols] = (pre * below).astype(LOW)
            slope = below + pre * (DENSITY * jnp.exp(-0.5 * (pre * pre)))
            r.slope[:, cols] = slope.astype(r.slope.dtype)

    def grad_wide(which, left, right, first):
        cols = pl.ds(first, half)
        put_wide(which, cols, dot(left[...], right[:, cols], 0, 0))

    def down_half(first):
        @pl.loop(0, half // TILE)
        def _(n):
            cols = pl.ds(pl.multiple_of(first + n * TILE, TILE), TILE)
            grad_act = dot(r.cot[...], wide(DOWN, cols), 1, 0)
            r.slope[:, cols] = (grad_act * r.slope[:, cols].astype(F32)).astype(LOW)

    move(gather_end, "up0")
    up_half(0)
    grad_wide(DOWN, r.cot, r.act, 0)
    move(reduce_b, "dn0")
    move(gather_end, "up1")
    up_half(half)
    grad_wide(DOWN, r.cot, r.act, half)
    move(reduce_b, "dn1")
    everything = pl.ds(0, g.ff)
    move(gather_end, "dn0")
    down_half(0)
    grad_wide(UP, r.a3, r.slope, 0)
    move(reduce_b, "up0")
    move(gather_turned, "dn1")
    down_half(half)
    exchange_start(2, lambda rows: dot(r.slope[rows], wide(UP, everything), 1, 1))
    grad_wide(UP, r.a3, r.slope, half)
    move(reduce_b, "up1")

    def after_up(rows, total):
        grad = r.cot[rows].astype(F32) + norm_back(2, r.resid_two[rows], total)
        r.grad[rows] = grad
        r.grad_low[rows] = grad.astype(LOW)

    move(reduce_a, "dn0")
    by_rows(2, after_up)
    put8(CO, dot(r.grad_low[...], r.cmixed[...], 0, 0))
    move(reduce_b, "co")
    r.g_mixed[...] = dot(r.grad_low[...], w8(CO), 1, 0).astype(LOW)

    def cross_back(m):
        @pl.loop(0, pairs)
        def _(h):
            lanes = pl.ds(pl.multiple_of(h * PAIR, PAIR), PAIR)
            queries, grads, soft = [], [], []
            for n in range(g.row_mb):
                row = m * g.row_mb + n
                rows = pl.ds(row * g.seq, g.seq)
                image = m * g.img_mb + r.image_ids[m, n]
                grads.append(stack_heads(r.g_mixed[rows, lanes], masks))
                queries.append(stack_heads(r.cq[rows, lanes], masks))
                weights_low = r.cross_p[row * pairs + h]
                soft.append(weights_low)
                prob = weights_low.astype(F32)
                grad_p = dot(r.kv[1, image, :, lanes], grads[-1], 1, 1)
                inner = jnp.sum(prob * grad_p, axis=0, keepdims=True)
                grad_s = (prob * (grad_p - inner)).astype(LOW)
                r.cross_ds[:, lanes_of(n)] = grad_s
                grad_q = join_heads(dot(grad_s, r.kv[0, image, :, lanes], 0, 0)) * score_scale
                r.cq[rows, lanes] = grad_q.astype(LOW)
            soft = jnp.concatenate(soft, axis=1)
            chosen = [
                [
                    jnp.where(r.image_ids[m, n] == i, jnp.ones((1, PAIR), F32), 0.0).astype(LOW)
                    for i in range(g.img_mb)
                ]
                for n in range(g.row_mb)
            ]

            def picked(parts):
                return jnp.concatenate(
                    [jnp.concatenate([v * c for c in cs], axis=1) for v, cs in zip(parts, chosen)], axis=0
                )

            for j, left, parts, scale in ((0, r.cross_ds[...], queries, score_scale), (1, soft, grads, 1.0)):
                both = dot(left, picked(parts), 1, 0)
                for i in range(g.img_mb):
                    part = both[:, i * PAIR:(i + 1) * PAIR] * scale
                    r.kv[j, m * g.img_mb + i, :, lanes] = part.astype(LOW)

    cross_back(0)
    move(reduce_on, "dn1", reduce_z, "dn0", reduce_a, "up0")
    cross_back(1)
    move(reduce_a, "up1", reduce_on, "co", reduce_z, "up0")
    exchange_start(3, lambda rows: dot(r.cq[rows], w8(CQ), 1, 1))
    def grad_images(j):
        put8(CKV + j, dot(r.enc[...], r.kv[j].reshape(g.images * g.ctx, g.f), 0, 0))

    put8(CQ, dot(r.a2[...], r.cq[...], 0, 0))
    move(reduce_b, "cq")
    move(reduce_turn, "dn1")
    grad_images(0)
    move(reduce_b, "ck")
    move(reduce_on, "dn0", reduce_z, "up1")
    grad_images(1)
    move(reduce_b, "cv")
    def after_query(rows, total):
        grad = r.grad[rows] + norm_back(1, r.resid_one[rows], total)
        r.grad[rows] = grad
        r.grad_low[rows] = grad.astype(LOW)

    move(reduce_turn, "co", reduce_a, "dn1", reduce_a, "cq")
    by_rows(3, after_query)
    move(reduce_on, "up0")
    put8(SO, dot(r.grad_low[...], r.mixed[...], 0, 0))
    move(reduce_b, "so")
    r.g_mixed[...] = dot(r.grad_low[...], w8(SO), 1, 0).astype(LOW)

    def self_back(first, last):
        @pl.loop(first, last)
        def _(p):
            rows = pl.ds(pl.multiple_of(p * PAIR, PAIR), PAIR)
            for h in range(pairs):
                lanes = lanes_of(h)
                queries = stack_heads(r.qkv[0, rows, lanes], masks)
                grads = stack_heads(r.g_mixed[rows, lanes], masks)
                weights_low = r.self_p[p, h]
                prob = weights_low.astype(F32)
                grad_p = dot(r.qkv[2, rows, lanes], grads, 1, 1)
                inner = jnp.sum(prob * grad_p, axis=0, keepdims=True)
                grad_s = (prob * (grad_p - inner)).astype(LOW)
                grad_q = join_heads(dot(grad_s, r.qkv[1, rows, lanes], 0, 0)) * score_scale
                grad_k = dot(grad_s, queries, 1, 0) * score_scale
                grad_v = dot(weights_low, grads, 1, 0)
                r.qkv[0, rows, lanes] = grad_q.astype(LOW)
                r.qkv[1, rows, lanes] = grad_k.astype(LOW)
                r.qkv[2, rows, lanes] = grad_v.astype(LOW)

    move(reduce_a, "ck")
    self_back(0, g.t // PAIR)
    move(reduce_on, "up1", reduce_z, "cq")
    exchange_start(
        4,
        lambda rows: dot(r.qkv[0, rows], w8(QKV), 1, 1)
        + dot(r.qkv[1, rows], w8(QKV + 1), 1, 1)
        + dot(r.qkv[2, rows], w8(QKV + 2), 1, 1),
    )
    for_name = ("q", "k", "v")

    def grad_project(j):
        put8(QKV + j, dot(r.a1[...], r.qkv[j], 0, 0))
        move(reduce_b, for_name[j])

    def after_qkv(rows, total):
        r.grad[rows] = r.grad[rows] + norm_back(0, r.hidden[rows].astype(F32), total)

    move(reduce_z, "ck", reduce_a, "cv", reduce_a, "co")
    grad_project(0)
    grad_project(1)
    grad_project(2)
    by_rows(4, after_qkv)
    write(r.grad, r.in_grad)
    move(reduce_on, "cq", reduce_on, "ck", reduce_a, "so", reduce_z, "cv")
    for i in range(3):
        r.gain_total[0, i:i + 1] = jnp.sum(r.gain_sum[i], axis=0, keepdims=True)
    if g.comm:
        first = len(small)
        for k in hops:
            meet(r.gain_total.at[0], r.total_land.at[k], at_z[k])

    def features(j, h):
        if g.comm:
            return r.w8[j, pl.ds(h * (g.nz // 2), g.nz // 2)].reshape(g.d // 2, g.f)
        return r.w8[j, pl.ds(pl.multiple_of(h * (g.d // 2), g.d // 2), g.d // 2)]

    def encoder_part(image, h):
        return dot(r.kv[0, image], features(CKV, h), 1, 1) + dot(r.kv[1, image], features(CKV + 1, h), 1, 1)

    strips = g.d // 2 // PAIR

    def encoder_keep(image, value):
        for h in range(strips):
            r.cross_p[image * strips + h] = value[:, h * PAIR:(h + 1) * PAIR].astype(LOW)

    def encoder_copy(image):
        part = pl.ds(image * strips, strips)
        return remote(r.cross_p.at[part], r.enc_land.at[part], r.enc_s.at[image], r.enc_r.at[image], sibling)

    def encoder_leave():
        @pl.loop(0, g.images)
        def _(image):
            encoder_keep(image, encoder_part(image, 1 - mp))

        for image in range(g.images):
            encoder_copy(image).start()

    def encoder_join():
        for image in range(g.images):
            encoder_copy(image).wait_recv()
            encoder_copy(image).wait_send()

        @pl.loop(0, g.images)
        def _(image):
            landed = jnp.concatenate([r.enc_land[image * strips + h] for h in range(strips)], axis=1)
            encoder_keep(image, encoder_part(image, mp) + landed.astype(F32))

        for image in range(g.images):
            for h in range(strips):
                rows = pl.ds(image * g.ctx, g.ctx)
                write(r.cross_p.at[image * strips + h], r.enc_grad.at[rows, lanes_of(h)])

    def after_down(rows, total):
        r.a3[rows] = (r.resid_two[rows] + total).astype(LOW)

    encoder_leave()
    move(reduce_a, "q")
    exchange_start(5, lambda rows: dot(r.act[rows], wide(DOWN, everything), 1, 1))
    move(reduce_on, "cv", reduce_z, "so")
    if g.comm:
        total = r.gain_total[0]
        for k in hops:
            small[first + k].wait_recv()
            total = total + r.total_land[k]
        r.gain_total[1] = total
        hop = meet(r.gain_total.at[1], r.total_land.at[3], at_x)
    move(
        reduce_end, "dn1", reduce_end, "dn0", reduce_end, "up0", reduce_end, "up1", reduce_end, "co",
        reduce_end, "cq", reduce_end, "ck",
    )
    encoder_join()
    move(reduce_on, "so", reduce_z, "q", reduce_a, "k", reduce_a, "v")
    by_rows(5, after_down)
    write(r.a3, r.out)
    move(reduce_end, "cv")
    if g.comm:
        hop.wait_recv()
        r.gain_total[2] = r.gain_total[1] + r.total_land[3]
        hop = meet(r.gain_total.at[2], r.total_land.at[4], at_y)
    move(reduce_end, "so", reduce_z, "k", reduce_z, "v", reduce_end, "q")
    if g.comm:
        hop.wait_recv()
        total = r.gain_total[2] + r.total_land[4]
    if g.comm:
        spot = lax.broadcasted_iota(jnp.int32, (g.d, g.blk), 1) + me * g.blk
        place = jnp.where(spot == lax.broadcasted_iota(jnp.int32, (g.d, g.blk), 0), 1.0, 0.0)
        mine = lax.dot_general(
            total, place, (((1,), (0,)), ((), ())), precision=lax.Precision.HIGHEST, preferred_element_type=F32
        )
        r.gain_out[...] = mine[0:3]
    else:
        r.gain_out[...] = r.gain_total[0, 0:3]
    move(reduce_end, "k", reduce_end, "v")
    for copy in written:
        copy.wait()
    for copy in small:
        copy.wait_send()
    for copy, condition in started:
        only(condition, copy.wait_send)


def run_layer(g, operands):
    vmem = pl.BlockSpec(memory_space=pltpu.VMEM)
    smem = pl.BlockSpec(memory_space=pltpu.SMEM)
    anywhere = pl.BlockSpec(memory_space=pl.ANY)
    shape = jax.ShapeDtypeStruct
    ins = dict(
        image_ids=smem, seg=vmem, hidden_in=anywhere, gains_in=vmem, cot_in=anywhere, enc_in=anywhere,
        qkv_in=anywhere, so_in=anywhere, cq_in=anywhere, ckv_in=anywhere, co_in=anywhere,
        up_in=anywhere, down_in=anywhere,
    )
    outs = dict(
        out=(shape((g.t, g.d), LOW), anywhere),
        in_grad=(shape((g.t, g.d), F32), anywhere),
        enc_grad=(shape((g.images * g.ctx, g.d // 2), LOW), anywhere),
        gain_out=(shape((3, g.blk if g.comm else g.d), F32), vmem),
    )
    grid = (g.nz, 4, g.blk) if g.comm else (g.d,)
    dma = pltpu.SemaphoreType.DMA
    scratch = dict(
        w8=pltpu.VMEM((MATS, *grid, g.f), LOW),
        wf=pltpu.VMEM((2, *grid, g.ff), LOW),
        hidden=pltpu.VMEM((g.t, g.d), LOW),
        enc=pltpu.VMEM((g.images * g.ctx, g.d), LOW),
        cot=pltpu.VMEM((g.t, g.d), LOW),
        gains=pltpu.VMEM((3, 1, g.d), F32),
        gain_sum=pltpu.VMEM((3, 8, g.d), F32),
        gain_total=pltpu.VMEM((3, 8, g.d), F32),
        bias=pltpu.VMEM((g.t // PAIR, PAIR, PAIR), F32),
        a1=pltpu.VMEM((g.t, g.d), LOW),
        a2=pltpu.VMEM((g.t, g.d), LOW),
        a3=pltpu.VMEM((g.t, g.d), LOW),
        qkv=pltpu.VMEM((3, g.t, g.f), LOW),
        mixed=pltpu.VMEM((g.t, g.f), LOW),
        cq=pltpu.VMEM((g.t, g.f), LOW),
        cmixed=pltpu.VMEM((g.t, g.f), LOW),
        g_mixed=pltpu.VMEM((g.t, g.f), LOW),
        kv=pltpu.VMEM((2, g.images, g.ctx, g.f), LOW),
        self_p=pltpu.VMEM((g.t // PAIR, g.f // PAIR, PAIR, 2 * PAIR), LOW),
        cross_p=pltpu.VMEM((g.rows * (g.f // PAIR), g.ctx, PAIR), LOW),
        cross_ds=pltpu.VMEM((g.ctx, g.row_mb * PAIR), LOW),
        resid_one=pltpu.VMEM((g.t, g.d), F32),
        resid_two=pltpu.VMEM((g.t, g.d), F32),
        grad=pltpu.VMEM((g.t, g.d), F32),
        grad_low=pltpu.VMEM((g.t, g.d), LOW),
        act=pltpu.VMEM((g.t, g.ff), LOW),
        slope=pltpu.VMEM((g.t, g.ff), LOW),
        stage=pltpu.VMEM((2, g.t, g.d), LOW),
        land=pltpu.VMEM((3, g.t, g.d), LOW),
        enc_land=pltpu.VMEM((g.images * (g.d // 2 // PAIR), g.ctx, PAIR), LOW),
        local_sem=dma((10,)),
        ex_s=dma((6, 2)), ex_r=dma((6, 2)),
        enc_s=dma((g.images,)), enc_r=dma((g.images,)),
        write_sem=dma((16 + g.images * (g.d // 2 // PAIR),)),
    )
    if g.comm:
        outs.update(
            g8_out=(shape((MATS, g.blk, g.f), F32), anywhere),
            gf_out=(shape((2, g.blk, g.ff), F32), anywhere),
        )
        hops = g.nz - 1
        scratch.update(
            g8=pltpu.VMEM((MATS, g.blk, g.f), F32),
            gf=pltpu.VMEM((2, g.blk, g.ff), F32),
            p8=pltpu.VMEM((MATS, *grid, g.f), LOW),
            pf=pltpu.VMEM((2, *grid, g.ff), LOW),
            lb8=pltpu.VMEM((2, MATS - 1, g.nz, g.blk, g.f), LOW),
            lbf=pltpu.VMEM((2, 3, g.nz, g.blk, g.ff // 2), LOW),
            la8=pltpu.VMEM((MATS - 1, g.nz, g.blk, g.f), LOW),
            laf=pltpu.VMEM((3, g.nz, g.blk, g.ff // 2), LOW),
            lz8=pltpu.VMEM((hops, MATS - 1, g.blk, g.f), LOW),
            lzf=pltpu.VMEM((hops, 3, g.blk, g.ff // 2), LOW),
            lx8=pltpu.VMEM((MATS - 1, g.blk, g.f), LOW),
            lxf=pltpu.VMEM((3, g.blk, g.ff // 2), LOW),
            turnf_z=pltpu.VMEM((hops, 4, g.blk, g.ff // 2), LOW),
            turnf_x=pltpu.VMEM((4, g.blk, g.ff // 2), LOW),
            turnf_b=pltpu.VMEM((2, g.blk, g.ff // 2), LOW),
            turnf_a=pltpu.VMEM((g.blk, g.ff // 2), LOW),
            turn8_z=pltpu.VMEM((hops, 1, 4, g.blk, g.f), LOW),
            turn8_x=pltpu.VMEM((1, 4, g.blk, g.f), LOW),
            turn8_b=pltpu.VMEM((2, 1, g.blk, g.f), LOW),
            turn8_a=pltpu.VMEM((1, g.blk, g.f), LOW),
            gain_land=pltpu.VMEM((hops + 2, 16, g.d), LOW),
            gain_pass=pltpu.VMEM((3, 16, g.d), LOW),
            total_land=pltpu.VMEM((hops + 2, 8, g.d), F32),
            agz_s=dma((12, 4)), agz_r=dma((12, 4)),
            aga_s=dma((12, g.nz)), aga_r=dma((12, g.nz)),
            agb_s=dma((12, g.nz + 1)), agb_r=dma((12, g.nz + 1)),
            rsz_s=dma((12, 4)), rsz_r=dma((12, 4)),
            rsa_s=dma((12,)), rsa_r=dma((12,)),
            rsb_s=dma((12, 2)), rsb_r=dma((12, 2)),
            small_s=dma((2 * hops + 4,)), small_r=dma((2 * hops + 4,)),
        )
    else:
        outs.update(
            p8=(shape((MATS, g.d, g.f), LOW), vmem),
            pf=(shape((2, g.d, g.ff), LOW), vmem),
        )
    g.names = (*ins, *outs, *scratch)
    return dict(zip(outs, pl.pallas_call(
        functools.partial(layer, g),
        out_shape=[o[0] for o in outs.values()],
        in_specs=list(ins.values()),
        out_specs=[o[1] for o in outs.values()],
        scratch_shapes=list(scratch.values()),
        compiler_params=pltpu.CompilerParams(
            collective_id=0, has_side_effects=True, vmem_limit_bytes=63 * 2**20
        ),
        name="layer",
    )(*operands)))


def pass_on(g, out, in_grad, enc, gain, g8, gf, *refs):
    outs, (v_out, v_in, v_gain, v_g8, v_gf, low, full, in_sem, out_sem) = refs[:11], refs[11:]
    coming, leaving = [], []

    def bring(src, dst):
        coming.append(pltpu.make_async_copy(src, dst, in_sem.at[len(coming)]))
        coming[-1].start()

    def leave(src, dst):
        leaving.append(pltpu.make_async_copy(src, dst, out_sem.at[len(leaving)]))
        leaving[-1].start()

    halves = [pl.ds(i * g.t // 2, g.t // 2) for i in range(2)]
    images = [pl.ds(i * g.ctx, g.ctx) for i in range(g.images)]
    for rows in images:
        bring(enc.at[rows], low.at[rows])
    for rows in halves:
        bring(in_grad.at[rows], v_in.at[rows])
    bring(out, v_out)
    bring(g8, v_g8)
    bring(gf, v_gf)
    bring(gain, v_gain)
    for i, rows in enumerate(images):
        coming[i].wait()
        full[rows] = low[rows].astype(F32)
        leave(full.at[rows], outs[2].at[rows])
    for copy, rows in zip(coming[g.images:], halves):
        copy.wait()
        leave(v_in.at[rows], outs[1].at[rows])
    for copy in coming[g.images + 2:]:
        copy.wait()
    leave(v_out, outs[0])
    leave(v_gain, outs[3])
    for src, dst in zip(
        (v_g8.at[pl.ds(QKV, 3)], v_g8.at[SO], v_g8.at[CQ], v_g8.at[pl.ds(CKV, 2)], v_g8.at[CO], v_gf.at[UP], v_gf.at[DOWN]),
        outs[4:],
    ):
        leave(src, dst)
    for copy in leaving:
        copy.wait()


def hand_over(g, o):
    shape = jax.ShapeDtypeStruct
    tokens, enc = (g.t, g.d), (g.images * g.ctx, g.d // 2)
    one, wide = (g.blk, g.f), (g.blk, g.ff)
    shapes = (tokens, tokens, enc, (3, g.blk), (3, *one), one, one, (2, *one), one, wide, wide)
    anywhere = pl.BlockSpec(memory_space=pl.ANY)
    dma = pltpu.SemaphoreType.DMA
    return pl.pallas_call(
        functools.partial(pass_on, g),
        out_shape=[shape(s, LOW if i == 0 else F32) for i, s in enumerate(shapes)],
        in_specs=[anywhere] * 6,
        out_specs=[anywhere] * 11,
        scratch_shapes=[
            pltpu.VMEM(tokens, LOW), pltpu.VMEM(tokens, F32), pltpu.VMEM((3, g.blk), F32),
            pltpu.VMEM((MATS, *one), F32), pltpu.VMEM((2, *wide), F32),
            pltpu.VMEM(enc, LOW), pltpu.VMEM(enc, F32), dma((g.images + 6,)), dma((g.images + 11,)),
        ],
        compiler_params=pltpu.CompilerParams(vmem_limit_bytes=63 * 2**20),
        name="hand_over",
    )(o["out"], o["in_grad"], o["enc_grad"], o["gain_out"], o["g8_out"], o["gf_out"])


def body(
    dp, mp, hidden, encoder_tokens, segment_ids, image_index, cotangent, norm_gains, qkv_weight,
    self_out_weight, cross_query_weight, cross_kv_weight, cross_out_weight, up_weight, down_weight,
):
    micro, row_mb, seq, d = hidden.shape
    img_mb, ctx = encoder_tokens.shape[1:3]
    blk, f = self_out_weight.shape
    g = SimpleNamespace(
        micro=micro, row_mb=row_mb, seq=seq, d=d, img_mb=img_mb, ctx=ctx, blk=blk, f=f,
        ff=up_weight.shape[1], rows=micro * row_mb, t=micro * row_mb * seq, images=micro * img_mb,
        nz=dp // 4, comm=dp == 16 and blk % 16 == 0,
    )
    weights = [
        qkv_weight, self_out_weight, cross_query_weight, cross_kv_weight, cross_out_weight, up_weight, down_weight,
    ]
    gains = norm_gains
    if not g.comm:
        gains = lax.all_gather(norm_gains, "dp", axis=1, tiled=True)
        weights = [lax.all_gather(w, "dp", axis=w.ndim - 2, tiled=True) for w in weights]
    for i in (1, 2, 4):
        weights[i] = weights[i][None]
    o = run_layer(g, (
        image_index, segment_ids, hidden.reshape(g.t, d), gains, cotangent.reshape(g.t, d),
        encoder_tokens.reshape(g.images * ctx, d), *weights,
    ))
    if g.comm:
        whole = hand_over(g, o)
    else:
        small = lax.psum_scatter(o["p8"].astype(F32), "dp", scatter_dimension=1, tiled=True)
        wide = lax.psum_scatter(o["pf"].astype(F32), "dp", scatter_dimension=1, tiled=True)
        whole = (
            o["out"], o["in_grad"], o["enc_grad"].astype(F32),
            lax.psum_scatter(o["gain_out"], "dp", scatter_dimension=1, tiled=True),
            small[QKV:QKV + 3], small[SO], small[CQ], small[CKV:CKV + 2], small[CO], wide[UP], wide[DOWN],
        )
    return (
        whole[0].reshape(hidden.shape), whole[1].reshape(hidden.shape),
        whole[2].reshape(micro, img_mb, ctx, d // 2), *whole[3:],
    )


def solution(mesh):
    tokens, kept = P(None, "dp", None, None), P("dp", "mp")
    three = P(None, "dp", "mp")
    return jax.shard_map(
        functools.partial(body, mesh.shape["dp"], mesh.shape["mp"]),
        mesh=mesh,
        in_specs=(
            tokens, tokens, P(None, "dp", None), P(None, "dp"), tokens, P(None, "dp"),
            three, kept, kept, three, kept, kept, kept,
        ),
        out_specs=(
            tokens, tokens, P(None, "dp", None, "mp"), P(None, "dp"),
            three, kept, kept, three, kept, kept, kept,
        ),
        check_vma=False,
    )
```
